32 devices in a mesh: dp: 8 (over z, y), tensor: 4 (over x, core).
Axes of the slice: x: 2, y: 2, z: 4, core: 2. Of those that a mesh axis runs over, the one named last changes fastest.
Arguments:
- tokens: bfloat16 [8704, 1280], P(('dp', 'tensor')), may hold values from -6 to 6
- w_query: bfloat16 [1280, 1280], P(None, 'tensor'), may hold values from -0.15625 to 0.15625
- w_key: bfloat16 [1280, 1280], P(None, 'tensor'), may hold values from -0.15625 to 0.15625
- w_value: bfloat16 [1280, 1280], P(None, 'tensor'), may hold values from -0.15625 to 0.15625
- b_query: float32 [1280], P('tensor'), may hold values from -3 to 3
- b_value: float32 [1280], P('tensor'), may hold values from -3 to 3
- w_out: bfloat16 [1280, 1280], P('tensor'), may hold values from -1.75 to 1.75
- b_out: float32 [1280], replicated, may hold values from -3 to 3
- w_up: bfloat16 [1280, 5120], P(None, 'tensor'), may hold values from -0.15625 to 0.15625
- b_up: float32 [5120], P('tensor'), may hold values from -3 to 3
- w_down: bfloat16 [5120, 1280], P('tensor'), may hold values from -0.15625 to 0.15625
- b_down: float32 [1280], replicated, may hold values from -3 to 3
- gain_attn: float32 [1280], replicated, may hold values from 0.5 to 1.5
- shift_attn: float32 [1280], replicated, may hold values from -2 to 2
- gain_ffn: float32 [1280], replicated, may hold values from 0.5 to 1.5
- shift_ffn: float32 [1280], replicated, may hold values from -2 to 2
- cell_lengths: int32 [8, 6], P('dp'), may hold values from 1 to 384, 1088 in all within a row
- d_output: bfloat16 [8704, 1280], P(('dp', 'tensor')), may hold values from -6 to 6
Outputs:
- output: bfloat16 [8704, 1280], P(('dp', 'tensor'))
- d_tokens: float32 [8704, 1280], P(('dp', 'tensor'))
- grad_w_query: float32 [1280, 1280], P(None, 'tensor')
- grad_w_key: float32 [1280, 1280], P(None, 'tensor')
- grad_w_value: float32 [1280, 1280], P(None, 'tensor')
- grad_b_query: float32 [1280], P('tensor')
- grad_b_value: float32 [1280], P('tensor')
- grad_w_out: float32 [1280, 1280], P('tensor')
- grad_b_out: float32 [1280], replicated
- grad_w_up: float32 [1280, 5120], P(None, 'tensor')
- grad_b_up: float32 [5120], P('tensor')
- grad_w_down: float32 [5120, 1280], P('tensor')
- grad_b_down: float32 [1280], replicated
- grad_gain_attn: float32 [1280], replicated
- grad_shift_attn: float32 [1280], replicated
- grad_gain_ffn: float32 [1280], replicated
- grad_shift_ffn: float32 [1280], replicated
The draws below stay inside these ranges and needn't reach their ends.
Inputs may be any that keep to these rules, and one draw needn't show every extreme that they name: `cell_lengths`: each row's 6 cell lengths sum to 1088; some cell of every row has exactly 384 tokens.
All inputs are finite; a program needn't handle non-finite values.
Results may differ from the reference program's by a relative error of at most 0.015.
Values may be sent and summed in bfloat16 or wider, within the bound.
A program may use at most 192 MiB of HBM per device.

```python
import math
import jax
import jax.numpy as jnp
import numpy as np
from jax import lax

D = 1280
HEADS = 20
HEAD_DIM = 64
FF = 5120
SEQ = 1088
CELLS = 6
MOST_CELL = 384
ROWS = 8
TOKENS = 8704


def shard_levels(stream_key, shape, pieces, low, high):
    def one(axis_at, blocks):
        heights = jax.random.uniform(jax.random.fold_in(jax.random.fold_in(stream_key, 6), axis_at), (blocks,), jnp.float32, low / len(pieces), high / len(pieces))
        return jnp.repeat(jnp.exp(heights), shape[axis_at] // blocks).reshape((-1,) + (1,) * (len(shape) - axis_at - 1))

    level = one(*pieces[0])
    for cut in pieces[1:]:
        level = level * one(*cut)
    return level


def split_up(count, total, most, skew):
    portions = [(1 << 20) // math.isqrt(standing ** skew) + 1 for standing in range(2, count + 1)]
    spare, counts = total - most - (count - 1), [1] * (count - 1)
    while spare > 0:
        free = [i for i in range(count - 1) if counts[i] < most]
        pool, remaining = sum([portions[i] for i in free]), spare
        for i in free:
            addition = min(most - counts[i], max(1, remaining * portions[i] // pool), spare)
            counts[i] = counts[i] + addition
            spare = spare - addition
    return np.array([most] + counts)


def uneven(stream_key, number_of, total, bound, slope):
    if number_of == 2:
        one = jax.random.randint(stream_key, (), max(1, total - bound), min(bound, total - 1) + 1)
        return jnp.stack([one, total - one])
    lengths = jnp.asarray(split_up(number_of, total, bound, slope), jnp.int32)
    couples = (number_of - 1) // 2
    donor, taker = lengths[1:1 + 2 * couples:2], lengths[2:2 + 2 * couples:2]
    margin = jnp.minimum(donor - 1, bound - taker)
    moved = jax.random.randint(jax.random.fold_in(stream_key, 1), (couples,), 0, 1 << 20) % (margin + 1)
    lengths = lengths.at[1:1 + 2 * couples:2].set(donor - moved).at[2:2 + 2 * couples:2].set(taker + moved)
    return lengths[jax.random.permutation(jax.random.fold_in(stream_key, 2), number_of)]


def centred(key, shape, scale, bound, cuts=(), held_as=jnp.bfloat16):
    entries = scale * jax.random.normal(key, shape, jnp.float32)
    if cuts:
        entries = entries * shard_levels(key, shape, cuts, -0.22, 0.18)
    return jnp.clip(entries, -bound, bound).astype(held_as)


def setup_inputs(seed: int = 0) -> dict:
    seeds = jax.random.split(jax.random.key(seed), 19)
    return {
        "tokens": centred(seeds[0], (TOKENS, D), 1.0, 6.0, ((0, 32),)),
        "w_query": centred(seeds[1], (D, D), D ** -0.5, 0.15625, ((1, 4),)),
        "w_key": centred(seeds[2], (D, D), D ** -0.5, 0.15625, ((1, 4),)),
        "w_value": centred(seeds[3], (D, D), D ** -0.5, 0.15625, ((1, 4),)),
        "b_query": centred(seeds[4], (D,), 0.5, 3.0, ((0, 4),), jnp.float32),
        "b_value": centred(seeds[5], (D,), 0.5, 3.0, ((0, 4),), jnp.float32),
        "w_out": centred(seeds[6], (D, D), (max(D // 96, 4)) ** -0.5, 1.75, ((0, 4),)),
        "b_out": centred(seeds[7], (D,), 0.5, 3.0, (), jnp.float32),
        "w_up": centred(seeds[8], (D, FF), D ** -0.5, 0.15625, ((1, 4),)),
        "b_up": centred(seeds[9], (FF,), 0.5, 3.0, ((0, 4),), jnp.float32),
        "w_down": centred(seeds[10], (FF, D), (FF // 4) ** -0.5, 0.15625, ((0, 4),)),
        "b_down": centred(seeds[11], (D,), 0.5, 3.0, (), jnp.float32),
        "gain_attn": jnp.clip(1.0 + 0.1 * jax.random.normal(seeds[12], (D,), jnp.float32), 0.5, 1.5),
        "shift_attn": centred(seeds[13], (D,), 0.3, 2.0, (), jnp.float32),
        "gain_ffn": jnp.clip(1.0 + 0.1 * jax.random.normal(seeds[14], (D,), jnp.float32), 0.5, 1.5),
        "shift_ffn": centred(seeds[15], (D,), 0.3, 2.0, (), jnp.float32),
        "cell_lengths": jax.vmap(lambda own: uneven(own, CELLS, SEQ, MOST_CELL, 2))(jax.random.split(seeds[16], ROWS)).reshape((ROWS, CELLS)).astype(jnp.int32),
        "d_output": centred(seeds[17], (TOKENS, D), 1.0, 6.0, ((0, 32),)),
    }


@jax.custom_vjp
def low(v):
    return lax.optimization_barrier(v.astype(jnp.bfloat16)).astype(jnp.float32)

@jax.custom_vjp
def low_back(v):
    return v

def low_keep(v):
    return (low(v), None)

def low_pass(kept, grad):
    return (grad,)

def back_keep(v):
    return (v, None)

def back_low(kept, grad):
    return (low(grad),)
low.defvjp(low_keep, low_pass)
low_back.defvjp(back_keep, back_low)
norm_eps = 1e-05
masked_score = -1e+30
highest = lax.Precision.HIGHEST

def both_ways(v):
    return low(low_back(v))

def norm_rows(values, gain, shift):
    center = values - lax.optimization_barrier(jnp.mean(values, axis=-1, keepdims=True))
    spread = lax.optimization_barrier(jnp.mean(center * center, axis=-1, keepdims=True))
    return center * lax.rsqrt(spread + norm_eps) * gain + shift

def cell_ids(lengths_row):
    bounds = jnp.cumsum(lengths_row).astype(jnp.int32)
    places = jnp.arange(SEQ, dtype=jnp.int32)
    return lax.optimization_barrier(jnp.sum((places[:, None] >= bounds[None, :]).astype(jnp.int32), axis=1))

def matmul(left, right):
    return jnp.dot(left, right, precision=highest)

def row_forward(row_in, cells, params):
    w_query, w_key, w_value, b_query, b_value, w_out, b_out, w_up, b_up, w_down, b_down, gain_attn, shift_attn, gain_ffn, shift_ffn = params
    normed = low(norm_rows(row_in, gain_attn, shift_attn))
    queries = both_ways(matmul(normed, w_query) + b_query).reshape(SEQ, HEADS, HEAD_DIM)
    key_rows = both_ways(matmul(normed, w_key)).reshape(SEQ, HEADS, HEAD_DIM)
    value_rows = both_ways(matmul(normed, w_value) + b_value).reshape(SEQ, HEADS, HEAD_DIM)
    scores = low_back(jnp.einsum('qhd,khd->hqk', queries, key_rows, precision=highest) * HEAD_DIM ** (-0.5))
    same = cells[:, None] == cells[None, :]
    scores = jnp.where(same[None], scores, masked_score)
    top = lax.optimization_barrier(jnp.max(scores, axis=-1, keepdims=True))
    expo = jnp.exp(scores - top)
    probs = low(expo / lax.optimization_barrier(jnp.sum(expo, axis=-1, keepdims=True)))
    attended = jnp.einsum('hqk,khd->qhd', probs, value_rows, precision=highest)
    attended = both_ways(attended.reshape(SEQ, D))
    middle = row_in + low_back(matmul(attended, w_out) + b_out)
    second = low(norm_rows(middle, gain_ffn, shift_ffn))
    hidden_pre = low_back(matmul(second, w_up) + b_up)
    activated = low(jax.nn.gelu(hidden_pre))
    return middle + low_back(matmul(activated, w_down) + b_down)

def reference(tokens, w_query, w_key, w_value, b_query, b_value, w_out, b_out, w_up, b_up, w_down, b_down, gain_attn, shift_attn, gain_ffn, shift_ffn, cell_lengths, d_output):
    params = tuple((w.astype(jnp.float32) for w in (w_query, w_key, w_value, b_query, b_value, w_out, b_out, w_up, b_up, w_down, b_down, gain_attn, shift_attn, gain_ffn, shift_ffn)))
    inputs = tokens.astype(jnp.float32).reshape(ROWS, SEQ, D)
    cotangents = d_output.astype(jnp.float32).reshape(ROWS, SEQ, D)
    zeros = jax.tree.map(jnp.zeros_like, params)

    def one_row(carry, item):
        row_in, lengths_row, row_cot = item
        cells = cell_ids(lengths_row)

        def forward(values, weights):
            return row_forward(values, cells, weights)
        row_out, pull = jax.vjp(forward, row_in, params)
        row_grad, weight_grads = pull(row_cot)
        carry = jax.tree.map(lambda a, b: a + b, carry, weight_grads)
        return (carry, (row_out.astype(jnp.bfloat16), row_grad))
    grads, (outputs, in_grads) = lax.scan(one_row, zeros, (inputs, cell_lengths, cotangents))
    return (outputs.reshape(TOKENS, D), in_grads.reshape(TOKENS, D), grads[0], grads[1], grads[2], grads[3], grads[4], grads[5], grads[6], grads[7], grads[8], grads[9], grads[10], grads[11], grads[12], grads[13], grads[14])
```

```python
import functools
import heapq

import jax
import jax.numpy as jnp
from jax import lax
from jax.experimental import pallas as pl
from jax.experimental.pallas import tpu as pltpu
from jax.sharding import PartitionSpec as P

D = 1280
HEAD_DIM = 64

MESH_ID = pl.DeviceIdType.MESH
LINK_RATE = 46.8e3
HOP_US = 1.6


def plan_order(chunks, add_us=0.5):
    free = dict.fromkeys(("Oy", "Iy", "OI", "IO", "M"), 0.0)
    order = {"O": [], "I": []}
    clock = {"O": 0.0, "I": 0.0}
    heap, seen = [], set()
    count = [0]

    def push(when, role, k, name):
        heapq.heappush(heap, (when, count[0], role, k, name))
        count[0] += 1

    def send(when, link, size):
        free[link] = max(when, free[link]) + size / LINK_RATE
        return free[link] + HOP_US

    for k, (_, _, ready) in enumerate(chunks):
        push(ready, "O", k, "start")
        push(ready, "I", k, "start")
    end = 0.0
    while heap:
        when, _, role, k, name = heapq.heappop(heap)
        kind, size, _ = chunks[k]
        when = max(when, clock[role])
        if (kind, role, name) == ("A", "I", "r2") and (k, "I", "r1") not in seen:
            push(when + 0.2, role, k, name)
            continue
        when += add_us * size / 800e3 if name in ("r0", "r1", "r2", "r3") else 0.05
        clock[role] = when
        order[role].append((k, name))
        seen.add((k, role, name))
        end = max(end, when)
        for link, part, to, event in SENDS.get((kind, role, name), ()):
            push(send(when, link, size * part), to, k, event)
    return order, end


SENDS = {
    ("A", "O", "start"): (("Oy", 0.5, "O", "r1"),),
    ("A", "I", "start"): (("Iy", 0.5, "I", "r1"),),
    ("A", "O", "r1"): (("OI", 0.5, "I", "r2"),),
    ("A", "I", "r2"): (("M", 0.25, "I", "r3"),),
    ("A", "I", "r3"): (("M", 0.25, "I", "r4"), ("IO", 0.25, "O", "r5a"), ("Iy", 0.25, "I", "r6a")),
    ("A", "I", "r4"): (("IO", 0.25, "O", "r5b"), ("Iy", 0.25, "I", "r6b")),
    ("A", "O", "r5a"): (("Oy", 0.25, "O", "r6a"),),
    ("A", "O", "r5b"): (("Oy", 0.25, "O", "r6b"),),
    ("B", "O", "start"): (("OI", 1.0, "I", "r1"),),
    ("B", "I", "r1"): (("M", 0.5, "I", "r2"),),
    ("B", "I", "r2"): (("Iy", 0.25, "I", "r3"),),
    ("B", "I", "r3"): (("Iy", 0.25, "I", "r4"), ("M", 0.25, "I", "r5a"), ("IO", 0.25, "O", "r6a")),
    ("B", "I", "r4"): (("M", 0.25, "I", "r5b"), ("IO", 0.25, "O", "r6b")),
    ("B", "I", "r5a"): (("IO", 0.25, "O", "r6c"),),
    ("B", "I", "r5b"): (("IO", 0.25, "O", "r6d"),),
    ("C", "O", "start"): (("OI", 0.5, "I", "r1"),),
    ("C", "I", "r1"): (("M", 0.5, "I", "r2"),),
    ("C", "I", "r2"): (("IO", 0.5, "O", "r3"),),
    ("C", "O", "r3"): (("Oy", 0.25, "O", "r0"),),
    ("C", "O", "r0"): (("Oy", 0.25, "O", "r4"), ("OI", 0.25, "I", "r5a")),
    ("C", "O", "r4"): (("OI", 0.25, "I", "r5b"),),
    ("C", "I", "r5a"): (("M", 0.25, "I", "r6a"),),
    ("C", "I", "r5b"): (("M", 0.25, "I", "r6b"),),
    ("C", "I", "r6a"): (("IO", 0.25, "O", "r7a"),),
    ("C", "I", "r6b"): (("IO", 0.25, "O", "r7b"),),
}
EVENTS = ("r0", "r1", "r2", "r3", "r4", "r5a", "r5b", "r6a", "r6b", "r6c", "r6d", "r7a", "r7b")


def slot_rows(kind, rows):
    if kind == "A":
        return {"r1": rows // 2, "r2": rows // 2, "r3": rows // 4}
    if kind == "B":
        return {"r1": rows, "r2": rows // 2, "r3": rows // 4}
    return {"r1": rows // 2, "r2": rows // 2, "r3": rows // 2, "r0": rows // 4}


class AllReduce:
    def __init__(self, chunks, grads, finals, lands, land_at, send_sem, recv_sem):
        self.chunks, self.grads, self.lands, self.land_at = chunks, grads, lands, land_at
        self.finals = finals
        self.send_sem, self.recv_sem = send_sem, recv_sem
        d, self.t = lax.axis_index("dp"), lax.axis_index("tensor")
        self.y, self.z = d % 2, d // 2
        self.side = self.z // 2
        self.inner = jnp.logical_or(self.z == 1, self.z == 2)
        self.to = {
            "y": (self.z * 2 + 1 - self.y, self.t),
            "pair": ((self.z + 1 - 2 * (self.z % 2)) * 2 + self.y, self.t),
            "mid": ((3 - self.z) * 2 + self.y, self.t),
        }
        self.sent = {"O": [], "I": []}

    def region(self, k, half=None, quarter=None, final=False):
        kind, g, first, rows = self.chunks[k]
        start = first
        if half is not None:
            start = start + half * (rows // 2)
            rows = rows // 2
        if quarter is not None:
            start = start + quarter * (rows // 2)
            rows = rows // 2
        if not isinstance(start, int):
            start = pl.multiple_of(start, 16)
        return (self.finals if final else self.grads)[g].at[pl.ds(start, rows)]

    def land(self, k, event):
        kind, g, first, rows = self.chunks[k]
        start, size = self.land_at[(k, event)]
        return self.lands[g].at[pl.ds(start, size)]

    def copy(self, k, event, src, dst, who):
        e = EVENTS.index(event)
        return pltpu.make_async_remote_copy(
            src_ref=src, dst_ref=dst, send_sem=self.send_sem.at[k, e], recv_sem=self.recv_sem.at[k, e],
            device_id=self.to[who], device_id_type=MESH_ID)

    def send(self, role, k, event, src, dst, who):
        c = self.copy(k, event, src, dst, who)
        c.start()
        self.sent[role].append((k, event, src.shape[0]))

    def arrive(self, k, event, dst):
        self.copy(k, event, dst, dst, "y").wait_recv()

    def add(self, k, event, half=None, quarter=None, final=False):
        land = self.land(k, event)
        self.arrive(k, event, land)
        src = self.region(k, half, quarter)
        dst = self.region(k, half, quarter, final)
        rows = land.shape[0]
        step = 32 if rows % 32 == 0 else 16

        def body(i, carry):
            at = pl.ds(pl.multiple_of(i * step, 16), step)
            dst[at] = (src[at].astype(jnp.float32) + land[at].astype(jnp.float32)).astype(jnp.bfloat16)
            return carry

        lax.fori_loop(0, rows // step, body, 0)

    def event(self, role, k, name):
        kind = self.chunks[k][0]
        s, y = self.side, self.y
        R = functools.partial(self.region, k)
        F = functools.partial(self.region, k, final=True)
        send = functools.partial(self.send, role, k)
        key = (kind, role, name)
        if kind == "A":
            if name == "start":
                send("r1", R(1 - y), self.land(k, "r1"), "y")
            elif name == "r1":
                self.add(k, "r1", y)
                if role == "O":
                    send("r2", R(y), self.land(k, "r2"), "pair")
            elif name == "r2":
                self.add(k, "r2", y)
                send("r3", R(y, 1 - s), self.land(k, "r3"), "mid")
            elif name == "r3":
                self.add(k, "r3", y, s, True)
                send("r4", F(y, s), F(y, s), "mid")
                send("r5a", F(y, s), F(y, s), "pair")
                send("r6a", F(y, s), F(y, s), "y")
            elif name == "r4":
                self.arrive(k, "r4", F(y, 1 - s))
                send("r5b", F(y, 1 - s), F(y, 1 - s), "pair")
                send("r6b", F(y, 1 - s), F(y, 1 - s), "y")
            elif name in ("r5a", "r5b"):
                q = s if name == "r5a" else 1 - s
                self.arrive(k, name, F(y, q))
                send("r6" + name[2], F(y, q), F(y, q), "y")
            elif name in ("r6a", "r6b"):
                q = s if name == "r6a" else 1 - s
                self.arrive(k, name, F(1 - y, q))
        elif kind == "B":
            if name == "start":
                if role == "O":
                    send("r1", R(), self.land(k, "r1"), "pair")
            elif name == "r1":
                self.add(k, "r1")
                send("r2", R(1 - s), self.land(k, "r2"), "mid")
            elif name == "r2":
                self.add(k, "r2", s)
                send("r3", R(s, 1 - y), self.land(k, "r3"), "y")
            elif name == "r3":
                self.add(k, "r3", s, y, True)
                for event, who in (("r4", "y"), ("r5a", "mid"), ("r6a", "pair")):
                    send(event, F(s, y), F(s, y), who)
            elif name == "r4":
                self.arrive(k, "r4", F(s, 1 - y))
                for event, who in (("r5b", "mid"), ("r6b", "pair")):
                    send(event, F(s, 1 - y), F(s, 1 - y), who)
            elif name in ("r5a", "r5b"):
                q = y if name == "r5a" else 1 - y
                self.arrive(k, name, F(1 - s, q))
                send("r6c" if name == "r5a" else "r6d", F(1 - s, q), F(1 - s, q), "pair")
            else:
                h = s if name in ("r6a", "r6b") else 1 - s
                q = y if name in ("r6a", "r6c") else 1 - y
                self.arrive(k, name, F(h, q))
        else:
            if name == "start":
                if role == "O":
                    send("r1", R(1 - s), self.land(k, "r1"), "pair")
            elif name == "r1":
                self.add(k, "r1", 1 - s)
                send("r2", R(1 - s), self.land(k, "r2"), "mid")
            elif name == "r2":
                self.add(k, "r2", s)
                send("r3", R(s), self.land(k, "r3"), "pair")
            elif name == "r3":
                self.add(k, "r3", s)
                send("r0", R(s, 1 - y), self.land(k, "r0"), "y")
            elif name == "r0":
                self.add(k, "r0", s, y, True)
                send("r4", F(s, y), F(s, y), "y")
                send("r5a", F(s, y), F(s, y), "pair")
            elif name == "r4":
                self.arrive(k, "r4", F(s, 1 - y))
                send("r5b", F(s, 1 - y), F(s, 1 - y), "pair")
            elif name in ("r5a", "r5b"):
                q = y if name == "r5a" else 1 - y
                self.arrive(k, name, F(s, q))
                send("r6" + name[2], F(s, q), F(s, q), "mid")
            elif name in ("r6a", "r6b"):
                q = y if name == "r6a" else 1 - y
                self.arrive(k, name, F(1 - s, q))
                send("r7" + name[2], F(1 - s, q), F(1 - s, q), "pair")
            else:
                q = y if name == "r7a" else 1 - y
                self.arrive(k, name, F(1 - s, q))

    def run(self, order):
        for role, here in (("I", self.inner), ("O", jnp.logical_not(self.inner))):
            if order[role]:

                @pl.when(here)
                def _(role=role):
                    for k, name in order[role]:
                        if k == "small":
                            self.small.step(name)
                        else:
                            self.event(role, k, name)

    def finish(self):
        for role, here in (("I", self.inner), ("O", jnp.logical_not(self.inner))):
            @pl.when(here)
            def _(role=role):
                for k, event, rows in self.sent[role]:
                    _, g, first, _ = self.chunks[k]
                    src = self.grads[g].at[pl.ds(first, rows)]
                    self.copy(k, event, src, src, "y").wait_send()


def lay_out(chunks, widths):
    at, used = {}, [0] * len(widths)
    for k, (kind, g, first, rows) in enumerate(chunks):
        for event, size in slot_rows(kind, rows).items():
            at[(k, event)] = (used[g], size)
            used[g] += size
    return at, used


class SmallSums:
    def __init__(self, source, totals, lands, send_sem, recv_sem):
        self.source, self.totals, self.lands = source, totals, lands
        self.send_sem, self.recv_sem = send_sem, recv_sem
        d, t = lax.axis_index("dp"), lax.axis_index("tensor")
        y, z = d % 2, d // 2
        self.to = (
            (z * 2 + 1 - y, t),
            ((z + 1 - 2 * (z % 2)) * 2 + y, t),
            (((z + 2) % 4) * 2 + y, t),
            (d, t + 1 - 2 * (t % 2)),
            (d, (t + 2) % 4),
        )

    def copy(self, i):
        src = self.source if i == 0 else self.totals.at[i - 1]
        return pltpu.make_async_remote_copy(
            src_ref=src, dst_ref=self.lands.at[i], send_sem=self.send_sem.at[i],
            recv_sem=self.recv_sem.at[i], device_id=self.to[i], device_id_type=MESH_ID)

    def step(self, i):
        if i > 0:
            self.copy(i - 1).wait_recv()
            have = self.source[...] if i == 1 else self.totals[i - 2]
            self.totals[i - 1] = have + self.lands[i - 1]
        if i < 5:
            self.copy(i).start()

    def finish(self):
        for i in range(5):
            self.copy(i).wait_send()


def reduce_kernel(chunks, order, land_at, *refs):
    sources, small, finals, small_dp, small_all = refs[:4], refs[4], refs[5:9], refs[9], refs[10]
    grads, lands = refs[11:15], refs[15:19]
    send_sem, recv_sem, in_sem, totals, small_lands, small_send, small_recv = refs[19:]
    ar = AllReduce(chunks, grads, finals, lands, land_at, send_sem, recv_sem)
    ar.small = SmallSums(small, totals, small_lands, small_send, small_recv)
    copies = [
        pltpu.make_async_copy(g, o, in_sem.at[i]) for i, (g, o) in enumerate(zip(sources, grads))
    ]
    for c in copies:
        c.start()
    barrier = pltpu.get_barrier_semaphore()
    peers = (ar.to["y"], ar.to["pair"], ar.to["mid"]) + ar.small.to[2:]
    for peer in peers:
        pl.semaphore_signal(barrier, inc=1, device_id=peer, device_id_type=MESH_ID)
    for c in copies:
        c.wait()
    pl.semaphore_wait(barrier, len(peers))
    ar.run(order)
    ar.finish()
    ar.small.finish()
    small_dp[...] = totals[2]
    small_all[...] = totals[4]


def cut_rows(shapes, size, kinds, pace):
    chunks, timed, ready = [], [], 0.0
    for g, (rows, columns) in enumerate(shapes):
        first = 0
        while first < rows:
            here = size if rows - first >= 2 * size or rows - first == size else rows - first
            kind = kinds[len(chunks) % len(kinds)]
            chunks.append((kind, g, first, here))
            timed.append((kind, here * columns * 2, ready))
            ready += pace * here * columns * 2 / LINK_RATE
            first += here
    return chunks, timed


def reduce_over_dp(grads, small):
    shapes = [g.shape for g in grads]
    chunks, timed = cut_rows(shapes, 128, "BACAA", 0.6)
    order, _ = plan_order(timed)
    for role in order:
        for i in range(6):
            order[role].insert(4 + 7 * i, ("small", i))
    land_at, used = lay_out(chunks, shapes)
    any_space = pl.BlockSpec(memory_space=pl.ANY)
    vmem = pl.BlockSpec(memory_space=pltpu.VMEM)
    dma = pltpu.SemaphoreType.DMA
    out = pl.pallas_call(
        functools.partial(reduce_kernel, chunks, order, land_at),
        out_shape=[jax.ShapeDtypeStruct(g.shape, g.dtype) for g in grads]
        + [jax.ShapeDtypeStruct(small.shape, small.dtype)] * 2,
        in_specs=[any_space] * 4 + [vmem],
        out_specs=[vmem] * 6,
        scratch_shapes=[pltpu.VMEM(g.shape, g.dtype) for g in grads]
        + [pltpu.VMEM((u, s[1]), jnp.bfloat16) for u, s in zip(used, shapes)]
        + [dma((len(chunks), len(EVENTS))), dma((len(chunks), len(EVENTS))), dma((4,))]
        + [pltpu.VMEM((5,) + small.shape, jnp.float32)] * 2
        + [dma((5,)), dma((5,))],
        compiler_params=pltpu.CompilerParams(
            collective_id=0, has_side_effects=True, vmem_limit_bytes=60 << 20
        ),
        name="sum_over_dp",
    )(*grads, small)
    return out[:4], out[4], out[5]


norm_eps = 1e-05
masked_score = -1e30


def norm_rows(values, gain, shift):
    center = values - jnp.mean(values, axis=-1, keepdims=True)
    spread = jnp.mean(center * center, axis=-1, keepdims=True)
    return center * lax.rsqrt(spread + norm_eps) * gain + shift


def cell_ids(lengths_row, seq_len):
    bounds = jnp.cumsum(lengths_row)
    places = jnp.arange(seq_len, dtype=jnp.int32)
    return jnp.sum((places[:, None] >= bounds[None, :]).astype(jnp.int32), axis=1)


def inner_rows(left, right):
    return lax.dot_general(
        left, right, (((0,), (0,)), ((), ())), preferred_element_type=jnp.float32
    )


def times_transposed(left, right):
    return lax.dot_general(
        left, right, (((1,), (1,)), ((), ())), preferred_element_type=jnp.float32
    )


def masked_scores(query_block, key_row, cells, lower, block, scale):
    same = cells[lower : lower + block, None] == cells[None, :]
    scores = (
        jnp.einsum("qhd,khd->hqk", query_block, key_row, preferred_element_type=jnp.float32) * scale
    )
    return jnp.where(same[None], scores, masked_score)


def attend_row(query_row, key_row, value_row, cells, scale):
    block = query_row.shape[0] // 2
    pieces = []
    totals = []
    for which_half in range(2):
        lower = which_half * block
        scores = masked_scores(
            query_row[lower : lower + block], key_row, cells, lower, block, scale
        )
        top = jnp.max(scores, axis=-1, keepdims=True)
        expo = jnp.exp(scores - top)
        total = jnp.sum(expo, axis=-1, keepdims=True)
        probs = (expo / total).astype(jnp.bfloat16)
        pieces.append(
            jnp.einsum("hqk,khd->qhd", probs, value_row, preferred_element_type=jnp.float32)
        )
        totals.append(top + jnp.log(total))
    return (jnp.concatenate(pieces, 0).astype(jnp.bfloat16), jnp.concatenate(totals, 1))


def attend_back(query_row, key_row, value_row, grad_row, lse_row, cells, scale):
    block = query_row.shape[0] // 2
    grad_keys = jnp.zeros(key_row.shape, jnp.float32)
    grad_values = jnp.zeros(value_row.shape, jnp.float32)
    query_parts = []
    for which_half in range(2):
        lower = which_half * block
        query_block = query_row[lower : lower + block]
        grad_block = grad_row[lower : lower + block]
        scores = masked_scores(query_block, key_row, cells, lower, block, scale)
        probs = jnp.exp(scores - lse_row[:, lower : lower + block])
        low_probs = probs.astype(jnp.bfloat16)
        grad_values = grad_values + jnp.einsum(
            "hqk,qhd->khd", low_probs, grad_block, preferred_element_type=jnp.float32
        )
        grad_probs = jnp.einsum(
            "qhd,khd->hqk", grad_block, value_row, preferred_element_type=jnp.float32
        )
        offset = jnp.sum(probs * grad_probs, axis=-1, keepdims=True)
        grad_scores = (probs * (grad_probs - offset)).astype(jnp.bfloat16)
        query_parts.append(
            jnp.einsum("hqk,khd->qhd", grad_scores, key_row, preferred_element_type=jnp.float32)
            * scale
        )
        grad_keys = (
            grad_keys
            + jnp.einsum(
                "hqk,qhd->khd", grad_scores, query_block, preferred_element_type=jnp.float32
            )
            * scale
        )
    return (jnp.concatenate(query_parts, 0), grad_keys, grad_values)


def local(
    tokens,
    w_query,
    w_key,
    w_value,
    b_query,
    b_value,
    w_out,
    b_out,
    w_up,
    b_up,
    w_down,
    b_down,
    gain_attn,
    shift_attn,
    gain_ffn,
    shift_ffn,
    cell_lengths,
    d_output,
):
    shard_rows = tokens.shape[0]
    width_tp = lax.axis_size("tensor")
    group_rows = shard_rows * width_tp
    rows_here = cell_lengths.shape[0]
    seq_len = group_rows // rows_here
    local_cols = w_query.shape[1]
    heads_here = local_cols // HEAD_DIM
    hidden_here = w_up.shape[1]
    scale = HEAD_DIM ** (-0.5)
    inputs = tokens.astype(jnp.float32)
    normed = norm_rows(inputs, gain_attn, shift_attn).astype(jnp.bfloat16)
    normed_all = lax.all_gather(normed, "tensor", axis=0, tiled=True)
    w_joined = jnp.concatenate([w_query, w_key, w_value], axis=1)
    bias_joined = jnp.concatenate([b_query, jnp.zeros_like(b_query), b_value])
    projected = jnp.dot(normed_all, w_joined, preferred_element_type=jnp.float32) + bias_joined
    projected = projected.astype(jnp.bfloat16)
    shaped = (rows_here, seq_len, heads_here, HEAD_DIM)
    queries = projected[:, :local_cols].reshape(shaped)
    key_rows = projected[:, local_cols : 2 * local_cols].reshape(shaped)
    value_rows = projected[:, 2 * local_cols :].reshape(shaped)
    cells_all = jax.vmap(lambda lengths_row: cell_ids(lengths_row, seq_len))(cell_lengths)
    attended, lse_all = lax.map(
        lambda item: attend_row(item[0], item[1], item[2], item[3], scale),
        (queries, key_rows, value_rows, cells_all),
    )
    attended = attended.reshape(group_rows, local_cols)
    attn_branch = lax.psum_scatter(
        jnp.dot(
            lax.slice_in_dim(attended, 0, lax.axis_size("tensor") * shard_rows, axis=0),
            w_out,
            preferred_element_type=jnp.float32,
        ).astype(jnp.bfloat16),
        "tensor",
        scatter_dimension=0,
        tiled=True,
    ).astype(jnp.float32)
    middle = inputs + attn_branch + b_out
    second = norm_rows(middle, gain_ffn, shift_ffn).astype(jnp.bfloat16)
    second_all = lax.all_gather(second, "tensor", axis=0, tiled=True)
    hidden_pre = jnp.dot(second_all, w_up, preferred_element_type=jnp.float32) + b_up
    activated = jax.nn.gelu(hidden_pre).astype(jnp.bfloat16)
    ffn_branch = lax.psum_scatter(
        jnp.dot(
            lax.slice_in_dim(activated, 0, shard_rows * lax.axis_size("tensor"), axis=0),
            w_down,
            preferred_element_type=jnp.float32,
        ).astype(jnp.bfloat16),
        "tensor",
        scatter_dimension=0,
        tiled=True,
    ).astype(jnp.float32)
    output = (middle + ffn_branch + b_down).astype(jnp.bfloat16)
    cot_local = d_output.astype(jnp.float32)
    grad_b_down = jnp.sum(cot_local, axis=0)
    piece = lax.all_gather(d_output, "tensor", axis=0, tiled=True)
    grad_down = jnp.zeros((hidden_here, D), jnp.float32)
    count = piece.shape[0]
    act_rows = lax.slice_in_dim(activated, 0, count, axis=0)
    grad_down = grad_down + inner_rows(act_rows, piece)
    grad_act = times_transposed(piece, w_down)
    grad_w_down, grad_act = (grad_down, grad_act)
    gelu_pull = jax.vjp(jax.nn.gelu, hidden_pre)[1]
    grad_pre = gelu_pull(grad_act)[0].astype(jnp.bfloat16)
    grad_b_up = jnp.sum(grad_pre.astype(jnp.float32), axis=0)
    grad_w_up = inner_rows(second_all, grad_pre)
    grad_second = lax.psum_scatter(
        times_transposed(
            lax.slice_in_dim(grad_pre, 0, lax.axis_size("tensor") * shard_rows, axis=0), w_up
        ).astype(jnp.bfloat16),
        "tensor",
        scatter_dimension=0,
        tiled=True,
    ).astype(jnp.float32)
    norm_two_pull = jax.vjp(norm_rows, middle, gain_ffn, shift_ffn)[1]
    mid_part, grad_gain_ffn, grad_shift_ffn = norm_two_pull(grad_second)
    grad_middle = cot_local + mid_part
    branch_grad = grad_middle.astype(jnp.bfloat16)
    grad_b_out = jnp.sum(branch_grad.astype(jnp.float32), axis=0)
    piece = lax.all_gather(branch_grad, "tensor", axis=0, tiled=True)
    start = jnp.int32(0)
    grad_out_w = jnp.zeros((local_cols, D), jnp.float32)
    grad_att = jnp.zeros((group_rows, local_cols), jnp.float32)
    count = piece.shape[0]
    att_rows = lax.dynamic_slice_in_dim(attended, start, count, 0)
    grad_out_w = grad_out_w + inner_rows(att_rows, piece)
    grad_att = lax.dynamic_update_slice_in_dim(grad_att, times_transposed(piece, w_out), start, 0)
    grad_w_out, grad_att = (grad_out_w, grad_att)
    grad_att = grad_att.astype(jnp.bfloat16).reshape(shaped)
    grad_q, grad_k, grad_v = lax.map(
        lambda item: attend_back(item[0], item[1], item[2], item[3], item[4], item[5], scale),
        (queries, key_rows, value_rows, grad_att, lse_all, cells_all),
    )
    grad_joined = jnp.concatenate(
        [
            grad_q.reshape(group_rows, local_cols),
            grad_k.reshape(group_rows, local_cols),
            grad_v.reshape(group_rows, local_cols),
        ],
        axis=1,
    ).astype(jnp.bfloat16)
    grad_col_sums = jnp.sum(grad_joined.astype(jnp.float32), axis=0)
    grad_b_query = grad_col_sums[:local_cols]
    grad_b_value = grad_col_sums[2 * local_cols :]
    grad_w_joined = inner_rows(normed_all, grad_joined)
    grad_first = lax.psum_scatter(
        times_transposed(
            lax.slice_in_dim(grad_joined, 0, shard_rows * lax.axis_size("tensor"), axis=0), w_joined
        ).astype(jnp.bfloat16),
        "tensor",
        scatter_dimension=0,
        tiled=True,
    ).astype(jnp.float32)
    norm_one_pull = jax.vjp(norm_rows, inputs, gain_attn, shift_attn)[1]
    in_part, grad_gain_attn, grad_shift_attn = norm_one_pull(grad_first)
    d_tokens = grad_middle + in_part
    grad_b_query, grad_b_value = grad_col_sums[:local_cols], grad_col_sums[2 * local_cols :]
    wide = (grad_b_out, grad_b_down, grad_gain_attn, grad_shift_attn, grad_gain_ffn, grad_shift_ffn)
    if lax.axis_size("dp") == 8:
        last = jnp.concatenate([grad_b_query, grad_b_value])
        last = jnp.pad(last, (0, D - last.shape[0]))
        small = jnp.stack(wide + (grad_b_up, last))
        grads = [
            g.astype(jnp.bfloat16) for g in (grad_w_down, grad_w_up, grad_w_out, grad_w_joined)
        ]
        grads, small_dp, small_all = reduce_over_dp(grads, small)
        grad_w_down, grad_w_up, grad_w_out, grad_w_joined = [g.astype(jnp.float32) for g in grads]
        wide = tuple(small_all[i] for i in range(6))
        grad_b_up = small_dp[6]
        grad_b_query = small_dp[7, :local_cols]
        grad_b_value = small_dp[7, local_cols : 2 * local_cols]
    else:
        sums = (grad_w_down, grad_w_up, grad_w_out, grad_w_joined, grad_b_up, grad_b_query, grad_b_value)
        sums = lax.psum(sums, "dp")
        grad_w_down, grad_w_up, grad_w_out, grad_w_joined, grad_b_up, grad_b_query, grad_b_value = sums
        wide = lax.psum(wide, ("dp", "tensor"))
    grad_b_out, grad_b_down, grad_gain_attn, grad_shift_attn, grad_gain_ffn, grad_shift_ffn = wide
    grad_w_query = grad_w_joined[:, :local_cols]
    grad_w_key = grad_w_joined[:, local_cols : 2 * local_cols]
    grad_w_value = grad_w_joined[:, 2 * local_cols :]
    return (
        output,
        d_tokens,
        grad_w_query,
        grad_w_key,
        grad_w_value,
        grad_b_query,
        grad_b_value,
        grad_w_out,
        grad_b_out,
        grad_w_up,
        grad_b_up,
        grad_w_down,
        grad_b_down,
        grad_gain_attn,
        grad_shift_attn,
        grad_gain_ffn,
        grad_shift_ffn,
    )


def solution(mesh):
    in_specs = (
        P(("dp", "tensor"), None),
        P(None, "tensor"),
        P(None, "tensor"),
        P(None, "tensor"),
        P("tensor"),
        P("tensor"),
        P("tensor", None),
        P(),
        P(None, "tensor"),
        P("tensor"),
        P("tensor", None),
        P(),
        P(),
        P(),
        P(),
        P(),
        P("dp", None),
        P(("dp", "tensor"), None),
    )
    out_specs = (
        P(("dp", "tensor"), None),
        P(("dp", "tensor"), None),
        P(None, "tensor"),
        P(None, "tensor"),
        P(None, "tensor"),
        P("tensor"),
        P("tensor"),
        P("tensor", None),
        P(),
        P(None, "tensor"),
        P("tensor"),
        P("tensor", None),
        P(),
        P(),
        P(),
        P(),
        P(),
    )
    return jax.shard_map(local, mesh=mesh, in_specs=in_specs, out_specs=out_specs, check_vma=False)
```

```python
import functools
import heapq

import jax
import jax.numpy as jnp
from jax import lax
from jax.experimental import pallas as pl
from jax.experimental.pallas import tpu as pltpu
from jax.sharding import PartitionSpec as P

D = 1280
HEAD_DIM = 64

MESH_ID = pl.DeviceIdType.MESH
LINK_RATE = 46.8e3
HOP_US = 1.6
DP, TP = "dp", "tensor"

KIND_A, KIND_B, KIND_C = range(3)
SMALL = -1
OUTER, INNER = range(2)
OUT_Y, IN_Y, OUT_IN, IN_OUT, MID = range(5)
TO_Y, TO_PAIR, TO_MID = range(3)
START, R0, R1, R2, R3, R4, R5A, R5B, R6A, R6B, R6C, R6D, R7A, R7B = range(14)


def plan_order(chunks, add_us=0.5):
    free = dict.fromkeys((OUT_Y, IN_Y, OUT_IN, IN_OUT, MID), 0.0)
    order = {OUTER: [], INNER: []}
    clock = {OUTER: 0.0, INNER: 0.0}
    heap, seen = [], set()
    count = [0]

    def push(when, role, k, name):
        heapq.heappush(heap, (when, count[0], role, k, name))
        count[0] += 1

    def send(when, link, size):
        free[link] = max(when, free[link]) + size / LINK_RATE
        return free[link] + HOP_US

    for k, (_, _, ready) in enumerate(chunks):
        push(ready, OUTER, k, START)
        push(ready, INNER, k, START)
    end = 0.0
    while heap:
        when, _, role, k, name = heapq.heappop(heap)
        kind, size, _ = chunks[k]
        when = max(when, clock[role])
        if (kind, role, name) == (KIND_A, INNER, R2) and (k, INNER, R1) not in seen:
            push(when + 0.2, role, k, name)
            continue
        when += add_us * size / 800e3 if name in (R0, R1, R2, R3) else 0.05
        clock[role] = when
        order[role].append((k, name))
        seen.add((k, role, name))
        end = max(end, when)
        for link, part, to, event in SENDS.get((kind, role, name), ()):
            push(send(when, link, size * part), to, k, event)
    return order, end


SENDS = {
    (KIND_A, OUTER, START): ((OUT_Y, 0.5, OUTER, R1),),
    (KIND_A, INNER, START): ((IN_Y, 0.5, INNER, R1),),
    (KIND_A, OUTER, R1): ((OUT_IN, 0.5, INNER, R2),),
    (KIND_A, INNER, R2): ((MID, 0.25, INNER, R3),),
    (KIND_A, INNER, R3): ((MID, 0.25, INNER, R4), (IN_OUT, 0.25, OUTER, R5A), (IN_Y, 0.25, INNER, R6A)),
    (KIND_A, INNER, R4): ((IN_OUT, 0.25, OUTER, R5B), (IN_Y, 0.25, INNER, R6B)),
    (KIND_A, OUTER, R5A): ((OUT_Y, 0.25, OUTER, R6A),),
    (KIND_A, OUTER, R5B): ((OUT_Y, 0.25, OUTER, R6B),),
    (KIND_B, OUTER, START): ((OUT_IN, 1.0, INNER, R1),),
    (KIND_B, INNER, R1): ((MID, 0.5, INNER, R2),),
    (KIND_B, INNER, R2): ((IN_Y, 0.25, INNER, R3),),
    (KIND_B, INNER, R3): ((IN_Y, 0.25, INNER, R4), (MID, 0.25, INNER, R5A), (IN_OUT, 0.25, OUTER, R6A)),
    (KIND_B, INNER, R4): ((MID, 0.25, INNER, R5B), (IN_OUT, 0.25, OUTER, R6B)),
    (KIND_B, INNER, R5A): ((IN_OUT, 0.25, OUTER, R6C),),
    (KIND_B, INNER, R5B): ((IN_OUT, 0.25, OUTER, R6D),),
    (KIND_C, OUTER, START): ((OUT_IN, 0.5, INNER, R1),),
    (KIND_C, INNER, R1): ((MID, 0.5, INNER, R2),),
    (KIND_C, INNER, R2): ((IN_OUT, 0.5, OUTER, R3),),
    (KIND_C, OUTER, R3): ((OUT_Y, 0.25, OUTER, R0),),
    (KIND_C, OUTER, R0): ((OUT_Y, 0.25, OUTER, R4), (OUT_IN, 0.25, INNER, R5A)),
    (KIND_C, OUTER, R4): ((OUT_IN, 0.25, INNER, R5B),),
    (KIND_C, INNER, R5A): ((MID, 0.25, INNER, R6A),),
    (KIND_C, INNER, R5B): ((MID, 0.25, INNER, R6B),),
    (KIND_C, INNER, R6A): ((IN_OUT, 0.25, OUTER, R7A),),
    (KIND_C, INNER, R6B): ((IN_OUT, 0.25, OUTER, R7B),),
}
EVENTS = (R0, R1, R2, R3, R4, R5A, R5B, R6A, R6B, R6C, R6D, R7A, R7B)


def slot_rows(kind, rows):
    if kind == KIND_A:
        return {R1: rows // 2, R2: rows // 2, R3: rows // 4}
    if kind == KIND_B:
        return {R1: rows, R2: rows // 2, R3: rows // 4}
    return {R1: rows // 2, R2: rows // 2, R3: rows // 2, R0: rows // 4}


class AllReduce:
    def __init__(self, chunks, grads, finals, lands, land_at, send_sem, recv_sem):
        self.chunks, self.grads, self.lands, self.land_at = chunks, grads, lands, land_at
        self.finals = finals
        self.send_sem, self.recv_sem = send_sem, recv_sem
        d, self.t = lax.axis_index(DP), lax.axis_index(TP)
        self.y, self.z = d % 2, d // 2
        self.side = self.z // 2
        self.inner = jnp.logical_or(self.z == 1, self.z == 2)
        self.to = {
            TO_Y: (self.z * 2 + 1 - self.y, self.t),
            TO_PAIR: ((self.z + 1 - 2 * (self.z % 2)) * 2 + self.y, self.t),
            TO_MID: ((3 - self.z) * 2 + self.y, self.t),
        }
        self.sent = {OUTER: [], INNER: []}

    def region(self, k, half=None, quarter=None, final=False):
        kind, g, first, rows = self.chunks[k]
        start = first
        if half is not None:
            start = start + half * (rows // 2)
            rows = rows // 2
        if quarter is not None:
            start = start + quarter * (rows // 2)
            rows = rows // 2
        if not isinstance(start, int):
            start = pl.multiple_of(start, 16)
        return (self.finals if final else self.grads)[g].at[pl.ds(start, rows)]

    def land(self, k, event):
        kind, g, first, rows = self.chunks[k]
        start, size = self.land_at[(k, event)]
        return self.lands[g].at[pl.ds(start, size)]

    def copy(self, k, event, src, dst, who):
        e = EVENTS.index(event)
        return pltpu.make_async_remote_copy(
            src_ref=src, dst_ref=dst, send_sem=self.send_sem.at[k, e], recv_sem=self.recv_sem.at[k, e],
            device_id=self.to[who], device_id_type=MESH_ID)

    def send(self, role, k, event, src, dst, who):
        c = self.copy(k, event, src, dst, who)
        c.start()
        self.sent[role].append((k, event, src.shape[0]))

    def arrive(self, k, event, dst):
        self.copy(k, event, dst, dst, TO_Y).wait_recv()

    def add(self, k, event, half=None, quarter=None, final=False):
        land = self.land(k, event)
        self.arrive(k, event, land)
        src = self.region(k, half, quarter)
        dst = self.region(k, half, quarter, final)
        rows = land.shape[0]
        step = 32 if rows % 32 == 0 else 16

        def body(i, carry):
            at = pl.ds(pl.multiple_of(i * step, 16), step)
            dst[at] = (src[at].astype(jnp.float32) + land[at].astype(jnp.float32)).astype(jnp.bfloat16)
            return carry

        lax.fori_loop(0, rows // step, body, 0)

    def event(self, role, k, name):
        kind = self.chunks[k][0]
        s, y = self.side, self.y
        R = functools.partial(self.region, k)
        F = functools.partial(self.region, k, final=True)
        send = functools.partial(self.send, role, k)
        key = (kind, role, name)
        if kind == KIND_A:
            if name == START:
                send(R1, R(1 - y), self.land(k, R1), TO_Y)
            elif name == R1:
                self.add(k, R1, y)
                if role == OUTER:
                    send(R2, R(y), self.land(k, R2), TO_PAIR)
            elif name == R2:
                self.add(k, R2, y)
                send(R3, R(y, 1 - s), self.land(k, R3), TO_MID)
            elif name == R3:
                self.add(k, R3, y, s, True)
                send(R4, F(y, s), F(y, s), TO_MID)
                send(R5A, F(y, s), F(y, s), TO_PAIR)
                send(R6A, F(y, s), F(y, s), TO_Y)
            elif name == R4:
                self.arrive(k, R4, F(y, 1 - s))
                send(R5B, F(y, 1 - s), F(y, 1 - s), TO_PAIR)
                send(R6B, F(y, 1 - s), F(y, 1 - s), TO_Y)
            elif name in (R5A, R5B):
                q = s if name == R5A else 1 - s
                self.arrive(k, name, F(y, q))
                send(R6A + name - R5A, F(y, q), F(y, q), TO_Y)
            elif name in (R6A, R6B):
                q = s if name == R6A else 1 - s
                self.arrive(k, name, F(1 - y, q))
        elif kind == KIND_B:
            if name == START:
                if role == OUTER:
                    send(R1, R(), self.land(k, R1), TO_PAIR)
            elif name == R1:
                self.add(k, R1)
                send(R2, R(1 - s), self.land(k, R2), TO_MID)
            elif name == R2:
                self.add(k, R2, s)
                send(R3, R(s, 1 - y), self.land(k, R3), TO_Y)
            elif name == R3:
                self.add(k, R3, s, y, True)
                for event, who in ((R4, TO_Y), (R5A, TO_MID), (R6A, TO_PAIR)):
                    send(event, F(s, y), F(s, y), who)
            elif name == R4:
                self.arrive(k, R4, F(s, 1 - y))
                for event, who in ((R5B, TO_MID), (R6B, TO_PAIR)):
                    send(event, F(s, 1 - y), F(s, 1 - y), who)
            elif name in (R5A, R5B):
                q = y if name == R5A else 1 - y
                self.arrive(k, name, F(1 - s, q))
                send(R6C if name == R5A else R6D, F(1 - s, q), F(1 - s, q), TO_PAIR)
            else:
                h = s if name in (R6A, R6B) else 1 - s
                q = y if name in (R6A, R6C) else 1 - y
                self.arrive(k, name, F(h, q))
        else:
            if name == START:
                if role == OUTER:
                    send(R1, R(1 - s), self.land(k, R1), TO_PAIR)
            elif name == R1:
                self.add(k, R1, 1 - s)
                send(R2, R(1 - s), self.land(k, R2), TO_MID)
            elif name == R2:
                self.add(k, R2, s)
                send(R3, R(s), self.land(k, R3), TO_PAIR)
            elif name == R3:
                self.add(k, R3, s)
                send(R0, R(s, 1 - y), self.land(k, R0), TO_Y)
            elif name == R0:
                self.add(k, R0, s, y, True)
                send(R4, F(s, y), F(s, y), TO_Y)
                send(R5A, F(s, y), F(s, y), TO_PAIR)
            elif name == R4:
                self.arrive(k, R4, F(s, 1 - y))
                send(R5B, F(s, 1 - y), F(s, 1 - y), TO_PAIR)
            elif name in (R5A, R5B):
                q = y if name == R5A else 1 - y
                self.arrive(k, name, F(s, q))
                send(R6A + name - R5A, F(s, q), F(s, q), TO_MID)
            elif name in (R6A, R6B):
                q = y if name == R6A else 1 - y
                self.arrive(k, name, F(1 - s, q))
                send(R7A + name - R6A, F(1 - s, q), F(1 - s, q), TO_PAIR)
            else:
                q = y if name == R7A else 1 - y
                self.arrive(k, name, F(1 - s, q))

    def run(self, order):
        for role, here in ((INNER, self.inner), (OUTER, jnp.logical_not(self.inner))):
            if order[role]:

                @pl.when(here)
                def _(role=role):
                    for k, name in order[role]:
                        if k == SMALL:
                            self.small.step(name)
                        else:
                            self.event(role, k, name)

    def finish(self):
        for role, here in ((INNER, self.inner), (OUTER, jnp.logical_not(self.inner))):
            @pl.when(here)
            def _(role=role):
                for k, event, rows in self.sent[role]:
                    _, g, first, _ = self.chunks[k]
                    src = self.grads[g].at[pl.ds(first, rows)]
                    self.copy(k, event, src, src, TO_Y).wait_send()


def lay_out(chunks, widths):
    at, used = {}, [0] * len(widths)
    for k, (kind, g, first, rows) in enumerate(chunks):
        for event, size in slot_rows(kind, rows).items():
            at[(k, event)] = (used[g], size)
            used[g] += size
    return at, used


class SmallSums:
    def __init__(self, source, totals, lands, send_sem, recv_sem):
        self.source, self.totals, self.lands = source, totals, lands
        self.send_sem, self.recv_sem = send_sem, recv_sem
        d, t = lax.axis_index(DP), lax.axis_index(TP)
        y, z = d % 2, d // 2
        self.to = (
            (z * 2 + 1 - y, t),
            ((z + 1 - 2 * (z % 2)) * 2 + y, t),
            (((z + 2) % 4) * 2 + y, t),
            (d, t + 1 - 2 * (t % 2)),
            (d, (t + 2) % 4),
        )

    def copy(self, i):
        src = self.source if i == 0 else self.totals.at[i - 1]
        return pltpu.make_async_remote_copy(
            src_ref=src, dst_ref=self.lands.at[i], send_sem=self.send_sem.at[i],
            recv_sem=self.recv_sem.at[i], device_id=self.to[i], device_id_type=MESH_ID)

    def step(self, i):
        if i > 0:
            self.copy(i - 1).wait_recv()
            have = self.source[...] if i == 1 else self.totals[i - 2]
            self.totals[i - 1] = have + self.lands[i - 1]
        if i < 5:
            self.copy(i).start()

    def finish(self):
        for i in range(5):
            self.copy(i).wait_send()


def reduce_kernel(chunks, order, land_at, *refs):
    sources, small, finals, small_dp, small_all = refs[:4], refs[4], refs[5:9], refs[9], refs[10]
    grads, lands = refs[11:15], refs[15:19]
    send_sem, recv_sem, in_sem, totals, small_lands, small_send, small_recv = refs[19:]
    ar = AllReduce(chunks, grads, finals, lands, land_at, send_sem, recv_sem)
    ar.small = SmallSums(small, totals, small_lands, small_send, small_recv)
    copies = [
        pltpu.make_async_copy(g, o, in_sem.at[i]) for i, (g, o) in enumerate(zip(sources, grads))
    ]
    for c in copies:
        c.start()
    barrier = pltpu.get_barrier_semaphore()
    peers = (ar.to[TO_Y], ar.to[TO_PAIR], ar.to[TO_MID]) + ar.small.to[2:]
    for peer in peers:
        pl.semaphore_signal(barrier, inc=1, device_id=peer, device_id_type=MESH_ID)
    for c in copies:
        c.wait()
    pl.semaphore_wait(barrier, len(peers))
    ar.run(order)
    ar.finish()
    ar.small.finish()
    small_dp[...] = totals[2]
    small_all[...] = totals[4]


def cut_rows(shapes, size, kinds, pace):
    chunks, timed, ready = [], [], 0.0
    for g, (rows, columns) in enumerate(shapes):
        first = 0
        while first < rows:
            here = size if rows - first >= 2 * size or rows - first == size else rows - first
            kind = kinds[len(chunks) % len(kinds)]
            chunks.append((kind, g, first, here))
            timed.append((kind, here * columns * 2, ready))
            ready += pace * here * columns * 2 / LINK_RATE
            first += here
    return chunks, timed


def reduce_over_dp(grads, small):
    shapes = [g.shape for g in grads]
    chunks, timed = cut_rows(shapes, 128, (KIND_B, KIND_A, KIND_C, KIND_A, KIND_A), 0.6)
    order, _ = plan_order(timed)
    for role in order:
        for i in range(6):
            order[role].insert(4 + 7 * i, (SMALL, i))
    land_at, used = lay_out(chunks, shapes)
    any_space = pl.BlockSpec(memory_space=pl.ANY)
    vmem = pl.BlockSpec(memory_space=pltpu.VMEM)
    dma = pltpu.SemaphoreType.DMA
    out = pl.pallas_call(
        functools.partial(reduce_kernel, chunks, order, land_at),
        out_shape=[jax.ShapeDtypeStruct(g.shape, g.dtype) for g in grads]
        + [jax.ShapeDtypeStruct(small.shape, small.dtype)] * 2,
        in_specs=[any_space] * 4 + [vmem],
        out_specs=[vmem] * 6,
        scratch_shapes=[pltpu.VMEM(g.shape, g.dtype) for g in grads]
        + [pltpu.VMEM((u, s[1]), jnp.bfloat16) for u, s in zip(used, shapes)]
        + [dma((len(chunks), len(EVENTS))), dma((len(chunks), len(EVENTS))), dma((4,))]
        + [pltpu.VMEM((5,) + small.shape, jnp.float32)] * 2
        + [dma((5,)), dma((5,))],
        compiler_params=pltpu.CompilerParams(
            collective_id=0, has_side_effects=True, vmem_limit_bytes=60 << 20
        ),
        name="sum_over_dp",
    )(*grads, small)
    return out[:4], out[4], out[5]


norm_eps = 1e-05
MASKED = -1e30
MOST_CELL = 384


def norm_rows(values, gain, shift):
    center = values - jnp.mean(values, axis=-1, keepdims=True)
    spread = jnp.mean(center * center, axis=-1, keepdims=True)
    return center * lax.rsqrt(spread + norm_eps) * gain + shift


def inner_rows(left, right):
    return lax.dot_general(
        left, right, (((0,), (0,)), ((), ())), preferred_element_type=jnp.float32
    )


def times_transposed(left, right):
    return lax.dot_general(
        left, right, (((1,), (1,)), ((), ())), preferred_element_type=jnp.float32
    )


def each_cell(lengths, row, seq_len, body):
    widths = sorted({min(w, seq_len) for w in (128, 256, MOST_CELL + 16)})

    def step(i, start):
        length = lengths[row, i]
        lower = 0
        for width in widths:
            first = pl.multiple_of(jnp.minimum(start // 16 * 16, seq_len - width), 16)

            @pl.when(jnp.logical_and(length > lower, length <= width - 16))
            def _(width=width, first=first):
                down = first + lax.broadcasted_iota(jnp.int32, (width, 1), 0)
                along = first + lax.broadcasted_iota(jnp.int32, (1, width), 1)
                inside = [jnp.logical_and(p >= start, p < start + length) for p in (down, along)]
                body(first, width, inside[0], inside[1])

            lower = width - 16
        return start + length

    lax.fori_loop(0, lengths.shape[1], step, jnp.int32(0))


def attend_kernel(heads, lengths, joined, out, lse):
    seq_len, wide = out.shape

    def body(first, width, down, along):
        rows = pl.ds(first, width)
        seen = jnp.logical_and(down, along)
        for h in range(heads):
            at = h * HEAD_DIM
            query = joined[rows, at : at + HEAD_DIM] * jnp.bfloat16(HEAD_DIM**-0.5)
            key = joined[rows, wide + at : wide + at + HEAD_DIM]
            value = joined[rows, 2 * wide + at : 2 * wide + at + HEAD_DIM]
            scores = jnp.where(seen, times_transposed(query, key), MASKED)
            top = jnp.max(scores, axis=1, keepdims=True)
            expo = jnp.exp(scores - top)
            total = jnp.sum(expo, axis=1, keepdims=True)
            probs = (expo * (1.0 / total)).astype(jnp.bfloat16)
            part = jnp.dot(probs, value, preferred_element_type=jnp.float32).astype(jnp.bfloat16)
            cols = slice(at, at + HEAD_DIM)
            out[rows, cols] = jnp.where(down, part, out[rows, cols])
            lse[rows, h : h + 1] = jnp.where(down, top + jnp.log(total), lse[rows, h : h + 1])

    each_cell(lengths, pl.program_id(0), seq_len, body)


def attend_back_kernel(heads, lengths, joined, grad, lse, out):
    seq_len, wide = grad.shape
    scale = HEAD_DIM**-0.5

    def body(first, width, down, along):
        rows = pl.ds(first, width)
        seen = jnp.logical_and(down, along)
        for h in range(heads):
            at = h * HEAD_DIM
            query = joined[rows, at : at + HEAD_DIM] * jnp.bfloat16(scale)
            key = joined[rows, wide + at : wide + at + HEAD_DIM]
            value = joined[rows, 2 * wide + at : 2 * wide + at + HEAD_DIM]
            cot = grad[rows, at : at + HEAD_DIM]
            scores = jnp.where(seen, times_transposed(query, key), MASKED)
            probs = jnp.exp(scores - lse[rows, h : h + 1])
            d_value = inner_rows(probs.astype(jnp.bfloat16), cot)
            d_probs = times_transposed(cot, value)
            offset = jnp.sum(probs * d_probs, axis=1, keepdims=True)
            d_scores = (probs * (d_probs - offset)).astype(jnp.bfloat16)
            d_query = jnp.dot(d_scores, key, preferred_element_type=jnp.float32) * scale
            d_key = inner_rows(d_scores, query)
            for i, part in enumerate((d_query, d_key, d_value)):
                cols = slice(i * wide + at, i * wide + at + HEAD_DIM)
                out[rows, cols] = jnp.where(down, part.astype(jnp.bfloat16), out[rows, cols])

    each_cell(lengths, pl.program_id(0), seq_len, body)


def attend(joined, lengths):
    n, wide = lengths.shape[0], joined.shape[1] // 3
    seq_len = joined.shape[0] // n
    heads = wide // HEAD_DIM
    return pl.pallas_call(
        functools.partial(attend_kernel, heads),
        grid=(n,),
        out_shape=[
            jax.ShapeDtypeStruct((joined.shape[0], wide), jnp.bfloat16),
            jax.ShapeDtypeStruct((joined.shape[0], 128), jnp.float32),
        ],
        in_specs=[
            pl.BlockSpec(memory_space=pltpu.SMEM),
            pl.BlockSpec((seq_len, 3 * wide), lambda i: (i, 0)),
        ],
        out_specs=[
            pl.BlockSpec((seq_len, wide), lambda i: (i, 0)),
            pl.BlockSpec((seq_len, 128), lambda i: (i, 0)),
        ],
        compiler_params=pltpu.CompilerParams(vmem_limit_bytes=40 << 20),
        name="attend",
    )(lengths, joined)


def attend_back(joined, grad, lse, lengths):
    n, wide = lengths.shape[0], grad.shape[1]
    seq_len = joined.shape[0] // n
    heads = wide // HEAD_DIM
    return pl.pallas_call(
        functools.partial(attend_back_kernel, heads),
        grid=(n,),
        out_shape=jax.ShapeDtypeStruct(joined.shape, jnp.bfloat16),
        in_specs=[
            pl.BlockSpec(memory_space=pltpu.SMEM),
            pl.BlockSpec((seq_len, 3 * wide), lambda i: (i, 0)),
            pl.BlockSpec((seq_len, wide), lambda i: (i, 0)),
            pl.BlockSpec((seq_len, 128), lambda i: (i, 0)),
        ],
        out_specs=pl.BlockSpec((seq_len, 3 * wide), lambda i: (i, 0)),
        compiler_params=pltpu.CompilerParams(vmem_limit_bytes=40 << 20),
        name="attend_back",
    )(lengths, joined, grad, lse)


def local(
    tokens,
    w_query,
    w_key,
    w_value,
    b_query,
    b_value,
    w_out,
    b_out,
    w_up,
    b_up,
    w_down,
    b_down,
    gain_attn,
    shift_attn,
    gain_ffn,
    shift_ffn,
    cell_lengths,
    d_output,
):
    shard_rows = tokens.shape[0]
    width_tp = lax.axis_size(TP)
    group_rows = shard_rows * width_tp
    local_cols = w_query.shape[1]
    hidden_here = w_up.shape[1]
    inputs = tokens.astype(jnp.float32)
    normed = norm_rows(inputs, gain_attn, shift_attn).astype(jnp.bfloat16)
    normed_all = lax.all_gather(normed, TP, axis=0, tiled=True)
    w_joined = jnp.concatenate([w_query, w_key, w_value], axis=1)
    bias_joined = jnp.concatenate([b_query, jnp.zeros_like(b_query), b_value])
    projected = jnp.dot(normed_all, w_joined, preferred_element_type=jnp.float32) + bias_joined
    projected = projected.astype(jnp.bfloat16)
    attended, lse = attend(projected, cell_lengths)
    attn_branch = lax.psum_scatter(
        jnp.dot(
            lax.slice_in_dim(attended, 0, lax.axis_size(TP) * shard_rows, axis=0),
            w_out,
            preferred_element_type=jnp.float32,
        ).astype(jnp.bfloat16),
        TP,
        scatter_dimension=0,
        tiled=True,
    ).astype(jnp.float32)
    middle = inputs + attn_branch + b_out
    second = norm_rows(middle, gain_ffn, shift_ffn).astype(jnp.bfloat16)
    second_all = lax.all_gather(second, TP, axis=0, tiled=True)
    hidden_pre = jnp.dot(second_all, w_up, preferred_element_type=jnp.float32) + b_up
    activated = jax.nn.gelu(hidden_pre).astype(jnp.bfloat16)
    ffn_branch = lax.psum_scatter(
        jnp.dot(
            lax.slice_in_dim(activated, 0, shard_rows * lax.axis_size(TP), axis=0),
            w_down,
            preferred_element_type=jnp.float32,
        ).astype(jnp.bfloat16),
        TP,
        scatter_dimension=0,
        tiled=True,
    ).astype(jnp.float32)
    output = (middle + ffn_branch + b_down).astype(jnp.bfloat16)
    cot_local = d_output.astype(jnp.float32)
    grad_b_down = jnp.sum(cot_local, axis=0)
    piece = lax.all_gather(d_output, TP, axis=0, tiled=True)
    grad_down = jnp.zeros((hidden_here, D), jnp.float32)
    count = piece.shape[0]
    act_rows = lax.slice_in_dim(activated, 0, count, axis=0)
    grad_down = grad_down + inner_rows(act_rows, piece)
    grad_act = times_transposed(piece, w_down)
    grad_w_down, grad_act = (grad_down, grad_act)
    gelu_pull = jax.vjp(jax.nn.gelu, hidden_pre)[1]
    grad_pre = gelu_pull(grad_act)[0].astype(jnp.bfloat16)
    grad_b_up = jnp.sum(grad_pre.astype(jnp.float32), axis=0)
    grad_w_up = inner_rows(second_all, grad_pre)
    grad_second = lax.psum_scatter(
        times_transposed(
            lax.slice_in_dim(grad_pre, 0, lax.axis_size(TP) * shard_rows, axis=0), w_up
        ).astype(jnp.bfloat16),
        TP,
        scatter_dimension=0,
        tiled=True,
    ).astype(jnp.float32)
    norm_two_pull = jax.vjp(norm_rows, middle, gain_ffn, shift_ffn)[1]
    mid_part, grad_gain_ffn, grad_shift_ffn = norm_two_pull(grad_second)
    grad_middle = cot_local + mid_part
    branch_grad = grad_middle.astype(jnp.bfloat16)
    grad_b_out = jnp.sum(branch_grad.astype(jnp.float32), axis=0)
    piece = lax.all_gather(branch_grad, TP, axis=0, tiled=True)
    grad_w_out = inner_rows(attended, piece)
    grad_att = times_transposed(piece, w_out)
    grad_joined = attend_back(projected, grad_att.astype(jnp.bfloat16), lse, cell_lengths)
    grad_col_sums = jnp.sum(grad_joined.astype(jnp.float32), axis=0)
    grad_b_query = grad_col_sums[:local_cols]
    grad_b_value = grad_col_sums[2 * local_cols :]
    grad_w_joined = inner_rows(normed_all, grad_joined)
    grad_first = lax.psum_scatter(
        times_transposed(
            lax.slice_in_dim(grad_joined, 0, shard_rows * lax.axis_size(TP), axis=0), w_joined
        ).astype(jnp.bfloat16),
        TP,
        scatter_dimension=0,
        tiled=True,
    ).astype(jnp.float32)
    norm_one_pull = jax.vjp(norm_rows, inputs, gain_attn, shift_attn)[1]
    in_part, grad_gain_attn, grad_shift_attn = norm_one_pull(grad_first)
    d_tokens = grad_middle + in_part
    grad_b_query, grad_b_value = grad_col_sums[:local_cols], grad_col_sums[2 * local_cols :]
    wide = (grad_b_out, grad_b_down, grad_gain_attn, grad_shift_attn, grad_gain_ffn, grad_shift_ffn)
    if lax.axis_size(DP) == 8:
        last = jnp.concatenate([grad_b_query, grad_b_value])
        last = jnp.pad(last, (0, D - last.shape[0]))
        small = jnp.stack(wide + (grad_b_up, last))
        grads = [
            g.astype(jnp.bfloat16) for g in (grad_w_down, grad_w_up, grad_w_out, grad_w_joined)
        ]
        grads, small_dp, small_all = reduce_over_dp(grads, small)
        grad_w_down, grad_w_up, grad_w_out, grad_w_joined = [g.astype(jnp.float32) for g in grads]
        wide = tuple(small_all[i] for i in range(6))
        grad_b_up = small_dp[6]
        grad_b_query = small_dp[7, :local_cols]
        grad_b_value = small_dp[7, local_cols : 2 * local_cols]
    else:
        sums = (grad_w_down, grad_w_up, grad_w_out, grad_w_joined, grad_b_up, grad_b_query, grad_b_value)
        sums = lax.psum(sums, DP)
        grad_w_down, grad_w_up, grad_w_out, grad_w_joined, grad_b_up, grad_b_query, grad_b_value = sums
        wide = lax.psum(wide, (DP, TP))
    grad_b_out, grad_b_down, grad_gain_attn, grad_shift_attn, grad_gain_ffn, grad_shift_ffn = wide
    grad_w_query = grad_w_joined[:, :local_cols]
    grad_w_key = grad_w_joined[:, local_cols : 2 * local_cols]
    grad_w_value = grad_w_joined[:, 2 * local_cols :]
    return (
        output,
        d_tokens,
        grad_w_query,
        grad_w_key,
        grad_w_value,
        grad_b_query,
        grad_b_value,
        grad_w_out,
        grad_b_out,
        grad_w_up,
        grad_b_up,
        grad_w_down,
        grad_b_down,
        grad_gain_attn,
        grad_shift_attn,
        grad_gain_ffn,
        grad_shift_ffn,
    )


def solution(mesh):
    in_specs = (
        P((DP, TP), None),
        P(None, TP),
        P(None, TP),
        P(None, TP),
        P(TP),
        P(TP),
        P(TP, None),
        P(),
        P(None, TP),
        P(TP),
        P(TP, None),
        P(),
        P(),
        P(),
        P(),
        P(),
        P(DP, None),
        P((DP, TP), None),
    )
    out_specs = (
        P((DP, TP), None),
        P((DP, TP), None),
        P(None, TP),
        P(None, TP),
        P(None, TP),
        P(TP),
        P(TP),
        P(TP, None),
        P(),
        P(None, TP),
        P(TP),
        P(TP, None),
        P(),
        P(),
        P(),
        P(),
        P(),
    )
    return jax.shard_map(local, mesh=mesh, in_specs=in_specs, out_specs=out_specs, check_vma=False)
```

```python
import functools
import heapq

import jax
import jax.numpy as jnp
from jax import lax
from jax.experimental import pallas as pl
from jax.experimental.pallas import tpu as pltpu
from jax.sharding import PartitionSpec as P

D = 1280
HEAD_DIM = 64

MESH_ID = pl.DeviceIdType.MESH
LINK_RATE = 46.8e3
HOP_US = 1.6
DP, TP = "dp", "tensor"

KIND_A, KIND_B, KIND_C = range(3)
SMALL = -1
OUTER, INNER = range(2)
OUT_Y, IN_Y, OUT_IN, IN_OUT, MID = range(5)
TO_Y, TO_PAIR, TO_MID = range(3)
START, R0, R1, R2, R3, R4, R5A, R5B, R6A, R6B, R6C, R6D, R7A, R7B = range(14)


def plan_order(chunks, gaps, small, add_us=0.5, margin=1.0):
    free = dict.fromkeys((OUT_Y, IN_Y, OUT_IN, IN_OUT, MID), 0.0)
    order = [{OUTER: [], INNER: []} for _ in gaps]
    clock = {OUTER: 0.0, INNER: 0.0}
    heap, seen = [], set()
    count = [0]

    def push(when, role, k, name):
        heapq.heappush(heap, (when, count[0], role, k, name))
        count[0] += 1

    def send(when, link, size):
        free[link] = max(when, free[link]) + size / LINK_RATE
        return free[link] + HOP_US

    for slot, gap in enumerate(gaps):
        last = slot == len(gaps) - 1
        for role in clock:
            clock[role] += gap
        for k, (_, _, ready) in enumerate(chunks):
            if ready == slot:
                push(clock[OUTER], OUTER, k, START)
                push(clock[INNER], INNER, k, START)
        if small and last:
            for role in clock:
                for i in range(6):
                    push(max(clock.values()) + 2.5 * i, role, SMALL, i)
        later, now = [], max(clock.values())
        while heap:
            when, n, role, k, name = heapq.heappop(heap)
            if k == SMALL:
                clock[role] = max(when, clock[role])
                order[slot][role].append((k, name))
                continue
            kind, size, _ = chunks[k]
            if not last and name != START and when + margin > now:
                later.append((when, n, role, k, name))
                continue
            when = max(when, clock[role])
            if (kind, role, name) == (KIND_A, INNER, R2) and (k, INNER, R1) not in seen:
                push(when + 0.2, role, k, name)
                continue
            when += add_us * size / 800e3 if name in (R0, R1, R2, R3) else 0.05
            clock[role] = when
            order[slot][role].append((k, name))
            seen.add((k, role, name))
            for link, part, to, event in SENDS.get((kind, role, name), ()):
                push(send(when, link, size * part), to, k, event)
        for item in later:
            heapq.heappush(heap, item)
    return order, max(clock.values())


SENDS = {
    (KIND_A, OUTER, START): ((OUT_Y, 0.5, OUTER, R1),),
    (KIND_A, INNER, START): ((IN_Y, 0.5, INNER, R1),),
    (KIND_A, OUTER, R1): ((OUT_IN, 0.5, INNER, R2),),
    (KIND_A, INNER, R2): ((MID, 0.25, INNER, R3),),
    (KIND_A, INNER, R3): ((MID, 0.25, INNER, R4), (IN_OUT, 0.25, OUTER, R5A), (IN_Y, 0.25, INNER, R6A)),
    (KIND_A, INNER, R4): ((IN_OUT, 0.25, OUTER, R5B), (IN_Y, 0.25, INNER, R6B)),
    (KIND_A, OUTER, R5A): ((OUT_Y, 0.25, OUTER, R6A),),
    (KIND_A, OUTER, R5B): ((OUT_Y, 0.25, OUTER, R6B),),
    (KIND_B, OUTER, START): ((OUT_IN, 1.0, INNER, R1),),
    (KIND_B, INNER, R1): ((MID, 0.5, INNER, R2),),
    (KIND_B, INNER, R2): ((IN_Y, 0.25, INNER, R3),),
    (KIND_B, INNER, R3): ((IN_Y, 0.25, INNER, R4), (MID, 0.25, INNER, R5A), (IN_OUT, 0.25, OUTER, R6A)),
    (KIND_B, INNER, R4): ((MID, 0.25, INNER, R5B), (IN_OUT, 0.25, OUTER, R6B)),
    (KIND_B, INNER, R5A): ((IN_OUT, 0.25, OUTER, R6C),),
    (KIND_B, INNER, R5B): ((IN_OUT, 0.25, OUTER, R6D),),
    (KIND_C, OUTER, START): ((OUT_IN, 0.5, INNER, R1),),
    (KIND_C, INNER, R1): ((MID, 0.5, INNER, R2),),
    (KIND_C, INNER, R2): ((IN_OUT, 0.5, OUTER, R3),),
    (KIND_C, OUTER, R3): ((OUT_Y, 0.25, OUTER, R0),),
    (KIND_C, OUTER, R0): ((OUT_Y, 0.25, OUTER, R4), (OUT_IN, 0.25, INNER, R5A)),
    (KIND_C, OUTER, R4): ((OUT_IN, 0.25, INNER, R5B),),
    (KIND_C, INNER, R5A): ((MID, 0.25, INNER, R6A),),
    (KIND_C, INNER, R5B): ((MID, 0.25, INNER, R6B),),
    (KIND_C, INNER, R6A): ((IN_OUT, 0.25, OUTER, R7A),),
    (KIND_C, INNER, R6B): ((IN_OUT, 0.25, OUTER, R7B),),
}
EVENTS = (R0, R1, R2, R3, R4, R5A, R5B, R6A, R6B, R6C, R6D, R7A, R7B)


def slot_rows(kind, rows):
    if kind == KIND_A:
        return {R1: rows // 2, R2: rows // 2, R3: rows // 4}
    if kind == KIND_B:
        return {R1: rows, R2: rows // 2, R3: rows // 4}
    return {R1: rows // 2, R2: rows // 2, R3: rows // 2, R0: rows // 4}


class AllReduce:
    def __init__(self, chunks, grads, finals, lands, land_at, send_sem, recv_sem):
        self.chunks, self.grads, self.lands, self.land_at = chunks, grads, lands, land_at
        self.finals = finals
        self.send_sem, self.recv_sem = send_sem, recv_sem
        d, self.t = lax.axis_index(DP), lax.axis_index(TP)
        self.y, self.z = d % 2, d // 2
        self.side = self.z // 2
        self.inner = jnp.logical_or(self.z == 1, self.z == 2)
        self.to = {
            TO_Y: (self.z * 2 + 1 - self.y, self.t),
            TO_PAIR: ((self.z + 1 - 2 * (self.z % 2)) * 2 + self.y, self.t),
            TO_MID: ((3 - self.z) * 2 + self.y, self.t),
        }
        self.sent = {OUTER: [], INNER: []}

    def region(self, k, half=None, quarter=None, final=False):
        kind, g, first, rows = self.chunks[k]
        start = first
        if half is not None:
            start = start + half * (rows // 2)
            rows = rows // 2
        if quarter is not None:
            start = start + quarter * (rows // 2)
            rows = rows // 2
        if not isinstance(start, int):
            start = pl.multiple_of(start, 16)
        return (self.finals if final else self.grads)[g].at[pl.ds(start, rows)]

    def land(self, k, event):
        kind, g, first, rows = self.chunks[k]
        start, size = self.land_at[(k, event)]
        return self.lands[g].at[pl.ds(start, size)]

    def copy(self, k, event, src, dst, who):
        e = EVENTS.index(event)
        return pltpu.make_async_remote_copy(
            src_ref=src, dst_ref=dst, send_sem=self.send_sem.at[k, e], recv_sem=self.recv_sem.at[k, e],
            device_id=self.to[who], device_id_type=MESH_ID)

    def send(self, role, k, event, src, dst, who):
        c = self.copy(k, event, src, dst, who)
        c.start()
        self.sent[role].append((k, event, src.shape[0]))

    def arrive(self, k, event, dst):
        self.copy(k, event, dst, dst, TO_Y).wait_recv()

    def add(self, k, event, half=None, quarter=None, final=False):
        land = self.land(k, event)
        self.arrive(k, event, land)
        src = self.region(k, half, quarter)
        dst = self.region(k, half, quarter, final)
        rows = land.shape[0]
        step = 32 if rows % 32 == 0 else 16

        def body(i, carry):
            at = pl.ds(pl.multiple_of(i * step, 16), step)
            dst[at] = (src[at].astype(jnp.float32) + land[at].astype(jnp.float32)).astype(jnp.bfloat16)
            return carry

        lax.fori_loop(0, rows // step, body, 0)

    def event(self, role, k, name):
        kind = self.chunks[k][0]
        s, y = self.side, self.y
        R = functools.partial(self.region, k)
        F = functools.partial(self.region, k, final=True)
        send = functools.partial(self.send, role, k)
        key = (kind, role, name)
        if kind == KIND_A:
            if name == START:
                send(R1, R(1 - y), self.land(k, R1), TO_Y)
            elif name == R1:
                self.add(k, R1, y)
                if role == OUTER:
                    send(R2, R(y), self.land(k, R2), TO_PAIR)
            elif name == R2:
                self.add(k, R2, y)
                send(R3, R(y, 1 - s), self.land(k, R3), TO_MID)
            elif name == R3:
                self.add(k, R3, y, s, True)
                send(R4, F(y, s), F(y, s), TO_MID)
                send(R5A, F(y, s), F(y, s), TO_PAIR)
                send(R6A, F(y, s), F(y, s), TO_Y)
            elif name == R4:
                self.arrive(k, R4, F(y, 1 - s))
                send(R5B, F(y, 1 - s), F(y, 1 - s), TO_PAIR)
                send(R6B, F(y, 1 - s), F(y, 1 - s), TO_Y)
            elif name in (R5A, R5B):
                q = s if name == R5A else 1 - s
                self.arrive(k, name, F(y, q))
                send(R6A + name - R5A, F(y, q), F(y, q), TO_Y)
            elif name in (R6A, R6B):
                q = s if name == R6A else 1 - s
                self.arrive(k, name, F(1 - y, q))
        elif kind == KIND_B:
            if name == START:
                if role == OUTER:
                    send(R1, R(), self.land(k, R1), TO_PAIR)
            elif name == R1:
                self.add(k, R1)
                send(R2, R(1 - s), self.land(k, R2), TO_MID)
            elif name == R2:
                self.add(k, R2, s)
                send(R3, R(s, 1 - y), self.land(k, R3), TO_Y)
            elif name == R3:
                self.add(k, R3, s, y, True)
                for event, who in ((R4, TO_Y), (R5A, TO_MID), (R6A, TO_PAIR)):
                    send(event, F(s, y), F(s, y), who)
            elif name == R4:
                self.arrive(k, R4, F(s, 1 - y))
                for event, who in ((R5B, TO_MID), (R6B, TO_PAIR)):
                    send(event, F(s, 1 - y), F(s, 1 - y), who)
            elif name in (R5A, R5B):
                q = y if name == R5A else 1 - y
                self.arrive(k, name, F(1 - s, q))
                send(R6C if name == R5A else R6D, F(1 - s, q), F(1 - s, q), TO_PAIR)
            else:
                h = s if name in (R6A, R6B) else 1 - s
                q = y if name in (R6A, R6C) else 1 - y
                self.arrive(k, name, F(h, q))
        else:
            if name == START:
                if role == OUTER:
                    send(R1, R(1 - s), self.land(k, R1), TO_PAIR)
            elif name == R1:
                self.add(k, R1, 1 - s)
                send(R2, R(1 - s), self.land(k, R2), TO_MID)
            elif name == R2:
                self.add(k, R2, s)
                send(R3, R(s), self.land(k, R3), TO_PAIR)
            elif name == R3:
                self.add(k, R3, s)
                send(R0, R(s, 1 - y), self.land(k, R0), TO_Y)
            elif name == R0:
                self.add(k, R0, s, y, True)
                send(R4, F(s, y), F(s, y), TO_Y)
                send(R5A, F(s, y), F(s, y), TO_PAIR)
            elif name == R4:
                self.arrive(k, R4, F(s, 1 - y))
                send(R5B, F(s, 1 - y), F(s, 1 - y), TO_PAIR)
            elif name in (R5A, R5B):
                q = y if name == R5A else 1 - y
                self.arrive(k, name, F(s, q))
                send(R6A + name - R5A, F(s, q), F(s, q), TO_MID)
            elif name in (R6A, R6B):
                q = y if name == R6A else 1 - y
                self.arrive(k, name, F(1 - s, q))
                send(R7A + name - R6A, F(1 - s, q), F(1 - s, q), TO_PAIR)
            else:
                q = y if name == R7A else 1 - y
                self.arrive(k, name, F(1 - s, q))

    def run(self, order):
        for role, here in ((INNER, self.inner), (OUTER, jnp.logical_not(self.inner))):
            if order[role]:

                @pl.when(here)
                def _(role=role):
                    for k, name in order[role]:
                        if k == SMALL:
                            self.small.step(name)
                        else:
                            self.event(role, k, name)

    def finish(self):
        for role, here in ((INNER, self.inner), (OUTER, jnp.logical_not(self.inner))):
            @pl.when(here)
            def _(role=role):
                for k, event, rows in self.sent[role]:
                    _, g, first, _ = self.chunks[k]
                    src = self.grads[g].at[pl.ds(first, rows)]
                    self.copy(k, event, src, src, TO_Y).wait_send()


def lay_out(chunks, widths):
    at, used = {}, [0] * len(widths)
    for k, (kind, g, first, rows) in enumerate(chunks):
        for event, size in slot_rows(kind, rows).items():
            at[(k, event)] = (used[g], size)
            used[g] += size
    return at, used


class SmallSums:
    def __init__(self, source, totals, lands, send_sem, recv_sem):
        self.source, self.totals, self.lands = source, totals, lands
        self.send_sem, self.recv_sem = send_sem, recv_sem
        d, t = lax.axis_index(DP), lax.axis_index(TP)
        y, z = d % 2, d // 2
        self.to = (
            (z * 2 + 1 - y, t),
            ((z + 1 - 2 * (z % 2)) * 2 + y, t),
            (((z + 2) % 4) * 2 + y, t),
            (d, t + 1 - 2 * (t % 2)),
            (d, (t + 2) % 4),
        )

    def copy(self, i):
        src = self.source if i == 0 else self.totals.at[i - 1]
        return pltpu.make_async_remote_copy(
            src_ref=src, dst_ref=self.lands.at[i], send_sem=self.send_sem.at[i],
            recv_sem=self.recv_sem.at[i], device_id=self.to[i], device_id_type=MESH_ID)

    def step(self, i):
        if i > 0:
            self.copy(i - 1).wait_recv()
            have = self.source[...] if i == 1 else self.totals[i - 2]
            self.totals[i - 1] = have + self.lands[i - 1]
        if i < 5:
            self.copy(i).start()

    def finish(self):
        for i in range(5):
            self.copy(i).wait_send()


norm_eps = 1e-05
MASKED = -1e30
MOST_CELL = 384


def norm_rows(values, gain, shift):
    center = values - jnp.mean(values, axis=-1, keepdims=True)
    spread = jnp.mean(center * center, axis=-1, keepdims=True)
    return center * lax.rsqrt(spread + norm_eps) * gain + shift


def inner_rows(left, right):
    return lax.dot_general(
        left, right, (((0,), (0,)), ((), ())), preferred_element_type=jnp.float32
    )


def times_transposed(left, right):
    return lax.dot_general(
        left, right, (((1,), (1,)), ((), ())), preferred_element_type=jnp.float32
    )


def each_cell(lengths, row, seq_len, body):
    widths = sorted({min(w, seq_len) for w in (128, 256, MOST_CELL + 16)})

    def step(i, start):
        length = lengths[row, i]
        lower = 0
        for width in widths:
            first = pl.multiple_of(jnp.minimum(start // 16 * 16, seq_len - width), 16)

            @pl.when(jnp.logical_and(length > lower, length <= width - 16))
            def _(width=width, first=first):
                down = first + lax.broadcasted_iota(jnp.int32, (width, 1), 0)
                along = first + lax.broadcasted_iota(jnp.int32, (1, width), 1)
                inside = [jnp.logical_and(p >= start, p < start + length) for p in (down, along)]
                body(first, width, inside[0], inside[1])

            lower = width - 16
        return start + length

    lax.fori_loop(0, lengths.shape[1], step, jnp.int32(0))


def attend_kernel(heads, lengths, joined, out, lse):
    seq_len, wide = out.shape

    def body(first, width, down, along):
        rows = pl.ds(first, width)
        seen = jnp.logical_and(down, along)
        for h in range(heads):
            at = h * HEAD_DIM
            query = joined[rows, at : at + HEAD_DIM] * jnp.bfloat16(HEAD_DIM**-0.5)
            key = joined[rows, wide + at : wide + at + HEAD_DIM]
            value = joined[rows, 2 * wide + at : 2 * wide + at + HEAD_DIM]
            scores = jnp.where(seen, times_transposed(query, key), MASKED)
            top = jnp.max(scores, axis=1, keepdims=True)
            expo = jnp.exp(scores - top)
            total = jnp.sum(expo, axis=1, keepdims=True)
            probs = (expo * (1.0 / total)).astype(jnp.bfloat16)
            part = jnp.dot(probs, value, preferred_element_type=jnp.float32).astype(jnp.bfloat16)
            cols = slice(at, at + HEAD_DIM)
            out[rows, cols] = jnp.where(down, part, out[rows, cols])
            lse[rows, h : h + 1] = jnp.where(down, top + jnp.log(total), lse[rows, h : h + 1])

    each_cell(lengths, pl.program_id(0), seq_len, body)


def attend_back_kernel(heads, lengths, joined, grad, lse, out):
    seq_len, wide = grad.shape
    scale = HEAD_DIM**-0.5

    def body(first, width, down, along):
        rows = pl.ds(first, width)
        seen = jnp.logical_and(down, along)
        for h in range(heads):
            at = h * HEAD_DIM
            query = joined[rows, at : at + HEAD_DIM] * jnp.bfloat16(scale)
            key = joined[rows, wide + at : wide + at + HEAD_DIM]
            value = joined[rows, 2 * wide + at : 2 * wide + at + HEAD_DIM]
            cot = grad[rows, at : at + HEAD_DIM]
            scores = jnp.where(seen, times_transposed(query, key), MASKED)
            probs = jnp.exp(scores - lse[rows, h : h + 1])
            d_value = inner_rows(probs.astype(jnp.bfloat16), cot)
            d_probs = times_transposed(cot, value)
            offset = jnp.sum(probs * d_probs, axis=1, keepdims=True)
            d_scores = (probs * (d_probs - offset)).astype(jnp.bfloat16)
            d_query = jnp.dot(d_scores, key, preferred_element_type=jnp.float32) * scale
            d_key = inner_rows(d_scores, query)
            for i, part in enumerate((d_query, d_key, d_value)):
                cols = slice(i * wide + at, i * wide + at + HEAD_DIM)
                out[rows, cols] = jnp.where(down, part.astype(jnp.bfloat16), out[rows, cols])

    each_cell(lengths, pl.program_id(0), seq_len, body)


def attend(joined, lengths):
    n, wide = lengths.shape[0], joined.shape[1] // 3
    seq_len = joined.shape[0] // n
    heads = wide // HEAD_DIM
    return pl.pallas_call(
        functools.partial(attend_kernel, heads),
        grid=(n,),
        out_shape=[
            jax.ShapeDtypeStruct((joined.shape[0], wide), jnp.bfloat16),
            jax.ShapeDtypeStruct((joined.shape[0], 128), jnp.float32),
        ],
        in_specs=[
            pl.BlockSpec(memory_space=pltpu.SMEM),
            pl.BlockSpec((seq_len, 3 * wide), lambda i: (i, 0)),
        ],
        out_specs=[
            pl.BlockSpec((seq_len, wide), lambda i: (i, 0)),
            pl.BlockSpec((seq_len, 128), lambda i: (i, 0)),
        ],
        compiler_params=pltpu.CompilerParams(vmem_limit_bytes=40 << 20),
        name="attend",
    )(lengths, joined)


def attend_back(joined, grad, lse, lengths):
    n, wide = lengths.shape[0], grad.shape[1]
    seq_len = joined.shape[0] // n
    heads = wide // HEAD_DIM
    return pl.pallas_call(
        functools.partial(attend_back_kernel, heads),
        grid=(n,),
        out_shape=jax.ShapeDtypeStruct(joined.shape, jnp.bfloat16),
        in_specs=[
            pl.BlockSpec(memory_space=pltpu.SMEM),
            pl.BlockSpec((seq_len, 3 * wide), lambda i: (i, 0)),
            pl.BlockSpec((seq_len, wide), lambda i: (i, 0)),
            pl.BlockSpec((seq_len, 128), lambda i: (i, 0)),
        ],
        out_specs=pl.BlockSpec((seq_len, 3 * wide), lambda i: (i, 0)),
        compiler_params=pltpu.CompilerParams(vmem_limit_bytes=40 << 20),
        name="attend_back",
    )(lengths, joined, grad, lse)


COLS = 256
BLOCK = 16


class Refs:
    def __init__(self, names, refs):
        self.__dict__.update(zip(names, refs))


def call(body, name, ins, loose, outs, scratch, collective_id):
    names = list(ins) + list(loose) + list(outs) + list(scratch)
    vmem = pl.BlockSpec(memory_space=pltpu.VMEM)
    out = pl.pallas_call(
        lambda *refs: body(Refs(names, refs)),
        out_shape=list(outs.values()),
        in_specs=[vmem] * len(ins) + [pl.BlockSpec(memory_space=pl.ANY)] * len(loose),
        out_specs=[vmem] * len(outs),
        scratch_shapes=list(scratch.values()),
        compiler_params=pltpu.CompilerParams(
            collective_id=collective_id, has_side_effects=True, vmem_limit_bytes=64000 << 10
        ),
        name=name,
    )(*ins.values(), *loose.values())
    return Refs(list(outs), out)


def low(*shape):
    return pltpu.VMEM(shape, jnp.bfloat16)


def full(*shape):
    return pltpu.VMEM(shape, jnp.float32)


def dma(*shape):
    return pltpu.SemaphoreType.DMA(shape)


def at_row(start, rows):
    return pl.ds(pl.multiple_of(start, 16), rows)


def at_col(i, cols=COLS):
    return pl.ds(pl.multiple_of(i * cols, cols), cols)


def remote(src, dst, send, recv, to):
    return pltpu.make_async_remote_copy(
        src_ref=src, dst_ref=dst, send_sem=send, recv_sem=recv, device_id=to, device_id_type=MESH_ID)


class Place:
    def __init__(self):
        self.d, self.t = lax.axis_index(DP), lax.axis_index(TP)
        self.across = self.t + 1 - 2 * (self.t % 2)
        self.beyond = (self.t + 2) % 4
        self.far = 3 - self.t

    def group(self):
        return [(self.d, self.across), (self.d, self.beyond)]


def meet(peers):
    barrier = pltpu.get_barrier_semaphore()
    for peer in peers:
        pl.semaphore_signal(barrier, inc=1, device_id=peer, device_id_type=MESH_ID)
    pl.semaphore_wait(barrier, len(peers))


class Gather:
    def __init__(self, place, whole, send, recv, cuts):
        self.p, self.whole, self.send, self.recv, self.cuts = place, whole, send, recv, cuts
        self.rows = sum(rows for _, rows in cuts)

    def piece(self, owner, i):
        first, rows = self.cuts[i]
        return self.whole.at[at_row(owner * self.rows + first, rows)]

    def copy(self, kind, i, owner):
        ref = self.piece(owner, i)
        to = self.p.beyond if kind == 1 else self.p.across
        return remote(ref, ref, self.send.at[kind, i], self.recv.at[kind, i], (self.p.d, to))

    def start(self, i):
        self.copy(1, i, self.p.t).start()
        self.copy(0, i, self.p.t).start()

    def across(self):
        for i in range(len(self.cuts)):
            self.copy(0, i, self.p.across).wait_recv()

    def beyond(self):
        for i in range(len(self.cuts)):
            self.copy(1, i, self.p.beyond).wait_recv()
            self.copy(2, i, self.p.beyond).start()

    def far(self):
        for i in range(len(self.cuts)):
            self.copy(2, i, self.p.far).wait_recv()

    def finish(self):
        for i in range(len(self.cuts)):
            self.copy(0, i, self.p.t).wait_send()
            self.copy(1, i, self.p.t).wait_send()
            self.copy(2, i, self.p.beyond).wait_send()


class Scatter:
    def __init__(self, place, rows, out, near, cross, last, own, send, recv):
        self.p, self.rows = place, rows
        self.out, self.near, self.cross, self.last, self.own = out, near, cross, last, own
        self.send, self.recv = send, recv

    def copies(self):
        d, p = self.p.d, self.p
        return (
            remote(self.out.at[0], self.near.at[0], self.send.at[0], self.recv.at[0], (d, p.across)),
            remote(self.out.at[1], self.near.at[1], self.send.at[1], self.recv.at[1], (d, p.across)),
            remote(self.cross, self.last, self.send.at[2], self.recv.at[2], (d, p.beyond)),
        )

    def start(self, compute):
        copies = self.copies()

        def keep(slot):
            def store(j, value):
                self.out[slot, :, at_col(j)] = value.astype(jnp.bfloat16)

            return store

        def add(j, value):
            total = value + self.near[0, :, at_col(j)].astype(jnp.float32)
            self.cross[:, at_col(j)] = total.astype(jnp.bfloat16)

        def hold(j, value):
            self.own[:, at_col(j)] = value

        compute(self.p.far * self.rows, keep(0))
        copies[0].start()
        compute(self.p.across * self.rows, keep(1))
        copies[1].start()
        copies[0].wait_recv()
        compute(self.p.beyond * self.rows, add)
        copies[2].start()
        compute(self.p.t * self.rows, hold)

    def arrive(self):
        copies = self.copies()
        copies[1].wait_recv()
        copies[2].wait_recv()

    def total(self, rows):
        return self.own[rows] + (self.near[1, rows].astype(jnp.float32) + self.last[rows].astype(jnp.float32))

    def finish(self):
        for c in self.copies():
            c.wait_send()


def scatter_scratch(prefix, rows):
    return {
        prefix + "out": low(2, rows, D), prefix + "near": low(2, rows, D), prefix + "cross": low(rows, D),
        prefix + "last": low(rows, D), prefix + "own": full(rows, D),
        prefix + "send": dma(3), prefix + "recv": dma(3),
    }


def scatter_of(refs, prefix, place, rows):
    names = ("out", "near", "cross", "last", "own", "send", "recv")
    return Scatter(place, rows, *[getattr(refs, prefix + n) for n in names])


def cuts_of(rows):
    half = (rows // 2 + 15) // 16 * 16
    return ((0, half), (half, rows - half))


def each_block(rows, body, init=0):
    def step(i, carry):
        out = body(at_row(i * BLOCK, BLOCK), carry)
        return carry if out is None else out

    return lax.fori_loop(0, rows // BLOCK, step, init)


def each_col(width, body):
    def step(j, carry):
        body(j)
        return carry

    lax.fori_loop(0, width // COLS, step, 0)


def norm_back(x, cot, gain):
    center = x - jnp.mean(x, axis=-1, keepdims=True)
    rate = lax.rsqrt(jnp.mean(center * center, axis=-1, keepdims=True) + norm_eps)
    hat = center * rate
    inner = cot * gain
    part = inner - jnp.mean(inner, axis=-1, keepdims=True) - hat * jnp.mean(inner * hat, axis=-1, keepdims=True)
    return part * rate, cot * hat


def reduce_scratch(chunks, shapes):
    at, used = lay_out(chunks, shapes)
    out = {}
    for i, (u, s) in enumerate(zip(used, shapes)):
        out["land%d" % i] = low(max(u, 16), s[1])
    out["send"] = dma(max(len(chunks), 1), len(EVENTS))
    out["recv"] = dma(max(len(chunks), 1), len(EVENTS))
    return out, at


def cut_rows(pieces, size, kinds):
    chunks, timed = [], []
    for g, first, rows, columns, slot in pieces:
        end = first + rows
        while first < end:
            here = size if end - first >= 2 * size or end - first == size else end - first
            kind = kinds[len(chunks) % len(kinds)]
            chunks.append((kind, g, first, here))
            timed.append((kind, here * columns * 2, slot))
            first += here
    return chunks, timed


def tail_kernel(chunks, order, land_at, reduce, r):
    place = Place()
    rows = r.tokens.shape[0]
    wide = r.w.shape[0]
    step = iter(order)
    if reduce:
        up, out, joined = r.up, r.out, r.joined
        ar = AllReduce(
            chunks, (up, out, joined), (r.sum_up, r.sum_out, r.sum_joined), (r.land0, r.land1, r.land2),
            land_at, r.send, r.recv)
        ar.small = SmallSums(r.small, r.totals, r.small_lands, r.small_send, r.small_recv)
        peers = [ar.to[TO_Y], ar.to[TO_PAIR], ar.to[TO_MID], ar.small.to[2]] + place.group()
    else:
        up, out, joined = r.sum_up, r.sum_out, r.sum_joined
        peers = place.group()
    fills = [pltpu.make_async_copy(r.up_in, up, r.fill.at[0]), pltpu.make_async_copy(r.out_in, out, r.fill.at[1])]
    for f in fills:
        f.start()
    meet(peers)
    for f in fills:
        f.wait()

    def advance():
        if reduce:
            ar.run(next(step))

    advance()
    scatter = scatter_of(r, "s", place, rows)

    def to_first(first, store):
        cots = r.cots[at_row(first, rows)]
        each_col(D, lambda j: store(j, jnp.dot(cots, r.w[:, at_col(j)], preferred_element_type=jnp.float32)))

    scatter.start(to_first)
    advance()
    for i in range(0, wide, COLS):
        n = min(COLS, wide - i)
        joined[i : i + n] = inner_rows(r.cots[:, i : i + n], r.normed[...]).astype(jnp.bfloat16)
        advance()
    r.small[...] = r.small_in[...]
    r.small[7:8, :wide] = each_block(
        r.cots.shape[0], lambda at, c: c + jnp.sum(r.cots[at].astype(jnp.float32), axis=0, keepdims=True),
        jnp.zeros((1, wide), jnp.float32))
    advance()
    scatter.arrive()
    gain = r.gain[...]

    def back(at, carry):
        cot = scatter.total(at)
        part, gained = norm_back(r.tokens[at].astype(jnp.float32), cot, gain)
        r.d_tokens[at] = r.d_mid[at] + part
        return carry[0] + gained, carry[1] + cot

    zero = jnp.zeros((BLOCK, D), jnp.float32)
    d_gain, d_shift = each_block(rows, back, (zero, zero))
    r.small[2:3] = jnp.sum(d_gain, axis=0, keepdims=True)
    r.small[3:4] = jnp.sum(d_shift, axis=0, keepdims=True)
    scatter.finish()
    advance()
    if reduce:
        ar.finish()
        ar.small.finish()
        r.small_dp[...] = r.totals[2]
        r.small_all[...] = r.totals[4]
    else:
        r.small_dp[...] = r.small[...]
        r.small_all[...] = r.small[...]


def copy_of(x):
    return jax.ShapeDtypeStruct(x.shape, x.dtype)


KINDS = (KIND_B, KIND_A, KIND_C, KIND_A, KIND_A)


def tail(cots, normed, w, tokens, d_mid, gain, up, out, small, reduce):
    rows, wide = tokens.shape[0], w.shape[0]
    joined = jax.ShapeDtypeStruct((wide, D), jnp.bfloat16)
    shapes = [up.shape, out.shape, joined.shape]
    pieces = [(0, 0, up.shape[0], D, 0), (1, 0, out.shape[0], D, 0)]
    pieces += [(2, i, min(COLS, wide - i), D, 2 + i // COLS) for i in range(0, wide, COLS)]
    chunks, timed = cut_rows(pieces, 128, KINDS)
    gaps = [0.0, 8.0] + [2.0] * len(range(0, wide, COLS)) + [2.0, 4.0]
    order, _ = plan_order(timed, gaps, True)
    scratch = scatter_scratch("s", rows)
    scratch.update(small=full(8, D), fill=dma(2))
    land_at = None
    if reduce:
        more, land_at = reduce_scratch(chunks, shapes)
        scratch.update(more)
        scratch.update(
            up=low(*up.shape), out=low(*out.shape), joined=low(wide, D), totals=full(5, 8, D),
            small_lands=full(5, 8, D), small_send=dma(5), small_recv=dma(5))
    return call(
        functools.partial(tail_kernel, chunks, order, land_at, reduce), "tail",
        dict(cots=cots, normed=normed, w=w, tokens=tokens, d_mid=d_mid, gain=gain.reshape(1, D), small_in=small),
        dict(up_in=up, out_in=out),
        dict(d_tokens=jax.ShapeDtypeStruct((rows, D), jnp.float32), sum_up=copy_of(up), sum_out=copy_of(out),
             sum_joined=joined, small_dp=copy_of(small), small_all=copy_of(small)),
        scratch, 0)


def gelu_and_slope(x):
    rate = (2.0 / jnp.pi) ** 0.5
    square = x * x
    bent = jnp.tanh(rate * x * (1.0 + 0.044715 * square))
    half = 0.5 * (1.0 + bent)
    return x * half, half + 0.5 * x * (1.0 - bent * bent) * rate * (1.0 + 0.134145 * square)


def middle_kernel(chunks, order, land_at, reduce, r):
    place = Place()
    rows = r.tokens.shape[0]
    every = r.attended.shape[0]
    hidden = r.w_up.shape[1]
    step = iter(order)
    down = r.down if reduce else r.sum_down
    peers = place.group()
    if reduce:
        ar = AllReduce(chunks, (down,), (r.sum_down,), (r.land0,), land_at, r.send, r.recv)
        peers += [ar.to[TO_Y], ar.to[TO_PAIR], ar.to[TO_MID]]

    def advance():
        if reduce:
            ar.run(next(step))

    cots = Gather(place, r.cots, r.cots_send, r.cots_recv, ((0, 64), (64, rows - 64)))
    second = Gather(place, r.second, r.second_send, r.second_recv, cuts_of(rows))
    branch = Gather(place, r.branch, r.branch_send, r.branch_recv, cuts_of(rows))
    mine = place.t * rows

    def fill(at, carry):
        r.cots[at_row(mine + at.start, BLOCK)] = r.d_output[at]

    each_block(rows, fill)
    meet(peers)

    def to_out(first, store):
        att = r.attended[at_row(first, rows)]
        each_col(D, lambda j: store(j, jnp.dot(att, r.w_out[:, at_col(j)], preferred_element_type=jnp.float32)))

    one = scatter_of(r, "s", place, rows)
    one.start(to_out)
    cots.start(0)
    one.arrive()
    gain, shift, b_out = r.gain[...], r.shift[...], r.b_out[...]
    for i, (first, count) in enumerate(second.cuts):

        def forward(at, carry, first=first):
            at = at_row(at.start + first, BLOCK)
            mid = r.tokens[at].astype(jnp.float32) + one.total(at) + b_out
            r.mid[at] = mid
            r.second[at_row(mine + at.start, BLOCK)] = norm_rows(mid, gain, shift).astype(jnp.bfloat16)

        each_block(count, forward)
        second.start(i)
    cots.start(1)
    one.finish()

    def up(owner):
        at = at_row(owner * rows, rows)

        def tile(j):
            col = at_col(j)
            pre = jnp.dot(r.second[at], r.w_up[:, col], preferred_element_type=jnp.float32) + r.b_up[:, col]
            act, slope = gelu_and_slope(pre)
            r.act[at, col] = act.astype(jnp.bfloat16)
            r.slope[at, col] = slope

        each_col(hidden, tile)

    up(place.t)
    second.across()
    up(place.across)
    second.beyond()
    up(place.beyond)
    second.far()
    up(place.far)

    def to_down(first, store):
        act = r.act[at_row(first, rows)]
        each_col(D, lambda j: store(j, jnp.dot(act, r.w_down[:, at_col(j)], preferred_element_type=jnp.float32)))

    three = Scatter(place, rows, r.sout, r.snear, r.scross, r.slast, r.sown, r.again_send, r.again_recv)
    three.start(to_down)
    cots.across()
    cots.beyond()
    cots.far()
    for i in range(hidden // COLS):
        col = slice(i * COLS, (i + 1) * COLS)
        down[col] = inner_rows(r.act[:, col], r.cots[...]).astype(jnp.bfloat16)
        advance()
    r.small[6:7] = jnp.zeros((1, D), jnp.float32)
    for b in range(every // rows):
        at = slice(b * rows, (b + 1) * rows)

        def tile(j, at=at):
            col = at_col(j)
            d_act = times_transposed(r.cots[at], r.w_down[at_row(j * COLS, COLS)])
            d_pre = (d_act * r.slope[at, col]).astype(jnp.bfloat16)
            r.d_pre[at, col] = d_pre
            r.small[6:7, col] += jnp.sum(d_pre.astype(jnp.float32), axis=0, keepdims=True)

        each_col(hidden, tile)
        advance()

    def to_second(first, store):
        d_pre = r.d_pre[at_row(first, rows)]
        each_col(D, lambda j: store(j, times_transposed(d_pre, r.w_up[at_row(j * COLS, COLS)])))

    two = scatter_of(r, "t", place, rows)
    two.start(to_second)
    advance()
    for i in range(D // COLS):
        col = slice(i * COLS, (i + 1) * COLS)
        r.grad_up[col] = inner_rows(r.second[:, col], r.d_pre[...]).astype(jnp.bfloat16)
        advance()
    three.arrive()
    b_down = r.b_down[...]

    def finish(at, carry):
        r.output[at] = (r.mid[at] + three.total(at) + b_down).astype(jnp.bfloat16)

    each_block(rows, finish)
    two.arrive()
    zero = jnp.zeros((BLOCK, D), jnp.float32)
    sums = (zero,) * 4
    for i, (first, count) in enumerate(branch.cuts):

        def back(at, carry, first=first):
            at = at_row(at.start + first, BLOCK)
            cot = two.total(at)
            part, gained = norm_back(r.mid[at], cot, gain)
            d_output = r.d_output[at].astype(jnp.float32)
            d_mid = d_output + part
            r.d_mid[at] = d_mid
            low_part = d_mid.astype(jnp.bfloat16)
            r.branch[at_row(mine + at.start, BLOCK)] = low_part
            more = (low_part.astype(jnp.float32), d_output, gained, cot)
            return tuple(a + b for a, b in zip(carry, more))

        sums = each_block(count, back, sums)
        branch.start(i)
    advance()
    r.small[2:4] = jnp.zeros((2, D), jnp.float32)
    r.small[7:8] = jnp.zeros((1, D), jnp.float32)
    for row, total in zip((0, 1, 4, 5), sums):
        r.small[row : row + 1] = jnp.sum(total, axis=0, keepdims=True)

    def attn(owner):
        at = at_row(owner * rows, rows)
        r.d_att[at] = times_transposed(r.branch[at], r.w_out[...]).astype(jnp.bfloat16)

    attn(place.t)
    branch.across()
    attn(place.across)
    advance()
    branch.beyond()
    attn(place.beyond)
    branch.far()
    attn(place.far)
    advance()
    wide = r.attended.shape[1]
    for i in range(0, wide, COLS):
        col = slice(i, min(wide, i + COLS))
        r.grad_out[col] = inner_rows(r.attended[:, col], r.branch[...]).astype(jnp.bfloat16)
    advance()
    for part in (cots, second, branch, two, three):
        part.finish()
    if reduce:
        ar.finish()


def middle(attended, tokens, d_output, w_out, w_up, w_down, b_out, b_up, b_down, gain, shift, reduce):
    rows, every = tokens.shape[0], attended.shape[0]
    hidden = w_up.shape[1]
    groups = hidden // COLS
    chunks, timed = cut_rows([(0, i * COLS, COLS, D, i) for i in range(groups)], 128, KINDS)
    gaps = [1.6] * groups + [2.2] * (every // rows) + [6.0] + [1.6] * (D // COLS) + [14.0, 4.0, 14.0, 3.0]
    order, _ = plan_order(timed, gaps, False)
    scratch = scatter_scratch("s", rows)
    scratch.update(scatter_scratch("t", rows))
    scratch.update(
        again_send=dma(3), again_recv=dma(3), cots=low(every, D), second=low(every, D), branch=low(every, D),
        cots_send=dma(3, 2), cots_recv=dma(3, 2), second_send=dma(3, 2), second_recv=dma(3, 2),
        branch_send=dma(3, 2), branch_recv=dma(3, 2), mid=full(rows, D), act=low(every, hidden),
        slope=full(every, hidden), d_pre=low(every, hidden))
    land_at = None
    if reduce:
        more, land_at = reduce_scratch(chunks, [w_down.shape])
        scratch.update(more, down=low(*w_down.shape))
    row = lambda v: v.reshape(1, -1)
    return call(
        functools.partial(middle_kernel, chunks, order, land_at, reduce), "middle",
        dict(attended=attended, tokens=tokens, d_output=d_output, w_out=w_out, w_up=w_up, w_down=w_down,
             b_out=row(b_out), b_up=row(b_up), b_down=row(b_down), gain=row(gain), shift=row(shift)),
        {},
        dict(output=copy_of(tokens), d_mid=jax.ShapeDtypeStruct((rows, D), jnp.float32), d_att=copy_of(attended),
             sum_down=copy_of(w_down), grad_up=copy_of(w_up), grad_out=copy_of(w_out),
             small=jax.ShapeDtypeStruct((8, D), jnp.float32)),
        scratch, 1)


def front_kernel(r):
    place = Place()
    rows = r.tokens.shape[0]
    wide = r.w.shape[0]
    third = wide // 3
    tokens = Gather(place, r.whole, r.send, r.recv, cuts_of(rows))
    mine = place.t * rows

    def fill(at, carry):
        r.whole[at_row(mine + at.start, BLOCK)] = r.tokens[at]

    each_block(rows, fill)
    meet(place.group())
    tokens.start(0)
    tokens.start(1)
    for i, part in enumerate((r.w_query, r.w_key, r.w_value)):
        r.w[i * third : (i + 1) * third] = part[...]
    gain, shift = r.gain[...], r.shift[...]

    def project(owner):
        def norm(at, carry):
            at = at_row(owner * rows + at.start, BLOCK)
            r.normed[at] = norm_rows(r.whole[at].astype(jnp.float32), gain, shift).astype(jnp.bfloat16)

        each_block(rows, norm)
        at = at_row(owner * rows, rows)
        for i in range(0, wide, COLS):
            col = slice(i, min(wide, i + COLS))
            part = times_transposed(r.normed[at], r.w[col]) + r.bias[:, col]
            r.joined[at, col] = part.astype(jnp.bfloat16)

    project(place.t)
    tokens.across()
    project(place.across)
    tokens.beyond()
    project(place.beyond)
    tokens.far()
    project(place.far)
    tokens.finish()


def front(tokens, w_query, w_key, w_value, b_query, b_value, gain, shift):
    rows = tokens.shape[0]
    every = rows * lax.axis_size(TP)
    parts = [w.T for w in (w_query, w_key, w_value)]
    wide = 3 * parts[0].shape[0]
    bias = jnp.concatenate([b_query, jnp.zeros_like(b_query), b_value]).reshape(1, wide)
    bf16 = jnp.bfloat16
    return call(
        front_kernel, "front",
        dict(tokens=tokens, w_query=parts[0], w_key=parts[1], w_value=parts[2], bias=bias,
             gain=gain.reshape(1, D), shift=shift.reshape(1, D)),
        {},
        dict(normed=jax.ShapeDtypeStruct((every, D), bf16), joined=jax.ShapeDtypeStruct((every, wide), bf16),
             w=jax.ShapeDtypeStruct((wide, D), bf16)),
        dict(whole=low(every, D), send=dma(3, 2), recv=dma(3, 2)), 2)


def local(
    tokens, w_query, w_key, w_value, b_query, b_value, w_out, b_out, w_up, b_up, w_down, b_down,
    gain_attn, shift_attn, gain_ffn, shift_ffn, cell_lengths, d_output,
):
    cols = w_query.shape[1]
    reduce = lax.axis_size(DP) == 8
    f = front(tokens, w_query, w_key, w_value, b_query, b_value, gain_attn, shift_attn)
    attended, lse = attend(f.joined, cell_lengths)
    m = middle(attended, tokens, d_output, w_out, w_up, w_down, b_out, b_up, b_down, gain_ffn, shift_ffn, reduce)
    cots = attend_back(f.joined, m.d_att, lse, cell_lengths)
    e = tail(cots, f.normed, f.w, tokens, m.d_mid, gain_attn, m.grad_up, m.grad_out, m.small, reduce)
    sums = tuple(g.astype(jnp.float32) for g in (m.sum_down, e.sum_up, e.sum_out, e.sum_joined))
    small_dp, small_all = e.small_dp, e.small_all
    if not reduce:
        sums = lax.psum(sums, DP)
        small_dp = lax.psum(small_dp, DP)
        small_all = lax.psum(small_all, (DP, TP))
    grad_down, grad_up, grad_out, joined = sums
    last = small_dp[7]
    return (
        m.output, e.d_tokens, joined[:cols].T, joined[cols : 2 * cols].T, joined[2 * cols :].T,
        last[:cols], last[2 * cols : 3 * cols], grad_out, small_all[0], grad_up, small_dp[6], grad_down,
        small_all[1], small_all[2], small_all[3], small_all[4], small_all[5],
    )


def solution(mesh):
    in_specs = (
        P((DP, TP), None),
        P(None, TP),
        P(None, TP),
        P(None, TP),
        P(TP),
        P(TP),
        P(TP, None),
        P(),
        P(None, TP),
        P(TP),
        P(TP, None),
        P(),
        P(),
        P(),
        P(),
        P(),
        P(DP, None),
        P((DP, TP), None),
    )
    out_specs = (
        P((DP, TP), None),
        P((DP, TP), None),
        P(None, TP),
        P(None, TP),
        P(None, TP),
        P(TP),
        P(TP),
        P(TP, None),
        P(),
        P(None, TP),
        P(TP),
        P(TP, None),
        P(),
        P(),
        P(),
        P(),
        P(),
    )
    return jax.shard_map(local, mesh=mesh, in_specs=in_specs, out_specs=out_specs, check_vma=False)
```

```python
import functools
import heapq

import jax
import jax.numpy as jnp
from jax import lax
from jax.experimental import pallas as pl
from jax.experimental.pallas import tpu as pltpu
from jax.sharding import PartitionSpec as P

D = 1280
HEAD_DIM = 64

MESH_ID = pl.DeviceIdType.MESH
LINK_RATE = 42e3
HOP_US = 2.2
DP, TP = "dp", "tensor"

KIND_A, KIND_B, KIND_C = range(3)
SMALL = -1
OUTER, INNER = range(2)
OUT_Y, IN_Y, OUT_IN, IN_OUT, MID = range(5)
TO_Y, TO_PAIR, TO_MID = range(3)
START, R0, R1, R2, R3, R4, R5A, R5B, R6A, R6B, R6C, R6D, R7A, R7B = range(14)


def plan_order(chunks, gaps, small, pace=0.6, margin=1.0):
    free = dict.fromkeys((OUT_Y, IN_Y, OUT_IN, IN_OUT, MID), 0.0)
    order = [{OUTER: [], INNER: []} for _ in gaps]
    clock = {OUTER: 0.0, INNER: 0.0}
    heap, seen = [], set()
    count = [0]
    turn = 0.0

    def push(when, role, k, name):
        heapq.heappush(heap, (when, count[0], role, k, name))
        count[0] += 1

    def send(when, link, size):
        free[link] = max(when, free[link]) + size / LINK_RATE
        return free[link] + HOP_US

    for slot, (gap, spare) in enumerate(gaps):
        last = slot == len(gaps) - 1
        for role in clock:
            clock[role] += gap
        for k, (_, size, ready) in enumerate(chunks):
            if ready == slot:
                turn = max(turn, max(clock.values()))
                push(turn, OUTER, k, START)
                push(turn, INNER, k, START)
                turn += pace * size / LINK_RATE
        if small and last:
            for role in clock:
                for i in range(6):
                    push(max(clock.values()) + 2.5 * i, role, SMALL, i)
        later, now = [], max(clock.values()) + spare
        while heap:
            when, n, role, k, name = heapq.heappop(heap)
            if k == SMALL:
                clock[role] = max(when, clock[role])
                order[slot][role].append((k, name))
                continue
            kind, size, _ = chunks[k]
            if not last and when + (0.0 if name == START else margin) > now:
                later.append((when, n, role, k, name))
                continue
            when = max(when, clock[role])
            if (kind, role, name) == (KIND_A, INNER, R2) and (k, INNER, R1) not in seen:
                push(when + 0.2, role, k, name)
                continue
            when += 0.2 + (size / 800e3 if name in (R0, R1, R2, R3) else 0.0)
            clock[role] = when
            order[slot][role].append((k, name))
            seen.add((k, role, name))
            for link, part, to, event in SENDS.get((kind, role, name), ()):
                push(send(when, link, size * part), to, k, event)
        for item in later:
            heapq.heappush(heap, item)
        for role in clock:
            clock[role] = max(clock[role], now)
    return order, max(clock.values())


SENDS = {
    (KIND_A, OUTER, START): ((OUT_Y, 0.5, OUTER, R1),),
    (KIND_A, INNER, START): ((IN_Y, 0.5, INNER, R1),),
    (KIND_A, OUTER, R1): ((OUT_IN, 0.5, INNER, R2),),
    (KIND_A, INNER, R2): ((MID, 0.25, INNER, R3),),
    (KIND_A, INNER, R3): ((MID, 0.25, INNER, R4), (IN_OUT, 0.25, OUTER, R5A), (IN_Y, 0.25, INNER, R6A)),
    (KIND_A, INNER, R4): ((IN_OUT, 0.25, OUTER, R5B), (IN_Y, 0.25, INNER, R6B)),
    (KIND_A, OUTER, R5A): ((OUT_Y, 0.25, OUTER, R6A),),
    (KIND_A, OUTER, R5B): ((OUT_Y, 0.25, OUTER, R6B),),
    (KIND_B, OUTER, START): ((OUT_IN, 1.0, INNER, R1),),
    (KIND_B, INNER, R1): ((MID, 0.5, INNER, R2),),
    (KIND_B, INNER, R2): ((IN_Y, 0.25, INNER, R3),),
    (KIND_B, INNER, R3): ((IN_Y, 0.25, INNER, R4), (MID, 0.25, INNER, R5A), (IN_OUT, 0.25, OUTER, R6A)),
    (KIND_B, INNER, R4): ((MID, 0.25, INNER, R5B), (IN_OUT, 0.25, OUTER, R6B)),
    (KIND_B, INNER, R5A): ((IN_OUT, 0.25, OUTER, R6C),),
    (KIND_B, INNER, R5B): ((IN_OUT, 0.25, OUTER, R6D),),
    (KIND_C, OUTER, START): ((OUT_IN, 0.5, INNER, R1),),
    (KIND_C, INNER, R1): ((MID, 0.5, INNER, R2),),
    (KIND_C, INNER, R2): ((IN_OUT, 0.5, OUTER, R3),),
    (KIND_C, OUTER, R3): ((OUT_Y, 0.25, OUTER, R0),),
    (KIND_C, OUTER, R0): ((OUT_Y, 0.25, OUTER, R4), (OUT_IN, 0.25, INNER, R5A)),
    (KIND_C, OUTER, R4): ((OUT_IN, 0.25, INNER, R5B),),
    (KIND_C, INNER, R5A): ((MID, 0.25, INNER, R6A),),
    (KIND_C, INNER, R5B): ((MID, 0.25, INNER, R6B),),
    (KIND_C, INNER, R6A): ((IN_OUT, 0.25, OUTER, R7A),),
    (KIND_C, INNER, R6B): ((IN_OUT, 0.25, OUTER, R7B),),
}
EVENTS = (R0, R1, R2, R3, R4, R5A, R5B, R6A, R6B, R6C, R6D, R7A, R7B)


def slot_rows(kind, rows):
    if kind == KIND_A:
        return {R1: rows // 2, R2: rows // 2, R3: rows // 4}
    if kind == KIND_B:
        return {R1: rows, R2: rows // 2, R3: rows // 4}
    return {R1: rows // 2, R2: rows // 2, R3: rows // 2, R0: rows // 4}


class AllReduce:
    def __init__(self, chunks, grads, finals, lands, land_at, send_sem, recv_sem):
        self.chunks, self.grads, self.lands, self.land_at = chunks, grads, lands, land_at
        self.finals = finals
        self.send_sem, self.recv_sem = send_sem, recv_sem
        d, self.t = lax.axis_index(DP), lax.axis_index(TP)
        self.y, self.z = d % 2, d // 2
        self.side = self.z // 2
        self.inner = jnp.logical_or(self.z == 1, self.z == 2)
        self.to = {
            TO_Y: (self.z * 2 + 1 - self.y, self.t),
            TO_PAIR: ((self.z + 1 - 2 * (self.z % 2)) * 2 + self.y, self.t),
            TO_MID: ((3 - self.z) * 2 + self.y, self.t),
        }
        self.sent = {OUTER: [], INNER: []}

    def region(self, k, half=None, quarter=None, final=False):
        kind, g, first, rows = self.chunks[k]
        start = first
        if half is not None:
            start = start + half * (rows // 2)
            rows = rows // 2
        if quarter is not None:
            start = start + quarter * (rows // 2)
            rows = rows // 2
        if not isinstance(start, int):
            start = pl.multiple_of(start, 16)
        return (self.finals if final else self.grads)[g].at[pl.ds(start, rows)]

    def land(self, k, event):
        kind, g, first, rows = self.chunks[k]
        start, size = self.land_at[(k, event)]
        return self.lands[g].at[pl.ds(start, size)]

    def copy(self, k, event, src, dst, who):
        e = EVENTS.index(event)
        return pltpu.make_async_remote_copy(
            src_ref=src, dst_ref=dst, send_sem=self.send_sem.at[k, e], recv_sem=self.recv_sem.at[k, e],
            device_id=self.to[who], device_id_type=MESH_ID)

    def send(self, role, k, event, src, dst, who):
        c = self.copy(k, event, src, dst, who)
        c.start()
        self.sent[role].append((k, event, src.shape[0]))

    def arrive(self, k, event, dst):
        self.copy(k, event, dst, dst, TO_Y).wait_recv()

    def add(self, k, event, half=None, quarter=None, final=False):
        land = self.land(k, event)
        self.arrive(k, event, land)
        src = self.region(k, half, quarter)
        dst = self.region(k, half, quarter, final)
        rows = land.shape[0]
        step = 32 if rows % 32 == 0 else 16

        def body(i, carry):
            at = pl.ds(pl.multiple_of(i * step, 16), step)
            dst[at] = (src[at].astype(jnp.float32) + land[at].astype(jnp.float32)).astype(jnp.bfloat16)
            return carry

        lax.fori_loop(0, rows // step, body, 0)

    def event(self, role, k, name):
        kind = self.chunks[k][0]
        s, y = self.side, self.y
        R = functools.partial(self.region, k)
        F = functools.partial(self.region, k, final=True)
        send = functools.partial(self.send, role, k)
        key = (kind, role, name)
        if kind == KIND_A:
            if name == START:
                send(R1, R(1 - y), self.land(k, R1), TO_Y)
            elif name == R1:
                self.add(k, R1, y)
                if role == OUTER:
                    send(R2, R(y), self.land(k, R2), TO_PAIR)
            elif name == R2:
                self.add(k, R2, y)
                send(R3, R(y, 1 - s), self.land(k, R3), TO_MID)
            elif name == R3:
                self.add(k, R3, y, s, True)
                send(R4, F(y, s), F(y, s), TO_MID)
                send(R5A, F(y, s), F(y, s), TO_PAIR)
                send(R6A, F(y, s), F(y, s), TO_Y)
            elif name == R4:
                self.arrive(k, R4, F(y, 1 - s))
                send(R5B, F(y, 1 - s), F(y, 1 - s), TO_PAIR)
                send(R6B, F(y, 1 - s), F(y, 1 - s), TO_Y)
            elif name in (R5A, R5B):
                q = s if name == R5A else 1 - s
                self.arrive(k, name, F(y, q))
                send(R6A + name - R5A, F(y, q), F(y, q), TO_Y)
            elif name in (R6A, R6B):
                q = s if name == R6A else 1 - s
                self.arrive(k, name, F(1 - y, q))
        elif kind == KIND_B:
            if name == START:
                if role == OUTER:
                    send(R1, R(), self.land(k, R1), TO_PAIR)
            elif name == R1:
                self.add(k, R1)
                send(R2, R(1 - s), self.land(k, R2), TO_MID)
            elif name == R2:
                self.add(k, R2, s)
                send(R3, R(s, 1 - y), self.land(k, R3), TO_Y)
            elif name == R3:
                self.add(k, R3, s, y, True)
                for event, who in ((R4, TO_Y), (R5A, TO_MID), (R6A, TO_PAIR)):
                    send(event, F(s, y), F(s, y), who)
            elif name == R4:
                self.arrive(k, R4, F(s, 1 - y))
                for event, who in ((R5B, TO_MID), (R6B, TO_PAIR)):
                    send(event, F(s, 1 - y), F(s, 1 - y), who)
            elif name in (R5A, R5B):
                q = y if name == R5A else 1 - y
                self.arrive(k, name, F(1 - s, q))
                send(R6C if name == R5A else R6D, F(1 - s, q), F(1 - s, q), TO_PAIR)
            else:
                h = s if name in (R6A, R6B) else 1 - s
                q = y if name in (R6A, R6C) else 1 - y
                self.arrive(k, name, F(h, q))
        else:
            if name == START:
                if role == OUTER:
                    send(R1, R(1 - s), self.land(k, R1), TO_PAIR)
            elif name == R1:
                self.add(k, R1, 1 - s)
                send(R2, R(1 - s), self.land(k, R2), TO_MID)
            elif name == R2:
                self.add(k, R2, s)
                send(R3, R(s), self.land(k, R3), TO_PAIR)
            elif name == R3:
                self.add(k, R3, s)
                send(R0, R(s, 1 - y), self.land(k, R0), TO_Y)
            elif name == R0:
                self.add(k, R0, s, y, True)
                send(R4, F(s, y), F(s, y), TO_Y)
                send(R5A, F(s, y), F(s, y), TO_PAIR)
            elif name == R4:
                self.arrive(k, R4, F(s, 1 - y))
                send(R5B, F(s, 1 - y), F(s, 1 - y), TO_PAIR)
            elif name in (R5A, R5B):
                q = y if name == R5A else 1 - y
                self.arrive(k, name, F(s, q))
                send(R6A + name - R5A, F(s, q), F(s, q), TO_MID)
            elif name in (R6A, R6B):
                q = y if name == R6A else 1 - y
                self.arrive(k, name, F(1 - s, q))
                send(R7A + name - R6A, F(1 - s, q), F(1 - s, q), TO_PAIR)
            else:
                q = y if name == R7A else 1 - y
                self.arrive(k, name, F(1 - s, q))

    def run(self, order):
        for role, here in ((INNER, self.inner), (OUTER, jnp.logical_not(self.inner))):
            if order[role]:

                @pl.when(here)
                def _(role=role):
                    for k, name in order[role]:
                        if k == SMALL:
                            self.small.step(name)
                        else:
                            self.event(role, k, name)

    def finish(self):
        for role, here in ((INNER, self.inner), (OUTER, jnp.logical_not(self.inner))):
            @pl.when(here)
            def _(role=role):
                for k, event, rows in self.sent[role]:
                    _, g, first, _ = self.chunks[k]
                    src = self.grads[g].at[pl.ds(first, rows)]
                    self.copy(k, event, src, src, TO_Y).wait_send()


def lay_out(chunks, widths):
    at, used = {}, [0] * len(widths)
    for k, (kind, g, first, rows) in enumerate(chunks):
        for event, size in slot_rows(kind, rows).items():
            at[(k, event)] = (used[g], size)
            used[g] += size
    return at, used


class SmallSums:
    def __init__(self, source, totals, lands, send_sem, recv_sem):
        self.source, self.totals, self.lands = source, totals, lands
        self.send_sem, self.recv_sem = send_sem, recv_sem
        d, t = lax.axis_index(DP), lax.axis_index(TP)
        y, z = d % 2, d // 2
        self.to = (
            (z * 2 + 1 - y, t),
            ((z + 1 - 2 * (z % 2)) * 2 + y, t),
            (((z + 2) % 4) * 2 + y, t),
            (d, t + 1 - 2 * (t % 2)),
            (d, (t + 2) % 4),
        )

    def copy(self, i):
        src = self.source if i == 0 else self.totals.at[i - 1]
        return pltpu.make_async_remote_copy(
            src_ref=src, dst_ref=self.lands.at[i], send_sem=self.send_sem.at[i],
            recv_sem=self.recv_sem.at[i], device_id=self.to[i], device_id_type=MESH_ID)

    def step(self, i):
        if i > 0:
            self.copy(i - 1).wait_recv()
            have = self.source[...] if i == 1 else self.totals[i - 2]
            self.totals[i - 1] = have + self.lands[i - 1]
        if i < 5:
            self.copy(i).start()

    def finish(self):
        for i in range(5):
            self.copy(i).wait_send()


norm_eps = 1e-05
MASKED = -1e30
MOST_CELL = 384


def norm_rows(values, gain, shift):
    center = values - jnp.mean(values, axis=-1, keepdims=True)
    spread = jnp.mean(center * center, axis=-1, keepdims=True)
    return center * lax.rsqrt(spread + norm_eps) * gain + shift


def inner_rows(left, right):
    return lax.dot_general(
        left, right, (((0,), (0,)), ((), ())), preferred_element_type=jnp.float32
    )


def times_transposed(left, right):
    return lax.dot_general(
        left, right, (((1,), (1,)), ((), ())), preferred_element_type=jnp.float32
    )


def each_cell(lengths, row, seq_len, body):
    widths = sorted({min(w, seq_len) for w in (128, 256, MOST_CELL + 16)})

    def step(i, start):
        length = lengths[row, i]
        lower = 0
        for width in widths:
            first = pl.multiple_of(jnp.minimum(start // 16 * 16, seq_len - width), 16)

            @pl.when(jnp.logical_and(length > lower, length <= width - 16))
            def _(width=width, first=first):
                down = first + lax.broadcasted_iota(jnp.int32, (width, 1), 0)
                along = first + lax.broadcasted_iota(jnp.int32, (1, width), 1)
                inside = [jnp.logical_and(p >= start, p < start + length) for p in (down, along)]
                body(first, width, inside[0], inside[1])

            lower = width - 16
        return start + length

    lax.fori_loop(0, lengths.shape[1], step, jnp.int32(0))


def attend_kernel(heads, lengths, joined, out, lse):
    seq_len, wide = out.shape

    def body(first, width, down, along):
        rows = pl.ds(first, width)
        seen = jnp.logical_and(down, along)
        for h in range(heads):
            at = h * HEAD_DIM
            query = joined[rows, at : at + HEAD_DIM] * jnp.bfloat16(HEAD_DIM**-0.5)
            key = joined[rows, wide + at : wide + at + HEAD_DIM]
            value = joined[rows, 2 * wide + at : 2 * wide + at + HEAD_DIM]
            scores = jnp.where(seen, times_transposed(query, key), MASKED)
            top = jnp.max(scores, axis=1, keepdims=True)
            expo = jnp.exp(scores - top)
            total = jnp.sum(expo, axis=1, keepdims=True)
            probs = (expo * (1.0 / total)).astype(jnp.bfloat16)
            part = jnp.dot(probs, value, preferred_element_type=jnp.float32).astype(jnp.bfloat16)
            cols = slice(at, at + HEAD_DIM)
            out[rows, cols] = jnp.where(down, part, out[rows, cols])
            lse[rows, h : h + 1] = jnp.where(down, top + jnp.log(total), lse[rows, h : h + 1])

    each_cell(lengths, pl.program_id(0), seq_len, body)


def attend_back_kernel(heads, lengths, joined, grad, lse, out):
    seq_len, wide = grad.shape
    scale = HEAD_DIM**-0.5

    def body(first, width, down, along):
        rows = pl.ds(first, width)
        seen = jnp.logical_and(down, along)
        for h in range(heads):
            at = h * HEAD_DIM
            query = joined[rows, at : at + HEAD_DIM] * jnp.bfloat16(scale)
            key = joined[rows, wide + at : wide + at + HEAD_DIM]
            value = joined[rows, 2 * wide + at : 2 * wide + at + HEAD_DIM]
            cot = grad[rows, at : at + HEAD_DIM]
            scores = jnp.where(seen, times_transposed(query, key), MASKED)
            probs = jnp.exp(scores - lse[rows, h : h + 1])
            d_value = inner_rows(probs.astype(jnp.bfloat16), cot)
            d_probs = times_transposed(cot, value)
            offset = jnp.sum(probs * d_probs, axis=1, keepdims=True)
            d_scores = (probs * (d_probs - offset)).astype(jnp.bfloat16)
            d_query = jnp.dot(d_scores, key, preferred_element_type=jnp.float32) * scale
            d_key = inner_rows(d_scores, query)
            for i, part in enumerate((d_query, d_key, d_value)):
                cols = slice(i * wide + at, i * wide + at + HEAD_DIM)
                out[rows, cols] = jnp.where(down, part.astype(jnp.bfloat16), out[rows, cols])

    each_cell(lengths, pl.program_id(0), seq_len, body)


def attend(joined, lengths):
    n, wide = lengths.shape[0], joined.shape[1] // 3
    seq_len = joined.shape[0] // n
    heads = wide // HEAD_DIM
    return pl.pallas_call(
        functools.partial(attend_kernel, heads),
        grid=(n,),
        out_shape=[
            jax.ShapeDtypeStruct((joined.shape[0], wide), jnp.bfloat16),
            jax.ShapeDtypeStruct((joined.shape[0], 128), jnp.float32),
        ],
        in_specs=[
            pl.BlockSpec(memory_space=pltpu.SMEM),
            pl.BlockSpec((seq_len, 3 * wide), lambda i: (i, 0)),
        ],
        out_specs=[
            pl.BlockSpec((seq_len, wide), lambda i: (i, 0)),
            pl.BlockSpec((seq_len, 128), lambda i: (i, 0)),
        ],
        compiler_params=pltpu.CompilerParams(vmem_limit_bytes=40 << 20),
        name="attend",
    )(lengths, joined)


def attend_back(joined, grad, lse, lengths):
    n, wide = lengths.shape[0], grad.shape[1]
    seq_len = joined.shape[0] // n
    heads = wide // HEAD_DIM
    return pl.pallas_call(
        functools.partial(attend_back_kernel, heads),
        grid=(n,),
        out_shape=jax.ShapeDtypeStruct(joined.shape, jnp.bfloat16),
        in_specs=[
            pl.BlockSpec(memory_space=pltpu.SMEM),
            pl.BlockSpec((seq_len, 3 * wide), lambda i: (i, 0)),
            pl.BlockSpec((seq_len, wide), lambda i: (i, 0)),
            pl.BlockSpec((seq_len, 128), lambda i: (i, 0)),
        ],
        out_specs=pl.BlockSpec((seq_len, 3 * wide), lambda i: (i, 0)),
        compiler_params=pltpu.CompilerParams(vmem_limit_bytes=40 << 20),
        name="attend_back",
    )(lengths, joined, grad, lse)


COLS = 256
B_OUT, B_DOWN, B_UP, GAIN_ATTN, SHIFT_ATTN, GAIN_FFN, SHIFT_FFN, B_QKV = range(8)


class Refs:
    def __init__(self, names, refs):
        self.__dict__.update(zip(names, refs))


def call(body, name, ins, loose, outs, loose_outs, scratch, collective_id):
    names = list(ins) + list(loose) + list(outs) + list(loose_outs) + list(scratch)
    vmem, stay = pl.BlockSpec(memory_space=pltpu.VMEM), pl.BlockSpec(memory_space=pl.ANY)
    out = pl.pallas_call(
        lambda *refs: body(Refs(names, refs)),
        out_shape=list(outs.values()) + list(loose_outs.values()),
        in_specs=[vmem] * len(ins) + [stay] * len(loose),
        out_specs=[vmem] * len(outs) + [stay] * len(loose_outs),
        scratch_shapes=list(scratch.values()),
        compiler_params=pltpu.CompilerParams(
            collective_id=collective_id, has_side_effects=True, vmem_limit_bytes=64000 << 10
        ),
        name=name,
    )(*ins.values(), *loose.values())
    return Refs(list(outs) + list(loose_outs), out)


def low(*shape):
    return pltpu.VMEM(shape, jnp.bfloat16)


def full(*shape):
    return pltpu.VMEM(shape, jnp.float32)


def dma(*shape):
    return pltpu.SemaphoreType.DMA(shape)


def at_row(start, rows):
    return pl.ds(pl.multiple_of(start, 16), rows)


def at_col(i, cols=COLS):
    return pl.ds(pl.multiple_of(i * cols, cols), cols)


def remote(src, dst, send, recv, to):
    return pltpu.make_async_remote_copy(
        src_ref=src, dst_ref=dst, send_sem=send, recv_sem=recv, device_id=to, device_id_type=MESH_ID)


class Place:
    def __init__(self):
        self.d, self.t = lax.axis_index(DP), lax.axis_index(TP)
        self.across = self.t + 1 - 2 * (self.t % 2)
        self.beyond = (self.t + 2) % 4
        self.far = 3 - self.t

    def group(self):
        return [(self.d, self.across), (self.d, self.beyond)]


def meet(peers):
    barrier = pltpu.get_barrier_semaphore()
    for peer in peers:
        pl.semaphore_signal(barrier, inc=1, device_id=peer, device_id_type=MESH_ID)
    pl.semaphore_wait(barrier, len(peers))


class Gather:
    def __init__(self, place, whole, send, recv, cuts):
        self.p, self.whole, self.send, self.recv, self.cuts = place, whole, send, recv, cuts
        self.rows = sum(rows for _, rows in cuts)

    def piece(self, owner, i):
        first, rows = self.cuts[i]
        return self.whole.at[at_row(owner * self.rows + first, rows)]

    def copy(self, kind, i, owner):
        ref = self.piece(owner, i)
        to = self.p.beyond if kind == 1 else self.p.across
        return remote(ref, ref, self.send.at[kind, i], self.recv.at[kind, i], (self.p.d, to))

    def start(self, i):
        self.copy(1, i, self.p.t).start()
        self.copy(0, i, self.p.t).start()

    def across(self):
        for i in range(len(self.cuts)):
            self.copy(0, i, self.p.across).wait_recv()

    def beyond(self, i):
        self.copy(1, i, self.p.beyond).wait_recv()
        self.copy(2, i, self.p.beyond).start()

    def far(self, i):
        self.copy(2, i, self.p.far).wait_recv()

    def rest(self):
        for i in range(len(self.cuts)):
            self.beyond(i)
        for i in range(len(self.cuts)):
            self.far(i)

    def finish(self):
        for i in range(len(self.cuts)):
            self.copy(0, i, self.p.t).wait_send()
            self.copy(1, i, self.p.t).wait_send()
            self.copy(2, i, self.p.beyond).wait_send()


class Scatter:
    def __init__(self, place, rows, out, near, cross, last, own, send, recv):
        self.p, self.rows = place, rows
        self.out, self.near, self.cross, self.last, self.own = out, near, cross, last, own
        self.send, self.recv = send, recv

    def copies(self):
        d, p = self.p.d, self.p
        return (
            remote(self.out.at[0], self.near.at[0], self.send.at[0], self.recv.at[0], (d, p.across)),
            remote(self.out.at[1], self.near.at[1], self.send.at[1], self.recv.at[1], (d, p.across)),
            remote(self.cross, self.last, self.send.at[2], self.recv.at[2], (d, p.beyond)),
        )

    def start(self, compute, between=lambda: None):
        copies = self.copies()

        def keep(slot):
            def store(j, value):
                self.out[slot, :, at_col(j)] = value.astype(jnp.bfloat16)

            return store

        def add(j, value):
            total = value + self.near[0, :, at_col(j)].astype(jnp.float32)
            self.cross[:, at_col(j)] = total.astype(jnp.bfloat16)

        def hold(j, value):
            self.own[:, at_col(j)] = value

        compute(self.p.far * self.rows, keep(0))
        copies[0].start()
        between()
        compute(self.p.across * self.rows, keep(1))
        copies[1].start()
        between()
        copies[0].wait_recv()
        compute(self.p.beyond * self.rows, add)
        copies[2].start()
        between()
        compute(self.p.t * self.rows, hold)

    def arrive(self):
        copies = self.copies()
        copies[1].wait_recv()
        copies[2].wait_recv()

    def total(self, rows):
        return self.own[rows] + (self.near[1, rows].astype(jnp.float32) + self.last[rows].astype(jnp.float32))

    def finish(self):
        for c in self.copies():
            c.wait_send()


def scatter_scratch(prefix, rows):
    return {
        prefix + "out": low(2, rows, D), prefix + "near": low(2, rows, D), prefix + "cross": low(rows, D),
        prefix + "last": low(rows, D), prefix + "own": full(rows, D),
        prefix + "send": dma(3), prefix + "recv": dma(3),
    }


def scatter_of(refs, prefix, place, rows):
    names = ("out", "near", "cross", "last", "own", "send", "recv")
    return Scatter(place, rows, *[getattr(refs, prefix + n) for n in names])


def cuts_of(rows):
    half = (rows // 2 + 15) // 16 * 16
    return ((0, half), (half, rows - half))


def each_block(rows, body, init=0):
    for first, count in cuts_of(rows):
        out = body(first, count, init)
        init = init if out is None else out
    return init


def each_col(width, body):
    def step(j, carry):
        body(j)
        return carry

    lax.fori_loop(0, width // COLS, step, 0)


def norm_back(x, cot, gain):
    center = x - jnp.mean(x, axis=-1, keepdims=True)
    rate = lax.rsqrt(jnp.mean(center * center, axis=-1, keepdims=True) + norm_eps)
    hat = center * rate
    inner = cot * gain
    part = inner - jnp.mean(inner, axis=-1, keepdims=True) - hat * jnp.mean(inner * hat, axis=-1, keepdims=True)
    return part * rate, cot * hat


def reduce_scratch(chunks, shapes):
    at, used = lay_out(chunks, shapes)
    out = {}
    for i, (u, s) in enumerate(zip(used, shapes)):
        out["land%d" % i] = low(max(u, 16), s[1])
    out["send"] = dma(max(len(chunks), 1), len(EVENTS))
    out["recv"] = dma(max(len(chunks), 1), len(EVENTS))
    return out, at


def cut_rows(pieces, size, kinds):
    chunks, timed = [], []
    for g, first, rows, columns, slot in pieces:
        end = first + rows
        while first < end:
            here = size if end - first >= 2 * size or end - first == size else end - first
            kind = kinds[len(chunks) % len(kinds)]
            chunks.append((kind, g, first, here))
            timed.append((kind, here * columns * 2, slot))
            first += here
    return chunks, timed


def tail_kernel(chunks, order, land_at, reduce, r):
    place = Place()
    rows = r.tokens.shape[0]
    wide = r.w.shape[0]
    step = iter(order)
    if reduce:
        up, out, joined = r.up, r.out, r.joined
        ar = AllReduce(
            chunks, (up, out, joined), (r.sum_up, r.sum_out, r.sum_joined), (r.land0, r.land1, r.land2),
            land_at, r.send, r.recv)
        ar.small = SmallSums(r.small, r.totals, r.small_lands, r.small_send, r.small_recv)
        peers = [ar.to[TO_Y], ar.to[TO_PAIR], ar.to[TO_MID], ar.small.to[2]] + place.group()
    else:
        up, out, joined = r.sum_up, r.sum_out, r.sum_joined
        peers = place.group()
    fills = [pltpu.make_async_copy(r.up_in, up, r.fill.at[0]), pltpu.make_async_copy(r.out_in, out, r.fill.at[1])]
    for f in fills:
        f.start()
    meet(peers)
    for f in fills:
        f.wait()

    def advance():
        if reduce:
            ar.run(next(step))

    scatter = scatter_of(r, "s", place, rows)
    advance()

    def to_first(first, store):
        cots = r.cots[at_row(first, rows)]
        each_col(D, lambda j: store(j, jnp.dot(cots, r.w[:, at_col(j)], preferred_element_type=jnp.float32)))

    scatter.start(to_first, advance)
    advance()
    for i in range(0, wide, COLS):
        n = min(COLS, wide - i)
        joined[i : i + n] = inner_rows(r.cots[:, i : i + n], r.normed[...]).astype(jnp.bfloat16)
        advance()
    r.small[...] = r.small_in[...]
    r.small[7:8, :wide] = lax.fori_loop(
        0, r.cots.shape[0] // rows,
        lambda i, c: c + jnp.sum(r.cots[at_row(i * rows, rows)].astype(jnp.float32), axis=0, keepdims=True),
        jnp.zeros((1, wide), jnp.float32))
    advance()
    scatter.arrive()
    gain = r.vectors[GAIN_ATTN]

    def back(first, count, carry):
        at = at_row(first, count)
        cot = scatter.total(at)
        part, gained = norm_back(r.tokens[at].astype(jnp.float32), cot, gain)
        r.d_tokens[at] = r.d_mid[at] + part
        return carry + jnp.stack([jnp.sum(gained, axis=0), jnp.sum(cot, axis=0)])

    r.small[2:4] = each_block(rows, back, jnp.zeros((2, D), jnp.float32))
    scatter.finish()
    advance()
    if reduce:
        ar.finish()
        ar.small.finish()
        r.small_dp[...] = r.totals[2]
        r.small_all[...] = r.totals[4]
    else:
        r.small_dp[...] = r.small[...]
        r.small_all[...] = r.small[...]


def copy_of(x):
    return jax.ShapeDtypeStruct(x.shape, x.dtype)


TAIL_KINDS = (1, 0, 0, 0, 2, 0, 2, 0, 2, 2, 0, 0, 0, 0, 0, 0, 0, 1, 0)
MID_KINDS = (2, 0, 0, 2, 2, 0, 0, 0, 2, 0)
TAIL_SIZE, TAIL_PACE, MID_SIZE, MID_PACE = 128, 0.26, 128, 0.16


def tail(cots, normed, w, tokens, d_mid, vectors, up, out, small, reduce):
    rows, wide = tokens.shape[0], w.shape[0]
    joined = jax.ShapeDtypeStruct((wide, D), jnp.bfloat16)
    shapes = [up.shape, out.shape, joined.shape]
    pieces = [(0, 0, up.shape[0], D, 0), (1, 0, out.shape[0], D, 0)]
    pieces += [(2, i, min(COLS, wide - i), D, 5 + i // COLS) for i in range(0, wide, COLS)]
    chunks, timed = cut_rows(pieces, TAIL_SIZE, TAIL_KINDS)
    gaps = [(0.0, 0.0)] + [(2.2, 0.0)] * 4 + [(1.6, 0.0)] * len(range(0, wide, COLS)) + [(1.5, 4.0), (3.0, 0.0)]
    order, _ = plan_order(timed, gaps, True, TAIL_PACE)
    scratch = scatter_scratch("s", rows)
    scratch.update(small=full(8, D), fill=dma(2))
    land_at = None
    if reduce:
        more, land_at = reduce_scratch(chunks, shapes)
        scratch.update(more)
        scratch.update(
            up=low(*up.shape), out=low(*out.shape), joined=low(wide, D), totals=full(5, 8, D),
            small_lands=full(5, 8, D), small_send=dma(5), small_recv=dma(5))
    return call(
        functools.partial(tail_kernel, chunks, order, land_at, reduce), "tail",
        dict(cots=cots, normed=normed, w=w, tokens=tokens, d_mid=d_mid, vectors=vectors, small_in=small),
        dict(up_in=up, out_in=out),
        dict(d_tokens=jax.ShapeDtypeStruct((rows, D), jnp.float32), sum_up=copy_of(up), sum_out=copy_of(out),
             sum_joined=joined, small_dp=copy_of(small), small_all=copy_of(small)),
        {}, scratch, 0)


def gelu_and_slope(x):
    rate = (2.0 / jnp.pi) ** 0.5
    square = x * x
    bent = jnp.tanh(rate * x * (1.0 + 0.044715 * square))
    half = 0.5 * (1.0 + bent)
    return x * half, half + 0.5 * x * (1.0 - bent * bent) * rate * (1.0 + 0.134145 * square)


def middle_kernel(chunks, order, land_at, reduce, r):
    place = Place()
    rows = r.tokens.shape[0]
    every = r.attended.shape[0]
    hidden = r.act.shape[1]
    step = iter(order)
    down = r.down if reduce else r.sum_down
    peers = place.group()
    if reduce:
        ar = AllReduce(chunks, (down,), (r.sum_down,), (r.land0,), land_at, r.send, r.recv)
        peers += [ar.to[TO_Y], ar.to[TO_PAIR], ar.to[TO_MID]]

    def advance():
        if reduce:
            ar.run(next(step))

    cots = Gather(place, r.cots, r.cots_send, r.cots_recv, ((0, 64), (64, rows - 64)))
    second = Gather(place, r.second, r.second_send, r.second_recv, cuts_of(rows))
    branch = Gather(place, r.branch, r.branch_send, r.branch_recv, cuts_of(rows))
    mine = place.t * rows

    fills = [
        pltpu.make_async_copy(r.d_output, r.cots.at[at_row(mine, rows)], r.fill.at[0]),
        pltpu.make_async_copy(r.w_up_in, r.w_up, r.fill.at[1]),
        pltpu.make_async_copy(r.w_down_in, r.w_down, r.fill.at[2]),
    ]
    drains = [
        pltpu.make_async_copy(r.grad_up, r.grad_up_out, r.fill.at[3]),
        pltpu.make_async_copy(r.output, r.output_out, r.fill.at[4]),
        pltpu.make_async_copy(r.mid, r.d_mid_out, r.fill.at[5]),
    ]
    for f in fills:
        f.start()
    meet(peers)

    def to_out(first, store):
        att = r.attended[at_row(first, rows)]
        each_col(D, lambda j: store(j, jnp.dot(att, r.w_out[:, at_col(j)], preferred_element_type=jnp.float32)))

    one = scatter_of(r, "s", place, rows)
    one.start(to_out)
    fills[0].wait()
    cots.start(0)
    one.arrive()
    gain, shift = r.vectors[GAIN_FFN], r.vectors[SHIFT_FFN]
    for i, (first, count) in enumerate(second.cuts):
        at = at_row(first, count)
        mid = r.tokens[at].astype(jnp.float32) + one.total(at) + r.vectors[B_OUT]
        r.mid[at] = mid
        r.second[at_row(mine + first, count)] = norm_rows(mid, gain, shift).astype(jnp.bfloat16)
        second.start(i)
    cots.start(1)
    one.finish()

    def up(first, count):
        at = at_row(first, count)

        def tile(j):
            col = at_col(j)
            pre = jnp.dot(r.second[at], r.w_up[:, col], preferred_element_type=jnp.float32) + r.vectors[B_UP, col]
            act, slope = gelu_and_slope(pre)
            r.act[at, col] = act.astype(jnp.bfloat16)
            r.slope[at, col] = slope

        each_col(hidden, tile)

    pair = place.t // 2 * 2 * rows
    fills[1].wait()
    fills[2].wait()
    second.across()
    up(pair, 2 * rows)
    second.rest()
    up(2 * rows - pair, 2 * rows)

    def to_down(first, store):
        act = r.act[at_row(first, rows)]
        each_col(D, lambda j: store(j, jnp.dot(act, r.w_down[:, at_col(j)], preferred_element_type=jnp.float32)))

    three = Scatter(place, rows, r.sout, r.snear, r.scross, r.slast, r.sown, r.again_send, r.again_recv)
    three.start(to_down)
    cots.across()
    cots.rest()
    for i in range(hidden // COLS):
        col = slice(i * COLS, (i + 1) * COLS)
        down[col] = inner_rows(r.act[:, col], r.cots[...]).astype(jnp.bfloat16)
        advance()
    for j in range(hidden // COLS):
        col = slice(j * COLS, (j + 1) * COLS)
        d_pre = (times_transposed(r.cots[...], r.w_down[col]) * r.slope[:, col]).astype(jnp.bfloat16)
        r.d_pre[:, col] = d_pre
        r.small[6:7, col] = jnp.sum(d_pre.astype(jnp.float32), axis=0, keepdims=True)
        advance()

    def to_second(first, store):
        d_pre = r.d_pre[at_row(first, rows)]
        each_col(D, lambda j: store(j, times_transposed(d_pre, r.w_up[at_row(j * COLS, COLS)])))

    two = scatter_of(r, "t", place, rows)
    two.start(to_second, advance)
    advance()
    for i in range(D // COLS):
        col = slice(i * COLS, (i + 1) * COLS)
        r.grad_up[col] = inner_rows(r.second[:, col], r.d_pre[...]).astype(jnp.bfloat16)
        advance()
    drains[0].start()
    three.arrive()

    def finish(first, count, carry):
        at = at_row(first, count)
        r.output[at] = (r.mid[at] + three.total(at) + r.vectors[B_DOWN]).astype(jnp.bfloat16)

    each_block(rows, finish)
    drains[1].start()
    advance()
    two.arrive()
    sums = jnp.zeros((4, D), jnp.float32)
    for i, (first, count) in enumerate(branch.cuts):
        at = at_row(first, count)
        cot = two.total(at)
        part, gained = norm_back(r.mid[at], cot, gain)
        d_output = r.cots[at_row(mine + first, count)].astype(jnp.float32)
        d_mid = d_output + part
        r.mid[at] = d_mid
        low_part = d_mid.astype(jnp.bfloat16)
        r.branch[at_row(mine + first, count)] = low_part
        branch.start(i)
        parts = (low_part.astype(jnp.float32), d_output, gained, cot)
        sums = sums + jnp.stack([jnp.sum(p, axis=0) for p in parts])
    drains[2].start()
    r.small[0:2] = sums[0:2]
    r.small[2:4] = jnp.zeros((2, D), jnp.float32)
    r.small[4:6] = sums[2:4]
    r.small[7:8] = jnp.zeros((1, D), jnp.float32)

    def attn(first, count):
        at = at_row(first, count)
        r.d_att[at] = times_transposed(r.branch[at], r.w_out[...]).astype(jnp.bfloat16)

    advance()
    branch.across()
    attn(pair, 2 * rows)
    advance()
    branch.rest()
    attn(2 * rows - pair, 2 * rows)
    wide = r.attended.shape[1]
    for i in range(0, wide, COLS):
        col = slice(i, min(wide, i + COLS))
        r.grad_out[col] = inner_rows(r.attended[:, col], r.branch[...]).astype(jnp.bfloat16)
    advance()
    for part in (cots, second, branch, two, three):
        part.finish()
    for part in drains:
        part.wait()
    if reduce:
        ar.finish()


def middle(attended, tokens, d_output, w_out, w_up, w_down, vectors, reduce):
    rows, every = tokens.shape[0], attended.shape[0]
    hidden = w_up.shape[1]
    groups = hidden // COLS
    chunks, timed = cut_rows([(0, i * COLS, COLS, D, i) for i in range(groups)], MID_SIZE, MID_KINDS)
    gaps = [(1.5, 0.0)] * groups + [(1.8, 0.0)] * groups + [(2.2, 0.0)] * 4 + [(1.5, 0.0)] * (D // COLS)
    gaps += [(1.5, 4.0), (2.5, 2.0), (2.0, 12.0), (5.0, 0.0)]
    order, _ = plan_order(timed, gaps, False, MID_PACE)
    scratch = scatter_scratch("s", rows)
    scratch.update(scatter_scratch("t", rows))
    scratch.update(
        again_send=dma(3), again_recv=dma(3), cots=low(every, D), second=low(every, D), branch=low(every, D),
        cots_send=dma(3, 2), cots_recv=dma(3, 2), second_send=dma(3, 2), second_recv=dma(3, 2),
        branch_send=dma(3, 2), branch_recv=dma(3, 2), mid=full(rows, D), act=low(every, hidden),
        slope=full(every, hidden), d_pre=low(every, hidden), w_up=low(*w_up.shape), w_down=low(*w_down.shape),
        output=low(rows, D), grad_up=low(*w_up.shape), fill=dma(6))
    land_at = None
    if reduce:
        more, land_at = reduce_scratch(chunks, [w_down.shape])
        scratch.update(more, down=low(*w_down.shape))
    return call(
        functools.partial(middle_kernel, chunks, order, land_at, reduce), "middle",
        dict(attended=attended, tokens=tokens, w_out=w_out, vectors=vectors),
        dict(d_output=d_output, w_up_in=w_up, w_down_in=w_down),
        dict(d_att=copy_of(attended), sum_down=copy_of(w_down), grad_out=copy_of(w_out),
             small=jax.ShapeDtypeStruct((8, D), jnp.float32)),
        dict(output_out=copy_of(tokens), d_mid_out=jax.ShapeDtypeStruct((rows, D), jnp.float32), grad_up_out=copy_of(w_up)),
        scratch, 1)


def front_kernel(r):
    place = Place()
    rows = r.tokens.shape[0]
    wide = r.w.shape[0]
    third = wide // 3
    tokens = Gather(place, r.whole, r.send, r.recv, cuts_of(rows))
    mine = place.t * rows

    r.whole[at_row(mine, rows)] = r.tokens[...]
    meet(place.group())
    tokens.start(0)
    tokens.start(1)
    for i, part in enumerate((r.w_query, r.w_key, r.w_value)):
        r.w[i * third : (i + 1) * third] = part[...]
    gain, shift = r.vectors[GAIN_ATTN], r.vectors[SHIFT_ATTN]

    def project(owner, first, count):
        at = at_row(owner * rows + first, count)
        r.normed[at] = norm_rows(r.whole[at].astype(jnp.float32), gain, shift).astype(jnp.bfloat16)
        for i in range(0, wide, COLS):
            col = slice(i, min(wide, i + COLS))
            part = times_transposed(r.normed[at], r.w[col]) + r.vectors[B_QKV, col]
            r.joined[at, col] = part.astype(jnp.bfloat16)

    project(place.t, 0, rows)
    tokens.across()
    project(place.across, 0, rows)
    for i, cut in enumerate(tokens.cuts):
        tokens.beyond(i)
        project(place.beyond, *cut)
        tokens.far(i)
        project(place.far, *cut)
    tokens.finish()


def front(tokens, w_query, w_key, w_value, vectors):
    rows = tokens.shape[0]
    every = rows * lax.axis_size(TP)
    parts = [w.T for w in (w_query, w_key, w_value)]
    wide = 3 * parts[0].shape[0]
    bf16 = jnp.bfloat16
    return call(
        front_kernel, "front",
        dict(tokens=tokens, w_query=parts[0], w_key=parts[1], w_value=parts[2], vectors=vectors),
        {},
        dict(normed=jax.ShapeDtypeStruct((every, D), bf16), joined=jax.ShapeDtypeStruct((every, wide), bf16),
             w=jax.ShapeDtypeStruct((wide, D), bf16)),
        {}, dict(whole=low(every, D), send=dma(3, 2), recv=dma(3, 2)), 2)


def local(
    tokens, w_query, w_key, w_value, b_query, b_value, w_out, b_out, w_up, b_up, w_down, b_down,
    gain_attn, shift_attn, gain_ffn, shift_ffn, cell_lengths, d_output,
):
    cols = w_query.shape[1]
    reduce = lax.axis_size(DP) == 8
    qkv = jnp.pad(jnp.concatenate([b_query, jnp.zeros_like(b_query), b_value]), (0, D - 3 * cols))
    vectors = jnp.stack([b_out, b_down, b_up, gain_attn, shift_attn, gain_ffn, shift_ffn, qkv])
    f = front(tokens, w_query, w_key, w_value, vectors)
    attended, lse = attend(f.joined, cell_lengths)
    m = middle(attended, tokens, d_output, w_out, w_up, w_down, vectors, reduce)
    cots = attend_back(f.joined, m.d_att, lse, cell_lengths)
    e = tail(cots, f.normed, f.w, tokens, m.d_mid_out, vectors, m.grad_up_out, m.grad_out, m.small, reduce)
    sums = tuple(g.astype(jnp.float32) for g in (m.sum_down, e.sum_up, e.sum_out, e.sum_joined))
    small_dp, small_all = e.small_dp, e.small_all
    if not reduce:
        sums = lax.psum(sums, DP)
        small_dp = lax.psum(small_dp, DP)
        small_all = lax.psum(small_all, (DP, TP))
    grad_down, grad_up, grad_out, joined = sums
    last = small_dp[7]
    return (
        m.output_out, e.d_tokens, joined[:cols].T, joined[cols : 2 * cols].T, joined[2 * cols :].T,
        last[:cols], last[2 * cols : 3 * cols], grad_out, small_all[0], grad_up, small_dp[6], grad_down,
        small_all[1], small_all[2], small_all[3], small_all[4], small_all[5],
    )


def solution(mesh):
    in_specs = (
        P((DP, TP), None),
        P(None, TP),
        P(None, TP),
        P(None, TP),
        P(TP),
        P(TP),
        P(TP, None),
        P(),
        P(None, TP),
        P(TP),
        P(TP, None),
        P(),
        P(),
        P(),
        P(),
        P(),
        P(DP, None),
        P((DP, TP), None),
    )
    out_specs = (
        P((DP, TP), None),
        P((DP, TP), None),
        P(None, TP),
        P(None, TP),
        P(None, TP),
        P(TP),
        P(TP),
        P(TP, None),
        P(),
        P(None, TP),
        P(TP),
        P(TP, None),
        P(),
        P(),
        P(),
        P(),
        P(),
    )
    return jax.shard_map(local, mesh=mesh, in_specs=in_specs, out_specs=out_specs, check_vma=False)
```

```python
import functools
import heapq

import jax
import jax.numpy as jnp
from jax import lax
from jax.experimental import pallas as pl
from jax.experimental.pallas import tpu as pltpu
from jax.sharding import PartitionSpec as P

D = 1280
HEAD_DIM = 64

MESH_ID = pl.DeviceIdType.MESH
LINK_RATE = 42e3
HOP_US = 2.2
DP, TP = "dp", "tensor"

KIND_A, KIND_B, KIND_C = range(3)
SMALL = -1
OUTER, INNER = range(2)
OUT_Y, IN_Y, OUT_IN, IN_OUT, MID = range(5)
TO_Y, TO_PAIR, TO_MID = range(3)
START, R0, R1, R2, R3, R4, R5A, R5B, R6A, R6B, R6C, R6D, R7A, R7B = range(14)


def plan_order(chunks, gaps, small, pace=0.6, margin=0.4):
    free = dict.fromkeys((OUT_Y, IN_Y, OUT_IN, IN_OUT, MID), 0.0)
    order = [{OUTER: [], INNER: []} for _ in gaps]
    clock = {OUTER: 0.0, INNER: 0.0}
    heap, seen = [], set()
    count = [0]
    turn = 0.0

    def push(when, role, k, name):
        heapq.heappush(heap, (when, count[0], role, k, name))
        count[0] += 1

    def send(when, link, size):
        free[link] = max(when, free[link]) + size / LINK_RATE
        return free[link] + HOP_US

    for slot, (gap, spare) in enumerate(gaps):
        last = slot == len(gaps) - 1
        for role in clock:
            clock[role] += gap
        for k, (_, size, ready) in enumerate(chunks):
            if ready == slot:
                turn = max(turn, max(clock.values()))
                push(turn, OUTER, k, START)
                push(turn, INNER, k, START)
                turn += pace * size / LINK_RATE
        if small and last:
            for role in clock:
                for i in range(6):
                    push(max(clock.values()) + 2.5 * i, role, SMALL, i)
        later, now = [], max(clock.values()) + spare
        while heap:
            when, n, role, k, name = heapq.heappop(heap)
            if k == SMALL:
                clock[role] = max(when, clock[role])
                order[slot][role].append((k, name))
                continue
            kind, size, _ = chunks[k]
            if not last and when + (0.0 if name == START else margin) > now:
                later.append((when, n, role, k, name))
                continue
            when = max(when, clock[role])
            if (kind, role, name) == (KIND_A, INNER, R2) and (k, INNER, R1) not in seen:
                push(when + 0.2, role, k, name)
                continue
            when += 0.2 + (size / 800e3 if name in (R0, R1, R2, R3) else 0.0)
            clock[role] = when
            order[slot][role].append((k, name))
            seen.add((k, role, name))
            for link, part, to, event in SENDS.get((kind, role, name), ()):
                push(send(when, link, size * part), to, k, event)
        for item in later:
            heapq.heappush(heap, item)
        for role in clock:
            clock[role] = max(clock[role], now)
    return order, max(clock.values())


SENDS = {
    (KIND_A, OUTER, START): ((OUT_Y, 0.5, OUTER, R1),),
    (KIND_A, INNER, START): ((IN_Y, 0.5, INNER, R1),),
    (KIND_A, OUTER, R1): ((OUT_IN, 0.5, INNER, R2),),
    (KIND_A, INNER, R2): ((MID, 0.25, INNER, R3),),
    (KIND_A, INNER, R3): ((MID, 0.25, INNER, R4), (IN_OUT, 0.25, OUTER, R5A), (IN_Y, 0.25, INNER, R6A)),
    (KIND_A, INNER, R4): ((IN_OUT, 0.25, OUTER, R5B), (IN_Y, 0.25, INNER, R6B)),
    (KIND_A, OUTER, R5A): ((OUT_Y, 0.25, OUTER, R6A),),
    (KIND_A, OUTER, R5B): ((OUT_Y, 0.25, OUTER, R6B),),
    (KIND_B, OUTER, START): ((OUT_IN, 1.0, INNER, R1),),
    (KIND_B, INNER, R1): ((MID, 0.5, INNER, R2),),
    (KIND_B, INNER, R2): ((IN_Y, 0.25, INNER, R3),),
    (KIND_B, INNER, R3): ((IN_Y, 0.25, INNER, R4), (MID, 0.25, INNER, R5A), (IN_OUT, 0.25, OUTER, R6A)),
    (KIND_B, INNER, R4): ((MID, 0.25, INNER, R5B), (IN_OUT, 0.25, OUTER, R6B)),
    (KIND_B, INNER, R5A): ((IN_OUT, 0.25, OUTER, R6C),),
    (KIND_B, INNER, R5B): ((IN_OUT, 0.25, OUTER, R6D),),
    (KIND_C, OUTER, START): ((OUT_IN, 0.5, INNER, R1),),
    (KIND_C, INNER, R1): ((MID, 0.5, INNER, R2),),
    (KIND_C, INNER, R2): ((IN_OUT, 0.5, OUTER, R3),),
    (KIND_C, OUTER, R3): ((OUT_Y, 0.25, OUTER, R0),),
    (KIND_C, OUTER, R0): ((OUT_Y, 0.25, OUTER, R4), (OUT_IN, 0.25, INNER, R5A)),
    (KIND_C, OUTER, R4): ((OUT_IN, 0.25, INNER, R5B),),
    (KIND_C, INNER, R5A): ((MID, 0.25, INNER, R6A),),
    (KIND_C, INNER, R5B): ((MID, 0.25, INNER, R6B),),
    (KIND_C, INNER, R6A): ((IN_OUT, 0.25, OUTER, R7A),),
    (KIND_C, INNER, R6B): ((IN_OUT, 0.25, OUTER, R7B),),
}
EVENTS = (R0, R1, R2, R3, R4, R5A, R5B, R6A, R6B, R6C, R6D, R7A, R7B)


def slot_rows(kind, rows):
    if kind == KIND_A:
        return {R1: rows // 2, R2: rows // 2, R3: rows // 4}
    if kind == KIND_B:
        return {R1: rows, R2: rows // 2, R3: rows // 4}
    return {R1: rows // 2, R2: rows // 2, R3: rows // 2, R0: rows // 4}


class AllReduce:
    def __init__(self, chunks, grads, finals, lands, land_at, send_sem, recv_sem):
        self.chunks, self.grads, self.lands, self.land_at = chunks, grads, lands, land_at
        self.finals = finals
        self.send_sem, self.recv_sem = send_sem, recv_sem
        d, self.t = lax.axis_index(DP), lax.axis_index(TP)
        self.y, self.z = d % 2, d // 2
        self.side = self.z // 2
        self.inner = jnp.logical_or(self.z == 1, self.z == 2)
        self.to = {
            TO_Y: (self.z * 2 + 1 - self.y, self.t),
            TO_PAIR: ((self.z + 1 - 2 * (self.z % 2)) * 2 + self.y, self.t),
            TO_MID: ((3 - self.z) * 2 + self.y, self.t),
        }
        self.sent = {OUTER: [], INNER: []}

    def region(self, k, half=None, quarter=None, final=False):
        kind, g, first, rows = self.chunks[k]
        start = first
        if half is not None:
            start = start + half * (rows // 2)
            rows = rows // 2
        if quarter is not None:
            start = start + quarter * (rows // 2)
            rows = rows // 2
        if not isinstance(start, int):
            start = pl.multiple_of(start, 16)
        return (self.finals if final else self.grads)[g].at[pl.ds(start, rows)]

    def land(self, k, event):
        kind, g, first, rows = self.chunks[k]
        start, size = self.land_at[(k, event)]
        return self.lands[g].at[pl.ds(start, size)]

    def copy(self, k, event, src, dst, who):
        e = EVENTS.index(event)
        return pltpu.make_async_remote_copy(
            src_ref=src, dst_ref=dst, send_sem=self.send_sem.at[k, e], recv_sem=self.recv_sem.at[k, e],
            device_id=self.to[who], device_id_type=MESH_ID)

    def send(self, role, k, event, src, dst, who):
        c = self.copy(k, event, src, dst, who)
        c.start()
        self.sent[role].append((k, event, src.shape[0]))

    def arrive(self, k, event, dst):
        self.copy(k, event, dst, dst, TO_Y).wait_recv()

    def add(self, k, event, half=None, quarter=None, final=False):
        land = self.land(k, event)
        self.arrive(k, event, land)
        src = self.region(k, half, quarter)
        dst = self.region(k, half, quarter, final)
        rows = land.shape[0]
        step = 32 if rows % 32 == 0 else 16

        def body(i, carry):
            at = pl.ds(pl.multiple_of(i * step, 16), step)
            dst[at] = (src[at].astype(jnp.float32) + land[at].astype(jnp.float32)).astype(jnp.bfloat16)
            return carry

        lax.fori_loop(0, rows // step, body, 0)

    def event(self, role, k, name):
        kind = self.chunks[k][0]
        s, y = self.side, self.y
        R = functools.partial(self.region, k)
        F = functools.partial(self.region, k, final=True)
        send = functools.partial(self.send, role, k)
        key = (kind, role, name)
        if kind == KIND_A:
            if name == START:
                send(R1, R(1 - y), self.land(k, R1), TO_Y)
            elif name == R1:
                self.add(k, R1, y)
                if role == OUTER:
                    send(R2, R(y), self.land(k, R2), TO_PAIR)
            elif name == R2:
                self.add(k, R2, y)
                send(R3, R(y, 1 - s), self.land(k, R3), TO_MID)
            elif name == R3:
                self.add(k, R3, y, s, True)
                send(R4, F(y, s), F(y, s), TO_MID)
                send(R5A, F(y, s), F(y, s), TO_PAIR)
                send(R6A, F(y, s), F(y, s), TO_Y)
            elif name == R4:
                self.arrive(k, R4, F(y, 1 - s))
                send(R5B, F(y, 1 - s), F(y, 1 - s), TO_PAIR)
                send(R6B, F(y, 1 - s), F(y, 1 - s), TO_Y)
            elif name in (R5A, R5B):
                q = s if name == R5A else 1 - s
                self.arrive(k, name, F(y, q))
                send(R6A + name - R5A, F(y, q), F(y, q), TO_Y)
            elif name in (R6A, R6B):
                q = s if name == R6A else 1 - s
                self.arrive(k, name, F(1 - y, q))
        elif kind == KIND_B:
            if name == START:
                if role == OUTER:
                    send(R1, R(), self.land(k, R1), TO_PAIR)
            elif name == R1:
                self.add(k, R1)
                send(R2, R(1 - s), self.land(k, R2), TO_MID)
            elif name == R2:
                self.add(k, R2, s)
                send(R3, R(s, 1 - y), self.land(k, R3), TO_Y)
            elif name == R3:
                self.add(k, R3, s, y, True)
                for event, who in ((R4, TO_Y), (R5A, TO_MID), (R6A, TO_PAIR)):
                    send(event, F(s, y), F(s, y), who)
            elif name == R4:
                self.arrive(k, R4, F(s, 1 - y))
                for event, who in ((R5B, TO_MID), (R6B, TO_PAIR)):
                    send(event, F(s, 1 - y), F(s, 1 - y), who)
            elif name in (R5A, R5B):
                q = y if name == R5A else 1 - y
                self.arrive(k, name, F(1 - s, q))
                send(R6C if name == R5A else R6D, F(1 - s, q), F(1 - s, q), TO_PAIR)
            else:
                h = s if name in (R6A, R6B) else 1 - s
                q = y if name in (R6A, R6C) else 1 - y
                self.arrive(k, name, F(h, q))
        else:
            if name == START:
                if role == OUTER:
                    send(R1, R(1 - s), self.land(k, R1), TO_PAIR)
            elif name == R1:
                self.add(k, R1, 1 - s)
                send(R2, R(1 - s), self.land(k, R2), TO_MID)
            elif name == R2:
                self.add(k, R2, s)
                send(R3, R(s), self.land(k, R3), TO_PAIR)
            elif name == R3:
                self.add(k, R3, s)
                send(R0, R(s, 1 - y), self.land(k, R0), TO_Y)
            elif name == R0:
                self.add(k, R0, s, y, True)
                send(R4, F(s, y), F(s, y), TO_Y)
                send(R5A, F(s, y), F(s, y), TO_PAIR)
            elif name == R4:
                self.arrive(k, R4, F(s, 1 - y))
                send(R5B, F(s, 1 - y), F(s, 1 - y), TO_PAIR)
            elif name in (R5A, R5B):
                q = y if name == R5A else 1 - y
                self.arrive(k, name, F(s, q))
                send(R6A + name - R5A, F(s, q), F(s, q), TO_MID)
            elif name in (R6A, R6B):
                q = y if name == R6A else 1 - y
                self.arrive(k, name, F(1 - s, q))
                send(R7A + name - R6A, F(1 - s, q), F(1 - s, q), TO_PAIR)
            else:
                q = y if name == R7A else 1 - y
                self.arrive(k, name, F(1 - s, q))

    def run(self, order):
        for role, here in ((INNER, self.inner), (OUTER, jnp.logical_not(self.inner))):
            if order[role]:

                @pl.when(here)
                def _(role=role):
                    for k, name in order[role]:
                        if k == SMALL:
                            self.small.step(name)
                        else:
                            self.event(role, k, name)

    def finish(self):
        for role, here in ((INNER, self.inner), (OUTER, jnp.logical_not(self.inner))):
            @pl.when(here)
            def _(role=role):
                for k, event, rows in self.sent[role]:
                    _, g, first, _ = self.chunks[k]
                    src = self.grads[g].at[pl.ds(first, rows)]
                    self.copy(k, event, src, src, TO_Y).wait_send()


def lay_out(chunks, widths):
    at, used = {}, [0] * len(widths)
    for k, (kind, g, first, rows) in enumerate(chunks):
        for event, size in slot_rows(kind, rows).items():
            at[(k, event)] = (used[g], size)
            used[g] += size
    return at, used


class SmallSums:
    def __init__(self, source, totals, lands, send_sem, recv_sem):
        self.source, self.totals, self.lands = source, totals, lands
        self.send_sem, self.recv_sem = send_sem, recv_sem
        d, t = lax.axis_index(DP), lax.axis_index(TP)
        y, z = d % 2, d // 2
        self.to = (
            (z * 2 + 1 - y, t),
            ((z + 1 - 2 * (z % 2)) * 2 + y, t),
            (((z + 2) % 4) * 2 + y, t),
            (d, t + 1 - 2 * (t % 2)),
            (d, (t + 2) % 4),
        )

    def copy(self, i):
        src = self.source if i == 0 else self.totals.at[i - 1]
        return pltpu.make_async_remote_copy(
            src_ref=src, dst_ref=self.lands.at[i], send_sem=self.send_sem.at[i],
            recv_sem=self.recv_sem.at[i], device_id=self.to[i], device_id_type=MESH_ID)

    def step(self, i):
        if i > 0:
            self.copy(i - 1).wait_recv()
            have = self.source[...] if i == 1 else self.totals[i - 2]
            self.totals[i - 1] = have + self.lands[i - 1]
        if i < 5:
            self.copy(i).start()

    def finish(self):
        for i in range(5):
            self.copy(i).wait_send()


norm_eps = 1e-05
MASKED = -1e30
MOST_CELL = 384


def norm_rows(values, gain, shift):
    center = values - jnp.mean(values, axis=-1, keepdims=True)
    spread = jnp.mean(center * center, axis=-1, keepdims=True)
    return center * lax.rsqrt(spread + norm_eps) * gain + shift


def inner_rows(left, right):
    return lax.dot_general(
        left, right, (((0,), (0,)), ((), ())), preferred_element_type=jnp.float32
    )


def times_transposed(left, right):
    return lax.dot_general(
        left, right, (((1,), (1,)), ((), ())), preferred_element_type=jnp.float32
    )


def each_cell(lengths, row, seq_len, body):
    widths = sorted({min(w, seq_len) for w in (128, 256, MOST_CELL + 16)})

    def step(i, start):
        length = lengths[row, i]
        lower = 0
        for width in widths:
            first = pl.multiple_of(jnp.minimum(start // 16 * 16, seq_len - width), 16)

            @pl.when(jnp.logical_and(length > lower, length <= width - 16))
            def _(width=width, first=first):
                down = first + lax.broadcasted_iota(jnp.int32, (width, 1), 0)
                along = first + lax.broadcasted_iota(jnp.int32, (1, width), 1)
                inside = [jnp.logical_and(p >= start, p < start + length) for p in (down, along)]
                body(i, first, width, inside[0], inside[1])

            lower = width - 16
        return start + length

    lax.fori_loop(0, lengths.shape[1], step, jnp.int32(0))


def attend_kernel(heads, lengths, joined, out, lse):
    seq_len, wide = out.shape

    def body(cell, first, width, down, along):
        rows = pl.ds(first, width)
        seen = jnp.logical_and(down, along)
        for h in range(heads):
            at = h * HEAD_DIM
            query = joined[rows, at : at + HEAD_DIM] * jnp.bfloat16(HEAD_DIM**-0.5)
            key = joined[rows, wide + at : wide + at + HEAD_DIM]
            value = joined[rows, 2 * wide + at : 2 * wide + at + HEAD_DIM]
            scores = jnp.where(seen, times_transposed(query, key), MASKED)
            top = jnp.max(scores, axis=1, keepdims=True)
            expo = jnp.exp(scores - top)
            total = jnp.sum(expo, axis=1, keepdims=True)
            probs = (expo * (1.0 / total)).astype(jnp.bfloat16)
            part = jnp.dot(probs, value, preferred_element_type=jnp.float32).astype(jnp.bfloat16)
            cols = slice(at, at + HEAD_DIM)
            out[rows, cols] = jnp.where(down, part, out[rows, cols])
            lse[rows, h : h + 1] = jnp.where(down, top + jnp.log(total), lse[rows, h : h + 1])
        number = jnp.full((width, 1), cell, jnp.int32).astype(jnp.float32)
        lse[rows, heads : heads + 1] = jnp.where(down, number, lse[rows, heads : heads + 1])

    each_cell(lengths, pl.program_id(0), seq_len, body)


def attend(joined, lengths):
    n, wide = lengths.shape[0], joined.shape[1] // 3
    seq_len = joined.shape[0] // n
    heads = wide // HEAD_DIM
    return pl.pallas_call(
        functools.partial(attend_kernel, heads),
        grid=(n,),
        out_shape=[
            jax.ShapeDtypeStruct((joined.shape[0], wide), jnp.bfloat16),
            jax.ShapeDtypeStruct((joined.shape[0], 128), jnp.float32),
        ],
        in_specs=[
            pl.BlockSpec(memory_space=pltpu.SMEM),
            pl.BlockSpec((seq_len, 3 * wide), lambda i: (i, 0)),
        ],
        out_specs=[
            pl.BlockSpec((seq_len, wide), lambda i: (i, 0)),
            pl.BlockSpec((seq_len, 128), lambda i: (i, 0)),
        ],
        compiler_params=pltpu.CompilerParams(vmem_limit_bytes=40 << 20),
        name="attend",
    )(lengths, joined)


COLS = 256
B_OUT, B_DOWN, B_UP, GAIN_ATTN, SHIFT_ATTN, GAIN_FFN, SHIFT_FFN, B_QKV = range(8)


class Refs:
    def __init__(self, names, refs):
        self.__dict__.update(zip(names, refs))


def call(body, name, ins, loose, outs, loose_outs, scratch, collective_id):
    names = list(ins) + list(loose) + list(outs) + list(loose_outs) + list(scratch)
    vmem, stay = pl.BlockSpec(memory_space=pltpu.VMEM), pl.BlockSpec(memory_space=pl.ANY)
    out = pl.pallas_call(
        lambda *refs: body(Refs(names, refs)),
        out_shape=list(outs.values()) + list(loose_outs.values()),
        in_specs=[vmem] * len(ins) + [stay] * len(loose),
        out_specs=[vmem] * len(outs) + [stay] * len(loose_outs),
        scratch_shapes=list(scratch.values()),
        compiler_params=pltpu.CompilerParams(
            collective_id=collective_id, has_side_effects=True, vmem_limit_bytes=64000 << 10
        ),
        name=name,
    )(*ins.values(), *loose.values())
    return Refs(list(outs) + list(loose_outs), out)


def low(*shape):
    return pltpu.VMEM(shape, jnp.bfloat16)


def full(*shape):
    return pltpu.VMEM(shape, jnp.float32)


def dma(*shape):
    return pltpu.SemaphoreType.DMA(shape)


def at_row(start, rows):
    return pl.ds(pl.multiple_of(start, 16), rows)


def at_col(i, cols=COLS):
    return pl.ds(pl.multiple_of(i * cols, cols), cols)


def remote(src, dst, send, recv, to):
    return pltpu.make_async_remote_copy(
        src_ref=src, dst_ref=dst, send_sem=send, recv_sem=recv, device_id=to, device_id_type=MESH_ID)


class Place:
    def __init__(self):
        self.d, self.t = lax.axis_index(DP), lax.axis_index(TP)
        self.across = self.t + 1 - 2 * (self.t % 2)
        self.beyond = (self.t + 2) % 4
        self.far = 3 - self.t

    def group(self):
        return [(self.d, self.across), (self.d, self.beyond)]


def meet(peers):
    barrier = pltpu.get_barrier_semaphore()
    for peer in peers:
        pl.semaphore_signal(barrier, inc=1, device_id=peer, device_id_type=MESH_ID)
    pl.semaphore_wait(barrier, len(peers))


class Gather:
    def __init__(self, place, whole, send, recv, cuts, rows):
        self.p, self.whole, self.send, self.recv, self.cuts = place, whole, send, recv, cuts
        self.rows = rows

    def piece(self, owner, i):
        first, rows = self.cuts[i]
        return self.whole.at[at_row(owner * self.rows + first, rows)]

    def copy(self, kind, i, owner):
        ref = self.piece(owner, i)
        to = self.p.beyond if kind == 1 else self.p.across
        return remote(ref, ref, self.send.at[kind, i], self.recv.at[kind, i], (self.p.d, to))

    def start(self, i):
        self.copy(1, i, self.p.t).start()
        self.copy(0, i, self.p.t).start()

    def across(self):
        for i in range(len(self.cuts)):
            self.copy(0, i, self.p.across).wait_recv()

    def beyond(self, i):
        self.copy(1, i, self.p.beyond).wait_recv()
        self.copy(2, i, self.p.beyond).start()

    def far(self, i):
        self.copy(2, i, self.p.far).wait_recv()

    def rest(self):
        for i in range(len(self.cuts)):
            self.beyond(i)
        for i in range(len(self.cuts)):
            self.far(i)

    def finish(self):
        for i in range(len(self.cuts)):
            self.copy(0, i, self.p.t).wait_send()
            self.copy(1, i, self.p.t).wait_send()
            self.copy(2, i, self.p.beyond).wait_send()


class Scatter:
    def __init__(self, place, rows, out, near, cross, last, own, send, recv):
        self.p, self.rows = place, rows
        self.out, self.near, self.cross, self.last, self.own = out, near, cross, last, own
        self.send, self.recv = send, recv

    def copies(self):
        d, p = self.p.d, self.p
        return (
            remote(self.out.at[0], self.near.at[0], self.send.at[0], self.recv.at[0], (d, p.across)),
            remote(self.out.at[1], self.near.at[1], self.send.at[1], self.recv.at[1], (d, p.across)),
        ) + tuple(
            remote(self.cross.at[pl.ds(*cut)], self.last.at[pl.ds(*cut)], self.send.at[2 + i], self.recv.at[2 + i], (d, p.beyond))
            for i, cut in enumerate(cuts_of(self.rows))
        )

    def start(self, compute, between=lambda: None):
        copies = self.copies()

        def keep(slot):
            def store(j, value):
                self.out[slot, :, at_col(j)] = value.astype(jnp.bfloat16)

            return store

        def add(j, value):
            total = value + self.near[0, :, at_col(j)].astype(jnp.float32)
            self.cross[:, at_col(j)] = total.astype(jnp.bfloat16)

        def hold(j, value):
            self.own[:, at_col(j)] = value

        compute(self.p.far * self.rows, keep(0))
        copies[0].start()
        between()
        compute(self.p.across * self.rows, keep(1))
        copies[1].start()
        between()
        copies[0].wait_recv()
        compute(self.p.beyond * self.rows, add)
        copies[2].start()
        copies[3].start()
        between()
        compute(self.p.t * self.rows, hold)

    def arrive(self, i):
        copies = self.copies()
        if i == 0:
            copies[1].wait_recv()
        copies[2 + i].wait_recv()

    def total(self, rows):
        return self.own[rows] + (self.near[1, rows].astype(jnp.float32) + self.last[rows].astype(jnp.float32))

    def finish(self):
        for c in self.copies():
            c.wait_send()


def scatter_scratch(prefix, rows):
    return {
        prefix + "out": low(2, rows, D), prefix + "near": low(2, rows, D), prefix + "cross": low(rows, D),
        prefix + "last": low(rows, D), prefix + "own": full(rows, D),
        prefix + "send": dma(4), prefix + "recv": dma(4),
    }


def scatter_of(refs, prefix, place, rows):
    names = ("out", "near", "cross", "last", "own", "send", "recv")
    return Scatter(place, rows, *[getattr(refs, prefix + n) for n in names])


def cuts_of(rows):
    half = (rows // 2 + 15) // 16 * 16
    return ((0, half), (half, rows - half))


def each_block(rows, body, init=0):
    for first, count in cuts_of(rows):
        out = body(first, count, init)
        init = init if out is None else out
    return init


def each_col(width, body):
    def step(j, carry):
        body(j)
        return carry

    lax.fori_loop(0, width // COLS, step, 0)


def norm_back(x, cot, gain):
    center = x - jnp.mean(x, axis=-1, keepdims=True)
    rate = lax.rsqrt(jnp.mean(center * center, axis=-1, keepdims=True) + norm_eps)
    hat = center * rate
    inner = cot * gain
    part = inner - jnp.mean(inner, axis=-1, keepdims=True) - hat * jnp.mean(inner * hat, axis=-1, keepdims=True)
    return part * rate, cot * hat


def reduce_scratch(chunks, shapes):
    at, used = lay_out(chunks, shapes)
    out = {}
    for i, (u, s) in enumerate(zip(used, shapes)):
        out["land%d" % i] = low(max(u, 16), s[1])
    out["send"] = dma(max(len(chunks), 1), len(EVENTS))
    out["recv"] = dma(max(len(chunks), 1), len(EVENTS))
    return out, at


def cut_rows(pieces, size, kinds):
    chunks, timed = [], []
    for g, first, rows, columns, slot in pieces:
        end = first + rows
        while first < end:
            here = size if end - first >= 2 * size or end - first == size else end - first
            kind = kinds[len(chunks) % len(kinds)]
            chunks.append((kind, g, first, here))
            timed.append((kind, here * columns * 2, slot))
            first += here
    return chunks, timed


def windows(seqs, every, rows):
    seq_len = every // seqs
    block = rows if seq_len % rows == 0 else seq_len
    for first in range(0, every, block):
        row = first // seq_len * seq_len
        low_key = max(0, first - row - MOST_CELL + 1) // 128 * 128
        high_key = min(seq_len, -(-(first - row + block + MOST_CELL - 1) // 128) * 128)
        yield first, block, row + low_key, row + high_key


def attend_back(r, seqs, advance):
    every, wide = r.d_att.shape
    heads, scale = wide // HEAD_DIM, HEAD_DIM**-0.5
    r.turned[...] = r.lse[...].T[: r.turned.shape[0]]
    r.d_keys[...] = jnp.zeros_like(r.d_keys)
    r.d_values[...] = jnp.zeros_like(r.d_values)
    for first, block, low_key, high_key in windows(seqs, every, r.tokens.shape[0]):
        here, keys = slice(first, first + block), slice(low_key, high_key)
        for h in range(heads):
            at = h * HEAD_DIM
            cols = slice(at, at + HEAD_DIM)
            query = r.qkv[here, cols] * jnp.bfloat16(scale)
            key = r.qkv[keys, wide + at : wide + at + HEAD_DIM]
            value = r.qkv[keys, 2 * wide + at : 2 * wide + at + HEAD_DIM]
            cot = r.d_att[here, cols]
            seen = r.lse[here, heads : heads + 1] == r.turned[heads : heads + 1, keys]
            scores = jnp.where(seen, times_transposed(query, key), MASKED)
            probs = jnp.exp(scores - r.lse[here, h : h + 1])
            r.d_values[h, keys] += inner_rows(probs.astype(jnp.bfloat16), cot)
            d_probs = times_transposed(cot, value)
            offset = jnp.sum(probs * d_probs, axis=1, keepdims=True)
            d_scores = (probs * (d_probs - offset)).astype(jnp.bfloat16)
            r.cots[here, cols] = (jnp.dot(d_scores, key, preferred_element_type=jnp.float32) * scale).astype(jnp.bfloat16)
            r.d_keys[h, keys] += inner_rows(d_scores, query)
            advance()
    for h in range(heads):
        for i, part in ((1, r.d_keys), (2, r.d_values)):
            r.cots[:, i * wide + h * HEAD_DIM : i * wide + (h + 1) * HEAD_DIM] = part[h].astype(jnp.bfloat16)


def tail_kernel(chunks, order, land_at, reduce, seqs, r):
    place = Place()
    rows = r.tokens.shape[0]
    wide = r.w.shape[0]
    step = iter(order)
    late = [
        pltpu.make_async_copy(src, dst, r.fill.at[2 + i])
        for i, (src, dst) in enumerate(zip((r.normed_in, r.w_in, r.tokens_in, r.d_mid_in), (r.normed, r.w, r.tokens, r.d_mid)))
    ]
    if reduce:
        up, out, joined = r.up, r.out, r.joined
        ar = AllReduce(
            chunks, (up, out, joined), (r.sum_up, r.sum_out, r.sum_joined), (r.land0, r.land1, r.land2),
            land_at, r.send, r.recv)
        ar.small = SmallSums(r.small, r.totals, r.small_lands, r.small_send, r.small_recv)
        peers = [ar.to[TO_Y], ar.to[TO_PAIR], ar.to[TO_MID], ar.small.to[2]] + place.group()
    else:
        up, out, joined = r.sum_up, r.sum_out, r.sum_joined
        peers = place.group()
    fills = [pltpu.make_async_copy(r.up_in, up, r.fill.at[0]), pltpu.make_async_copy(r.out_in, out, r.fill.at[1])]
    for f in fills + late:
        f.start()
    meet(peers)
    for f in fills:
        f.wait()

    def advance():
        if reduce:
            ar.run(next(step))

    scatter = scatter_of(r, "s", place, rows)
    advance()
    attend_back(r, seqs, advance)
    for f in late:
        f.wait()

    def to_first(first, store):
        cots = r.cots[at_row(first, rows)]
        each_col(D, lambda j: store(j, jnp.dot(cots, r.w[:, at_col(j)], preferred_element_type=jnp.float32)))

    scatter.start(to_first, advance)
    advance()
    for i in range(0, wide, COLS):
        n = min(COLS, wide - i)
        joined[i : i + n] = inner_rows(r.cots[:, i : i + n], r.normed[...]).astype(jnp.bfloat16)
        advance()
    r.small[...] = r.small_in[...]
    r.small[7:8, :wide] = lax.fori_loop(
        0, r.cots.shape[0] // rows,
        lambda i, c: c + jnp.sum(r.cots[at_row(i * rows, rows)].astype(jnp.float32), axis=0, keepdims=True),
        jnp.zeros((1, wide), jnp.float32))
    advance()
    scatter.arrive(0)
    scatter.arrive(1)
    gain = r.vectors[GAIN_ATTN]

    def back(first, count, carry):
        at = at_row(first, count)
        cot = scatter.total(at)
        part, gained = norm_back(r.tokens[at].astype(jnp.float32), cot, gain)
        r.d_tokens[at] = r.d_mid[at] + part
        return carry + jnp.stack([jnp.sum(gained, axis=0), jnp.sum(cot, axis=0)])

    r.small[2:4] = each_block(rows, back, jnp.zeros((2, D), jnp.float32))
    scatter.finish()
    advance()
    if reduce:
        ar.finish()
        ar.small.finish()
        r.small_dp[...] = r.totals[2]
        r.small_all[...] = r.totals[4]
    else:
        r.small_dp[...] = r.small[...]
        r.small_all[...] = r.small[...]


def copy_of(x):
    return jax.ShapeDtypeStruct(x.shape, x.dtype)


TAIL_KINDS = (0, 0, 2, 0, 2, 0, 0, 2, 2, 2, 1, 0, 0, 2, 0, 2, 0, 0, 0)
MID_KINDS = (2, 2, 0, 2, 2, 0, 2, 0, 0, 0)
TAIL_SIZE, TAIL_PACE, MID_SIZE, MID_PACE = 128, 0.125, 128, 0.52


def tail(qkv, d_att, lse, seqs, normed, w, tokens, d_mid, vectors, up, out, small, reduce):
    rows, wide = tokens.shape[0], w.shape[0]
    every = qkv.shape[0]
    heads = d_att.shape[1] // HEAD_DIM
    units = heads * len(list(windows(seqs, every, rows)))
    joined = jax.ShapeDtypeStruct((wide, D), jnp.bfloat16)
    shapes = [up.shape, out.shape, joined.shape]
    pieces = [(0, 0, up.shape[0], D, 0), (1, 0, out.shape[0], D, 0)]
    pieces += [(2, i, min(COLS, wide - i), D, 5 + units + i // COLS) for i in range(0, wide, COLS)]
    chunks, timed = cut_rows(pieces, TAIL_SIZE, TAIL_KINDS)
    gaps = [(0.0, 0.0)] + [(2.2, 0.0)] * (units + 4) + [(1.6, 0.0)] * len(range(0, wide, COLS)) + [(1.5, 4.0), (3.0, 0.0)]
    order, _ = plan_order(timed, gaps, True, TAIL_PACE)
    scratch = scatter_scratch("s", rows)
    scratch.update(
        small=full(8, D), fill=dma(6), turned=full(8, every), cots=low(*qkv.shape), d_keys=full(heads, every, HEAD_DIM),
        d_values=full(heads, every, HEAD_DIM), normed=low(every, D), w=low(wide, D), tokens=low(rows, D),
        d_mid=full(rows, D))
    land_at = None
    if reduce:
        more, land_at = reduce_scratch(chunks, shapes)
        scratch.update(more)
        scratch.update(
            up=low(*up.shape), out=low(*out.shape), joined=low(wide, D), totals=full(5, 8, D),
            small_lands=full(5, 8, D), small_send=dma(5), small_recv=dma(5))
    return call(
        functools.partial(tail_kernel, chunks, order, land_at, reduce, seqs), "tail",
        dict(qkv=qkv, d_att=d_att, lse=lse, vectors=vectors, small_in=small),
        dict(normed_in=normed, w_in=w, tokens_in=tokens, d_mid_in=d_mid, up_in=up, out_in=out),
        dict(d_tokens=jax.ShapeDtypeStruct((rows, D), jnp.float32), sum_up=copy_of(up), sum_out=copy_of(out),
             sum_joined=joined, small_dp=copy_of(small), small_all=copy_of(small)),
        {}, scratch, 0)


def gelu_and_slope(x):
    rate = (2.0 / jnp.pi) ** 0.5
    square = x * x
    bent = jnp.tanh(rate * x * (1.0 + 0.044715 * square))
    half = 0.5 * (1.0 + bent)
    return x * half, half + 0.5 * x * (1.0 - bent * bent) * rate * (1.0 + 0.134145 * square)


def middle_kernel(chunks, order, land_at, reduce, r):
    place = Place()
    rows = r.tokens.shape[0]
    every = r.attended.shape[0]
    hidden = r.act.shape[1]
    step = iter(order)
    down = r.down if reduce else r.sum_down
    peers = place.group()
    if reduce:
        ar = AllReduce(chunks, (down,), (r.sum_down,), (r.land0,), land_at, r.send, r.recv)
        peers += [ar.to[TO_Y], ar.to[TO_PAIR], ar.to[TO_MID]]

    def advance():
        if reduce:
            ar.run(next(step))

    soon = cuts_of(rows)[0][1]
    cots = Gather(place, r.cots, r.cots_send, r.cots_recv, ((soon, rows - soon),), rows)
    second = Gather(place, r.second, r.second_send, r.second_recv, cuts_of(rows), rows)
    branch = Gather(place, r.branch, r.branch_send, r.branch_recv, cuts_of(rows), rows)
    mine = place.t * rows

    fills = [
        pltpu.make_async_copy(
            r.d_output.at[pl.ds(soon, rows - soon)], r.cots.at[at_row(mine + soon, rows - soon)], r.fill.at[0])
    ] + [
        pltpu.make_async_copy(r.early.at[pl.ds(i * soon, soon)], r.cots.at[pl.ds(i * rows, soon)], r.fill.at[1 + i])
        for i in range(4)
    ] + [
        pltpu.make_async_copy(r.w_up_in, r.w_up, r.fill.at[5]),
        pltpu.make_async_copy(r.w_down_in, r.w_down, r.fill.at[6]),
    ]
    drains = [
        pltpu.make_async_copy(r.grad_up, r.grad_up_out, r.fill.at[7]),
        pltpu.make_async_copy(r.output, r.output_out, r.fill.at[8]),
        pltpu.make_async_copy(r.mid, r.d_mid_out, r.fill.at[9]),
    ]
    for f in fills:
        f.start()
    meet(peers)

    def to_out(first, store):
        att = r.attended[at_row(first, rows)]
        each_col(D, lambda j: store(j, jnp.dot(att, r.w_out[:, at_col(j)], preferred_element_type=jnp.float32)))

    one = scatter_of(r, "s", place, rows)
    one.start(to_out)
    gain, shift = r.vectors[GAIN_FFN], r.vectors[SHIFT_FFN]
    for i, (first, count) in enumerate(second.cuts):
        at = at_row(first, count)
        one.arrive(i)
        mid = r.tokens[at].astype(jnp.float32) + one.total(at) + r.vectors[B_OUT]
        r.mid[at] = mid
        r.second[at_row(mine + first, count)] = norm_rows(mid, gain, shift).astype(jnp.bfloat16)
        second.start(i)
    for f in fills[:5]:
        f.wait()
    cots.start(0)
    one.finish()

    def up(first, count):
        at = at_row(first, count)

        def tile(j):
            col = at_col(j)
            pre = jnp.dot(r.second[at], r.w_up[:, col], preferred_element_type=jnp.float32) + r.vectors[B_UP, col]
            act, slope = gelu_and_slope(pre)
            r.act[at, col] = act.astype(jnp.bfloat16)
            r.slope[at, col] = slope

        each_col(hidden, tile)

    pair = place.t // 2 * 2 * rows
    fills[5].wait()
    fills[6].wait()
    second.across()
    up(pair, 2 * rows)
    second.rest()
    up(2 * rows - pair, 2 * rows)

    def to_down(first, store):
        act = r.act[at_row(first, rows)]
        each_col(D, lambda j: store(j, jnp.dot(act, r.w_down[:, at_col(j)], preferred_element_type=jnp.float32)))

    cots.across()
    cots.rest()
    for i in range(hidden // COLS):
        col = slice(i * COLS, (i + 1) * COLS)
        down[col] = inner_rows(r.act[:, col], r.cots[...]).astype(jnp.bfloat16)
        advance()
    three = Scatter(place, rows, r.sout, r.snear, r.scross, r.slast, r.sown, r.again_send, r.again_recv)
    three.start(to_down, advance)
    advance()
    for j in range(hidden // COLS):
        col = slice(j * COLS, (j + 1) * COLS)
        d_pre = (times_transposed(r.cots[...], r.w_down[col]) * r.slope[:, col]).astype(jnp.bfloat16)
        r.d_pre[:, col] = d_pre
        r.small[6:7, col] = jnp.sum(d_pre.astype(jnp.float32), axis=0, keepdims=True)
        advance()

    def to_second(first, store):
        d_pre = r.d_pre[at_row(first, rows)]
        each_col(D, lambda j: store(j, times_transposed(d_pre, r.w_up[at_row(j * COLS, COLS)])))

    two = scatter_of(r, "t", place, rows)
    two.start(to_second, advance)
    advance()
    for i in range(D // COLS):
        col = slice(i * COLS, (i + 1) * COLS)
        r.grad_up[col] = inner_rows(r.second[:, col], r.d_pre[...]).astype(jnp.bfloat16)
        advance()
    drains[0].start()
    three.arrive(0)
    three.arrive(1)

    def finish(first, count, carry):
        at = at_row(first, count)
        r.output[at] = (r.mid[at] + three.total(at) + r.vectors[B_DOWN]).astype(jnp.bfloat16)

    each_block(rows, finish)
    drains[1].start()
    advance()
    sums = jnp.zeros((4, D), jnp.float32)
    for i, (first, count) in enumerate(branch.cuts):
        at = at_row(first, count)
        two.arrive(i)
        cot = two.total(at)
        part, gained = norm_back(r.mid[at], cot, gain)
        d_output = r.cots[at_row(mine + first, count)].astype(jnp.float32)
        d_mid = d_output + part
        r.mid[at] = d_mid
        low_part = d_mid.astype(jnp.bfloat16)
        r.branch[at_row(mine + first, count)] = low_part
        branch.start(i)
        parts = (low_part.astype(jnp.float32), d_output, gained, cot)
        sums = sums + jnp.stack([jnp.sum(p, axis=0) for p in parts])
    drains[2].start()
    r.small[0:2] = sums[0:2]
    r.small[2:4] = jnp.zeros((2, D), jnp.float32)
    r.small[4:6] = sums[2:4]
    r.small[7:8] = jnp.zeros((1, D), jnp.float32)

    def attn(first, count):
        at = at_row(first, count)
        r.d_att[at] = times_transposed(r.branch[at], r.w_out[...]).astype(jnp.bfloat16)

    advance()
    branch.across()
    attn(pair, 2 * rows)
    advance()
    branch.rest()
    attn(2 * rows - pair, 2 * rows)
    wide = r.attended.shape[1]
    for i in range(0, wide, COLS):
        col = slice(i, min(wide, i + COLS))
        r.grad_out[col] = inner_rows(r.attended[:, col], r.branch[...]).astype(jnp.bfloat16)
    advance()
    for part in (cots, second, branch, two, three):
        part.finish()
    for part in drains:
        part.wait()
    if reduce:
        ar.finish()


def middle(attended, tokens, d_output, early, w_out, w_up, w_down, vectors, reduce):
    rows, every = tokens.shape[0], attended.shape[0]
    hidden = w_up.shape[1]
    groups = hidden // COLS
    chunks, timed = cut_rows([(0, i * COLS, COLS, D, i) for i in range(groups)], MID_SIZE, MID_KINDS)
    gaps = [(1.5, 0.0)] * groups + [(2.2, 0.0)] * 4 + [(1.8, 0.0)] * groups + [(2.2, 0.0)] * 4 + [(1.5, 0.0)] * (D // COLS)
    gaps += [(1.5, 3.0), (2.5, 2.0), (2.0, 12.0), (5.0, 0.0)]
    order, _ = plan_order(timed, gaps, False, MID_PACE)
    scratch = scatter_scratch("s", rows)
    scratch.update(scatter_scratch("t", rows))
    scratch.update(
        again_send=dma(4), again_recv=dma(4), cots=low(every, D), second=low(every, D), branch=low(every, D),
        cots_send=dma(3, 2), cots_recv=dma(3, 2), second_send=dma(3, 2), second_recv=dma(3, 2),
        branch_send=dma(3, 2), branch_recv=dma(3, 2), mid=full(rows, D), act=low(every, hidden),
        slope=full(every, hidden), d_pre=low(every, hidden), w_up=low(*w_up.shape), w_down=low(*w_down.shape),
        output=low(rows, D), grad_up=low(*w_up.shape), fill=dma(10))
    land_at = None
    if reduce:
        more, land_at = reduce_scratch(chunks, [w_down.shape])
        scratch.update(more, down=low(*w_down.shape))
    return call(
        functools.partial(middle_kernel, chunks, order, land_at, reduce), "middle",
        dict(attended=attended, tokens=tokens, w_out=w_out, vectors=vectors),
        dict(d_output=d_output, early=early, w_up_in=w_up, w_down_in=w_down),
        dict(d_att=copy_of(attended), sum_down=copy_of(w_down), grad_out=copy_of(w_out),
             small=jax.ShapeDtypeStruct((8, D), jnp.float32)),
        dict(output_out=copy_of(tokens), d_mid_out=jax.ShapeDtypeStruct((rows, D), jnp.float32), grad_up_out=copy_of(w_up)),
        scratch, 1)


def front_kernel(r):
    place = Place()
    rows = r.tokens.shape[0]
    wide = r.w.shape[0]
    third = wide // 3
    cuts = cuts_of(rows)
    soon = cuts[0][1]
    tokens = Gather(place, r.whole, r.send, r.recv, cuts, rows)
    cots = Gather(place, r.early, r.cots_send, r.cots_recv, ((0, soon),), soon)
    mine = place.t * rows
    r.whole[at_row(mine, rows)] = r.tokens[...]
    fill = pltpu.make_async_copy(r.d_output.at[pl.ds(0, soon)], r.early.at[at_row(place.t * soon, soon)], r.fill.at[0])
    fill.start()
    meet(place.group())
    tokens.start(0)
    tokens.start(1)
    fill.wait()
    cots.start(0)
    for i, part in enumerate((r.w_query, r.w_key, r.w_value)):
        r.w[i * third : (i + 1) * third] = part[...]
    drains = [pltpu.make_async_copy(r.w, r.w_out, r.fill.at[1])]
    drains[0].start()
    gain, shift = r.vectors[GAIN_ATTN], r.vectors[SHIFT_ATTN]

    def project(owner, first, count):
        at = at_row(owner * rows + first, count)
        r.normed[at] = norm_rows(r.whole[at].astype(jnp.float32), gain, shift).astype(jnp.bfloat16)
        for i in range(0, wide, COLS):
            col = slice(i, min(wide, i + COLS))
            part = times_transposed(r.normed[at], r.w[col]) + r.vectors[B_QKV, col]
            r.joined[at, col] = part.astype(jnp.bfloat16)
        for src, dst in ((r.normed, r.normed_out), (r.joined, r.joined_out)):
            drains.append(pltpu.make_async_copy(src.at[at], dst.at[at], r.fill.at[1 + len(drains)]))
            drains[-1].start()

    project(place.t, 0, rows)
    tokens.across()
    project(place.across, 0, rows)
    for i, cut in enumerate(cuts):
        tokens.beyond(i)
        project(place.beyond, *cut)
        tokens.far(i)
        project(place.far, *cut)
    tokens.finish()
    cots.across()
    cots.rest()
    cots.finish()
    for part in drains:
        part.wait()


def front(tokens, d_output, w_query, w_key, w_value, vectors):
    rows = tokens.shape[0]
    every = rows * lax.axis_size(TP)
    parts = [w.T for w in (w_query, w_key, w_value)]
    wide = 3 * parts[0].shape[0]
    early = cuts_of(rows)[0][1] * lax.axis_size(TP)
    bf16 = jnp.bfloat16
    return call(
        front_kernel, "front",
        dict(tokens=tokens, w_query=parts[0], w_key=parts[1], w_value=parts[2], vectors=vectors),
        dict(d_output=d_output),
        dict(early=jax.ShapeDtypeStruct((early, D), bf16)),
        dict(normed_out=jax.ShapeDtypeStruct((every, D), bf16), joined_out=jax.ShapeDtypeStruct((every, wide), bf16),
             w_out=jax.ShapeDtypeStruct((wide, D), bf16)),
        dict(whole=low(every, D), normed=low(every, D), joined=low(every, wide), w=low(wide, D), send=dma(3, 2),
             recv=dma(3, 2), cots_send=dma(3, 1), cots_recv=dma(3, 1), fill=dma(16)), 2)


def local(
    tokens, w_query, w_key, w_value, b_query, b_value, w_out, b_out, w_up, b_up, w_down, b_down,
    gain_attn, shift_attn, gain_ffn, shift_ffn, cell_lengths, d_output,
):
    cols = w_query.shape[1]
    reduce = lax.axis_size(DP) == 8
    vectors = jnp.concatenate(
        [b_out, b_down, b_up, gain_attn, shift_attn, gain_ffn, shift_ffn, b_query, jnp.zeros_like(b_query), b_value,
         jnp.zeros(D - 3 * cols)]
    ).reshape(8, D)
    f = front(tokens, d_output, w_query, w_key, w_value, vectors)
    attended, lse = attend(f.joined_out, cell_lengths)
    m = middle(attended, tokens, d_output, f.early, w_out, w_up, w_down, vectors, reduce)
    seqs = cell_lengths.shape[0]
    e = tail(f.joined_out, m.d_att, lse, seqs, f.normed_out, f.w_out, tokens, m.d_mid_out, vectors, m.grad_up_out, m.grad_out, m.small, reduce)
    sums = tuple(g.astype(jnp.float32) for g in (m.sum_down, e.sum_up, e.sum_out, e.sum_joined))
    small_dp, small_all = e.small_dp, e.small_all
    if not reduce:
        sums = lax.psum(sums, DP)
        small_dp = lax.psum(small_dp, DP)
        small_all = lax.psum(small_all, (DP, TP))
    grad_down, grad_up, grad_out, joined = sums
    last = small_dp[7]
    return (
        m.output_out, e.d_tokens, joined[:cols].T, joined[cols : 2 * cols].T, joined[2 * cols :].T,
        last[:cols], last[2 * cols : 3 * cols], grad_out, small_all[0], grad_up, small_dp[6], grad_down,
        small_all[1], small_all[2], small_all[3], small_all[4], small_all[5],
    )


def solution(mesh):
    in_specs = (
        P((DP, TP), None),
        P(None, TP),
        P(None, TP),
        P(None, TP),
        P(TP),
        P(TP),
        P(TP, None),
        P(),
        P(None, TP),
        P(TP),
        P(TP, None),
        P(),
        P(),
        P(),
        P(),
        P(),
        P(DP, None),
        P((DP, TP), None),
    )
    out_specs = (
        P((DP, TP), None),
        P((DP, TP), None),
        P(None, TP),
        P(None, TP),
        P(None, TP),
        P(TP),
        P(TP),
        P(TP, None),
        P(),
        P(None, TP),
        P(TP),
        P(TP, None),
        P(),
        P(),
        P(),
        P(),
        P(),
    )
    return jax.shard_map(local, mesh=mesh, in_specs=in_specs, out_specs=out_specs, check_vma=False)
```

```python
import functools
import heapq

import jax
import jax.numpy as jnp
from jax import lax
from jax.experimental import pallas as pl
from jax.experimental.pallas import tpu as pltpu
from jax.sharding import PartitionSpec as P

D = 1280
HEAD_DIM = 64

MESH_ID = pl.DeviceIdType.MESH
LINK_RATE = 42e3
HOP_US = 2.2
DP, TP = "dp", "tensor"

KIND_A, KIND_B, KIND_C = range(3)
SMALL = -1
OUTER, INNER = range(2)
OUT_Y, IN_Y, OUT_IN, IN_OUT, MID = range(5)
TO_Y, TO_PAIR, TO_MID = range(3)
START, R0, R1, R2, R3, R4, R5A, R5B, R6A, R6B, R6C, R6D, R7A, R7B = range(14)


def plan_order(chunks, gaps, small, pace=0.6, margin=0.4):
    free = dict.fromkeys((OUT_Y, IN_Y, OUT_IN, IN_OUT, MID), 0.0)
    order = [{OUTER: [], INNER: []} for _ in gaps]
    clock = {OUTER: 0.0, INNER: 0.0}
    heap, seen = [], set()
    count = [0]
    turn = 0.0

    def push(when, role, k, name):
        heapq.heappush(heap, (when, count[0], role, k, name))
        count[0] += 1

    def send(when, link, size):
        free[link] = max(when, free[link]) + size / LINK_RATE
        return free[link] + HOP_US

    for slot, (gap, spare) in enumerate(gaps):
        last = slot == len(gaps) - 1
        for role in clock:
            clock[role] += gap
        for k, (_, size, ready) in enumerate(chunks):
            if ready == slot:
                turn = max(turn, max(clock.values()))
                push(turn, OUTER, k, START)
                push(turn, INNER, k, START)
                turn += pace * size / LINK_RATE
        if small and last:
            for role in clock:
                for i in range(6):
                    push(max(clock.values()) + 2.5 * i, role, SMALL, i)
        later, now = [], max(clock.values()) + spare
        while heap:
            when, n, role, k, name = heapq.heappop(heap)
            if k == SMALL:
                clock[role] = max(when, clock[role])
                order[slot][role].append((k, name))
                continue
            kind, size, _ = chunks[k]
            if not last and when + (0.0 if name == START else margin) > now:
                later.append((when, n, role, k, name))
                continue
            when = max(when, clock[role])
            if (kind, role, name) == (KIND_A, INNER, R2) and (k, INNER, R1) not in seen:
                push(when + 0.2, role, k, name)
                continue
            when += 0.2 + (size / 800e3 if name in (R0, R1, R2, R3) else 0.0)
            clock[role] = when
            order[slot][role].append((k, name))
            seen.add((k, role, name))
            for link, part, to, event in SENDS.get((kind, role, name), ()):
                push(send(when, link, size * part), to, k, event)
        for item in later:
            heapq.heappush(heap, item)
        for role in clock:
            clock[role] = max(clock[role], now)
    return order, max(clock.values())


SENDS = {
    (KIND_A, OUTER, START): ((OUT_Y, 0.5, OUTER, R1),),
    (KIND_A, INNER, START): ((IN_Y, 0.5, INNER, R1),),
    (KIND_A, OUTER, R1): ((OUT_IN, 0.5, INNER, R2),),
    (KIND_A, INNER, R2): ((MID, 0.25, INNER, R3),),
    (KIND_A, INNER, R3): ((MID, 0.25, INNER, R4), (IN_OUT, 0.25, OUTER, R5A), (IN_Y, 0.25, INNER, R6A)),
    (KIND_A, INNER, R4): ((IN_OUT, 0.25, OUTER, R5B), (IN_Y, 0.25, INNER, R6B)),
    (KIND_A, OUTER, R5A): ((OUT_Y, 0.25, OUTER, R6A),),
    (KIND_A, OUTER, R5B): ((OUT_Y, 0.25, OUTER, R6B),),
    (KIND_B, OUTER, START): ((OUT_IN, 1.0, INNER, R1),),
    (KIND_B, INNER, R1): ((MID, 0.5, INNER, R2),),
    (KIND_B, INNER, R2): ((IN_Y, 0.25, INNER, R3),),
    (KIND_B, INNER, R3): ((IN_Y, 0.25, INNER, R4), (MID, 0.25, INNER, R5A), (IN_OUT, 0.25, OUTER, R6A)),
    (KIND_B, INNER, R4): ((MID, 0.25, INNER, R5B), (IN_OUT, 0.25, OUTER, R6B)),
    (KIND_B, INNER, R5A): ((IN_OUT, 0.25, OUTER, R6C),),
    (KIND_B, INNER, R5B): ((IN_OUT, 0.25, OUTER, R6D),),
    (KIND_C, OUTER, START): ((OUT_IN, 0.5, INNER, R1),),
    (KIND_C, INNER, R1): ((MID, 0.5, INNER, R2),),
    (KIND_C, INNER, R2): ((IN_OUT, 0.5, OUTER, R3),),
    (KIND_C, OUTER, R3): ((OUT_Y, 0.25, OUTER, R0),),
    (KIND_C, OUTER, R0): ((OUT_Y, 0.25, OUTER, R4), (OUT_IN, 0.25, INNER, R5A)),
    (KIND_C, OUTER, R4): ((OUT_IN, 0.25, INNER, R5B),),
    (KIND_C, INNER, R5A): ((MID, 0.25, INNER, R6A),),
    (KIND_C, INNER, R5B): ((MID, 0.25, INNER, R6B),),
    (KIND_C, INNER, R6A): ((IN_OUT, 0.25, OUTER, R7A),),
    (KIND_C, INNER, R6B): ((IN_OUT, 0.25, OUTER, R7B),),
}
EVENTS = (R0, R1, R2, R3, R4, R5A, R5B, R6A, R6B, R6C, R6D, R7A, R7B)


def slot_rows(kind, rows):
    if kind == KIND_A:
        return {R1: rows // 2, R2: rows // 2, R3: rows // 4}
    if kind == KIND_B:
        return {R1: rows, R2: rows // 2, R3: rows // 4}
    return {R1: rows // 2, R2: rows // 2, R3: rows // 2, R0: rows // 4}


class AllReduce:
    def __init__(self, chunks, grads, finals, lands, land_at, send_sem, recv_sem):
        self.chunks, self.grads, self.lands, self.land_at = chunks, grads, lands, land_at
        self.finals = finals
        self.send_sem, self.recv_sem = send_sem, recv_sem
        d, self.t = lax.axis_index(DP), lax.axis_index(TP)
        self.y, self.z = d % 2, d // 2
        self.side = self.z // 2
        self.inner = jnp.logical_or(self.z == 1, self.z == 2)
        self.to = {
            TO_Y: (self.z * 2 + 1 - self.y, self.t),
            TO_PAIR: ((self.z + 1 - 2 * (self.z % 2)) * 2 + self.y, self.t),
            TO_MID: ((3 - self.z) * 2 + self.y, self.t),
        }
        self.sent = {OUTER: [], INNER: []}

    def region(self, k, half=None, quarter=None, final=False):
        kind, g, first, rows = self.chunks[k]
        start = first
        if half is not None:
            start = start + half * (rows // 2)
            rows = rows // 2
        if quarter is not None:
            start = start + quarter * (rows // 2)
            rows = rows // 2
        if not isinstance(start, int):
            start = pl.multiple_of(start, 16)
        return (self.finals if final else self.grads)[g].at[pl.ds(start, rows)]

    def land(self, k, event):
        kind, g, first, rows = self.chunks[k]
        start, size = self.land_at[(k, event)]
        return self.lands[g].at[pl.ds(start, size)]

    def copy(self, k, event, src, dst, who):
        e = EVENTS.index(event)
        return pltpu.make_async_remote_copy(
            src_ref=src, dst_ref=dst, send_sem=self.send_sem.at[k, e], recv_sem=self.recv_sem.at[k, e],
            device_id=self.to[who], device_id_type=MESH_ID)

    def send(self, role, k, event, src, dst, who):
        c = self.copy(k, event, src, dst, who)
        c.start()
        self.sent[role].append((k, event, src.shape[0]))

    def arrive(self, k, event, dst):
        self.copy(k, event, dst, dst, TO_Y).wait_recv()

    def add(self, k, event, half=None, quarter=None, final=False):
        land = self.land(k, event)
        self.arrive(k, event, land)
        src = self.region(k, half, quarter)
        dst = self.region(k, half, quarter, final)
        rows = land.shape[0]
        step = 32 if rows % 32 == 0 else 16

        def body(i, carry):
            at = pl.ds(pl.multiple_of(i * step, 16), step)
            dst[at] = (src[at].astype(jnp.float32) + land[at].astype(jnp.float32)).astype(jnp.bfloat16)
            return carry

        lax.fori_loop(0, rows // step, body, 0)

    def event(self, role, k, name):
        kind = self.chunks[k][0]
        s, y = self.side, self.y
        R = functools.partial(self.region, k)
        F = functools.partial(self.region, k, final=True)
        send = functools.partial(self.send, role, k)
        key = (kind, role, name)
        if kind == KIND_A:
            if name == START:
                send(R1, R(1 - y), self.land(k, R1), TO_Y)
            elif name == R1:
                self.add(k, R1, y)
                if role == OUTER:
                    send(R2, R(y), self.land(k, R2), TO_PAIR)
            elif name == R2:
                self.add(k, R2, y)
                send(R3, R(y, 1 - s), self.land(k, R3), TO_MID)
            elif name == R3:
                self.add(k, R3, y, s, True)
                send(R4, F(y, s), F(y, s), TO_MID)
                send(R5A, F(y, s), F(y, s), TO_PAIR)
                send(R6A, F(y, s), F(y, s), TO_Y)
            elif name == R4:
                self.arrive(k, R4, F(y, 1 - s))
                send(R5B, F(y, 1 - s), F(y, 1 - s), TO_PAIR)
                send(R6B, F(y, 1 - s), F(y, 1 - s), TO_Y)
            elif name in (R5A, R5B):
                q = s if name == R5A else 1 - s
                self.arrive(k, name, F(y, q))
                send(R6A + name - R5A, F(y, q), F(y, q), TO_Y)
            elif name in (R6A, R6B):
                q = s if name == R6A else 1 - s
                self.arrive(k, name, F(1 - y, q))
        elif kind == KIND_B:
            if name == START:
                if role == OUTER:
                    send(R1, R(), self.land(k, R1), TO_PAIR)
            elif name == R1:
                self.add(k, R1)
                send(R2, R(1 - s), self.land(k, R2), TO_MID)
            elif name == R2:
                self.add(k, R2, s)
                send(R3, R(s, 1 - y), self.land(k, R3), TO_Y)
            elif name == R3:
                self.add(k, R3, s, y, True)
                for event, who in ((R4, TO_Y), (R5A, TO_MID), (R6A, TO_PAIR)):
                    send(event, F(s, y), F(s, y), who)
            elif name == R4:
                self.arrive(k, R4, F(s, 1 - y))
                for event, who in ((R5B, TO_MID), (R6B, TO_PAIR)):
                    send(event, F(s, 1 - y), F(s, 1 - y), who)
            elif name in (R5A, R5B):
                q = y if name == R5A else 1 - y
                self.arrive(k, name, F(1 - s, q))
                send(R6C if name == R5A else R6D, F(1 - s, q), F(1 - s, q), TO_PAIR)
            else:
                h = s if name in (R6A, R6B) else 1 - s
                q = y if name in (R6A, R6C) else 1 - y
                self.arrive(k, name, F(h, q))
        else:
            if name == START:
                if role == OUTER:
                    send(R1, R(1 - s), self.land(k, R1), TO_PAIR)
            elif name == R1:
                self.add(k, R1, 1 - s)
                send(R2, R(1 - s), self.land(k, R2), TO_MID)
            elif name == R2:
                self.add(k, R2, s)
                send(R3, R(s), self.land(k, R3), TO_PAIR)
            elif name == R3:
                self.add(k, R3, s)
                send(R0, R(s, 1 - y), self.land(k, R0), TO_Y)
            elif name == R0:
                self.add(k, R0, s, y, True)
                send(R4, F(s, y), F(s, y), TO_Y)
                send(R5A, F(s, y), F(s, y), TO_PAIR)
            elif name == R4:
                self.arrive(k, R4, F(s, 1 - y))
                send(R5B, F(s, 1 - y), F(s, 1 - y), TO_PAIR)
            elif name in (R5A, R5B):
                q = y if name == R5A else 1 - y
                self.arrive(k, name, F(s, q))
                send(R6A + name - R5A, F(s, q), F(s, q), TO_MID)
            elif name in (R6A, R6B):
                q = y if name == R6A else 1 - y
                self.arrive(k, name, F(1 - s, q))
                send(R7A + name - R6A, F(1 - s, q), F(1 - s, q), TO_PAIR)
            else:
                q = y if name == R7A else 1 - y
                self.arrive(k, name, F(1 - s, q))

    def run(self, order):
        for role, here in ((INNER, self.inner), (OUTER, jnp.logical_not(self.inner))):
            if order[role]:

                @pl.when(here)
                def _(role=role):
                    for k, name in order[role]:
                        if k == SMALL:
                            self.small.step(name)
                        else:
                            self.event(role, k, name)

    def finish(self):
        for role, here in ((INNER, self.inner), (OUTER, jnp.logical_not(self.inner))):
            @pl.when(here)
            def _(role=role):
                for k, event, rows in self.sent[role]:
                    _, g, first, _ = self.chunks[k]
                    src = self.grads[g].at[pl.ds(first, rows)]
                    self.copy(k, event, src, src, TO_Y).wait_send()


def lay_out(chunks, widths):
    at, used = {}, [0] * len(widths)
    for k, (kind, g, first, rows) in enumerate(chunks):
        for event, size in slot_rows(kind, rows).items():
            at[(k, event)] = (used[g], size)
            used[g] += size
    return at, used


class SmallSums:
    def __init__(self, source, totals, lands, send_sem, recv_sem):
        self.source, self.totals, self.lands = source, totals, lands
        self.send_sem, self.recv_sem = send_sem, recv_sem
        d, t = lax.axis_index(DP), lax.axis_index(TP)
        y, z = d % 2, d // 2
        self.to = (
            (z * 2 + 1 - y, t),
            ((z + 1 - 2 * (z % 2)) * 2 + y, t),
            (((z + 2) % 4) * 2 + y, t),
            (d, t + 1 - 2 * (t % 2)),
            (d, (t + 2) % 4),
        )

    def copy(self, i):
        src = self.source if i == 0 else self.totals.at[i - 1]
        return pltpu.make_async_remote_copy(
            src_ref=src, dst_ref=self.lands.at[i], send_sem=self.send_sem.at[i],
            recv_sem=self.recv_sem.at[i], device_id=self.to[i], device_id_type=MESH_ID)

    def step(self, i):
        if i > 0:
            self.copy(i - 1).wait_recv()
            have = self.source[...] if i == 1 else self.totals[i - 2]
            self.totals[i - 1] = have + self.lands[i - 1]
        if i < 5:
            self.copy(i).start()

    def finish(self):
        for i in range(5):
            self.copy(i).wait_send()


norm_eps = 1e-05
MASKED = -1e30
MOST_CELL = 384


def norm_rows(values, gain, shift):
    center = values - jnp.mean(values, axis=-1, keepdims=True)
    spread = jnp.mean(center * center, axis=-1, keepdims=True)
    return center * lax.rsqrt(spread + norm_eps) * gain + shift


def inner_rows(left, right):
    return lax.dot_general(
        left, right, (((0,), (0,)), ((), ())), preferred_element_type=jnp.float32
    )


def times_transposed(left, right):
    return lax.dot_general(
        left, right, (((1,), (1,)), ((), ())), preferred_element_type=jnp.float32
    )


def each_cell(lengths, row, seq_len, body):
    widths = sorted({min(w, seq_len) for w in (128, 256, MOST_CELL + 16)})

    def step(i, start):
        length = lengths[row, i]
        lower = 0
        for width in widths:
            first = pl.multiple_of(jnp.minimum(start // 16 * 16, seq_len - width), 16)

            @pl.when(jnp.logical_and(length > lower, length <= width - 16))
            def _(width=width, first=first):
                down = first + lax.broadcasted_iota(jnp.int32, (width, 1), 0)
                along = first + lax.broadcasted_iota(jnp.int32, (1, width), 1)
                inside = [jnp.logical_and(p >= start, p < start + length) for p in (down, along)]
                body(i, first, width, inside[0], inside[1])

            lower = width - 16
        return start + length

    lax.fori_loop(0, lengths.shape[1], step, jnp.int32(0))


def attend_kernel(heads, lengths, joined, out, lse):
    seq_len, wide = out.shape

    def body(cell, first, width, down, along):
        rows = pl.ds(first, width)
        seen = jnp.logical_and(down, along)
        parts = []
        for h in range(heads):
            at = h * HEAD_DIM
            query = joined[rows, at : at + HEAD_DIM] * jnp.bfloat16(HEAD_DIM**-0.5)
            key = joined[rows, wide + at : wide + at + HEAD_DIM]
            value = joined[rows, 2 * wide + at : 2 * wide + at + HEAD_DIM]
            scores = jnp.where(seen, times_transposed(query, key), MASKED)
            top = jnp.max(scores, axis=1, keepdims=True)
            expo = jnp.exp(scores - top)
            total = jnp.sum(expo, axis=1, keepdims=True)
            probs = (expo * (1.0 / total)).astype(jnp.bfloat16)
            part = jnp.dot(probs, value, preferred_element_type=jnp.float32).astype(jnp.bfloat16)
            parts.append((part, top + jnp.log(total)))
        for h, (part, height) in enumerate(parts):
            cols = slice(h * HEAD_DIM, (h + 1) * HEAD_DIM)
            out[rows, cols] = jnp.where(down, part, out[rows, cols])
            lse[rows, h : h + 1] = jnp.where(down, height, lse[rows, h : h + 1])
        number = jnp.full((width, 1), cell, jnp.int32).astype(jnp.float32)
        lse[rows, heads : heads + 1] = jnp.where(down, number, lse[rows, heads : heads + 1])

    each_cell(lengths, pl.program_id(0), seq_len, body)


def attend(joined, lengths):
    n, wide = lengths.shape[0], joined.shape[1] // 3
    seq_len = joined.shape[0] // n
    heads = wide // HEAD_DIM
    return pl.pallas_call(
        functools.partial(attend_kernel, heads),
        grid=(n,),
        out_shape=[
            jax.ShapeDtypeStruct((joined.shape[0], wide), jnp.bfloat16),
            jax.ShapeDtypeStruct((joined.shape[0], 128), jnp.float32),
        ],
        in_specs=[
            pl.BlockSpec(memory_space=pltpu.SMEM),
            pl.BlockSpec((seq_len, 3 * wide), lambda i: (i, 0)),
        ],
        out_specs=[
            pl.BlockSpec((seq_len, wide), lambda i: (i, 0)),
            pl.BlockSpec((seq_len, 128), lambda i: (i, 0)),
        ],
        compiler_params=pltpu.CompilerParams(vmem_limit_bytes=40 << 20),
        name="attend",
    )(lengths, joined)


COLS = 256
B_OUT, B_DOWN, B_UP, GAIN_ATTN, SHIFT_ATTN, GAIN_FFN, SHIFT_FFN, B_QKV = range(8)


class Refs:
    def __init__(self, names, refs):
        self.__dict__.update(zip(names, refs))


def call(body, name, ins, loose, outs, loose_outs, scratch, collective_id):
    names = list(ins) + list(loose) + list(outs) + list(loose_outs) + list(scratch)
    vmem, stay = pl.BlockSpec(memory_space=pltpu.VMEM), pl.BlockSpec(memory_space=pl.ANY)
    out = pl.pallas_call(
        lambda *refs: body(Refs(names, refs)),
        out_shape=list(outs.values()) + list(loose_outs.values()),
        in_specs=[vmem] * len(ins) + [stay] * len(loose),
        out_specs=[vmem] * len(outs) + [stay] * len(loose_outs),
        scratch_shapes=list(scratch.values()),
        compiler_params=pltpu.CompilerParams(
            collective_id=collective_id, has_side_effects=True, vmem_limit_bytes=64000 << 10
        ),
        name=name,
    )(*ins.values(), *loose.values())
    return Refs(list(outs) + list(loose_outs), out)


def low(*shape):
    return pltpu.VMEM(shape, jnp.bfloat16)


def full(*shape):
    return pltpu.VMEM(shape, jnp.float32)


def dma(*shape):
    return pltpu.SemaphoreType.DMA(shape)


def at_row(start, rows):
    return pl.ds(pl.multiple_of(start, 16), rows)


def at_col(i, cols=COLS):
    return pl.ds(pl.multiple_of(i * cols, cols), cols)


def remote(src, dst, send, recv, to):
    return pltpu.make_async_remote_copy(
        src_ref=src, dst_ref=dst, send_sem=send, recv_sem=recv, device_id=to, device_id_type=MESH_ID)


class Place:
    def __init__(self):
        self.d, self.t = lax.axis_index(DP), lax.axis_index(TP)
        self.across = self.t + 1 - 2 * (self.t % 2)
        self.beyond = (self.t + 2) % 4
        self.far = 3 - self.t

    def group(self):
        return [(self.d, self.across), (self.d, self.beyond)]


def meet(peers):
    barrier = pltpu.get_barrier_semaphore()
    for peer in peers:
        pl.semaphore_signal(barrier, inc=1, device_id=peer, device_id_type=MESH_ID)
    pl.semaphore_wait(barrier, len(peers))


class Gather:
    def __init__(self, place, whole, send, recv, cuts, rows):
        self.p, self.whole, self.send, self.recv, self.cuts = place, whole, send, recv, cuts
        self.rows = rows

    def piece(self, owner, i):
        first, rows = self.cuts[i]
        return self.whole.at[at_row(owner * self.rows + first, rows)]

    def copy(self, kind, i, owner):
        ref = self.piece(owner, i)
        to = self.p.beyond if kind == 1 else self.p.across
        return remote(ref, ref, self.send.at[kind, i], self.recv.at[kind, i], (self.p.d, to))

    def start(self, i):
        self.copy(1, i, self.p.t).start()
        self.copy(0, i, self.p.t).start()

    def across(self):
        for i in range(len(self.cuts)):
            self.copy(0, i, self.p.across).wait_recv()

    def beyond(self, i):
        self.copy(1, i, self.p.beyond).wait_recv()
        self.copy(2, i, self.p.beyond).start()

    def far(self, i):
        self.copy(2, i, self.p.far).wait_recv()

    def rest(self):
        for i in range(len(self.cuts)):
            self.beyond(i)
        for i in range(len(self.cuts)):
            self.far(i)

    def finish(self):
        for i in range(len(self.cuts)):
            self.copy(0, i, self.p.t).wait_send()
            self.copy(1, i, self.p.t).wait_send()
            self.copy(2, i, self.p.beyond).wait_send()


class Scatter:
    def __init__(self, place, rows, out, near, cross, last, own, send, recv):
        self.p, self.rows = place, rows
        self.out, self.near, self.cross, self.last, self.own = out, near, cross, last, own
        self.send, self.recv = send, recv

    def copies(self):
        d, p = self.p.d, self.p
        return (
            remote(self.out.at[0], self.near.at[0], self.send.at[0], self.recv.at[0], (d, p.across)),
            remote(self.out.at[1], self.near.at[1], self.send.at[1], self.recv.at[1], (d, p.across)),
        ) + tuple(
            remote(self.cross.at[pl.ds(*cut)], self.last.at[pl.ds(*cut)], self.send.at[2 + i], self.recv.at[2 + i], (d, p.beyond))
            for i, cut in enumerate(cuts_of(self.rows))
        )

    def start(self, compute, between=lambda: None):
        copies = self.copies()

        def keep(slot):
            def store(j, value):
                self.out[slot, :, at_col(j)] = value.astype(jnp.bfloat16)

            return store

        def add(j, value):
            total = value + self.near[0, :, at_col(j)].astype(jnp.float32)
            self.cross[:, at_col(j)] = total.astype(jnp.bfloat16)

        def hold(j, value):
            self.own[:, at_col(j)] = value

        compute(self.p.far * self.rows, keep(0))
        copies[0].start()
        between()
        compute(self.p.across * self.rows, keep(1))
        copies[1].start()
        between()
        copies[0].wait_recv()
        compute(self.p.beyond * self.rows, add)
        copies[2].start()
        copies[3].start()
        between()
        compute(self.p.t * self.rows, hold)

    def arrive(self, i):
        copies = self.copies()
        if i == 0:
            copies[1].wait_recv()
        copies[2 + i].wait_recv()

    def total(self, rows):
        return self.own[rows] + (self.near[1, rows].astype(jnp.float32) + self.last[rows].astype(jnp.float32))

    def finish(self):
        for c in self.copies():
            c.wait_send()


def scatter_scratch(prefix, rows):
    return {
        prefix + "out": low(2, rows, D), prefix + "near": low(2, rows, D), prefix + "cross": low(rows, D),
        prefix + "last": low(rows, D), prefix + "own": full(rows, D),
        prefix + "send": dma(4), prefix + "recv": dma(4),
    }


def scatter_of(refs, prefix, place, rows):
    names = ("out", "near", "cross", "last", "own", "send", "recv")
    return Scatter(place, rows, *[getattr(refs, prefix + n) for n in names])


def cuts_of(rows):
    half = (rows // 2 + 15) // 16 * 16
    return ((0, half), (half, rows - half))


def each_block(rows, body, init=0):
    for first, count in cuts_of(rows):
        out = body(first, count, init)
        init = init if out is None else out
    return init


def each_col(width, body):
    def step(j, carry):
        body(j)
        return carry

    lax.fori_loop(0, width // COLS, step, 0)


def norm_back(x, cot, gain):
    center = x - jnp.mean(x, axis=-1, keepdims=True)
    rate = lax.rsqrt(jnp.mean(center * center, axis=-1, keepdims=True) + norm_eps)
    hat = center * rate
    inner = cot * gain
    part = inner - jnp.mean(inner, axis=-1, keepdims=True) - hat * jnp.mean(inner * hat, axis=-1, keepdims=True)
    return part * rate, cot * hat


def reduce_scratch(chunks, shapes):
    at, used = lay_out(chunks, shapes)
    out = {}
    for i, (u, s) in enumerate(zip(used, shapes)):
        out["land%d" % i] = low(max(u, 16), s[1])
    out["send"] = dma(max(len(chunks), 1), len(EVENTS))
    out["recv"] = dma(max(len(chunks), 1), len(EVENTS))
    return out, at


def cut_rows(pieces, size, kinds):
    chunks, timed = [], []
    for g, first, rows, columns, slot in pieces:
        end = first + rows
        while first < end:
            here = size if end - first >= 2 * size or end - first == size else end - first
            kind = kinds[len(chunks) % len(kinds)]
            chunks.append((kind, g, first, here))
            timed.append((kind, here * columns * 2, slot))
            first += here
    return chunks, timed


def windows(seqs, every, rows):
    seq_len = every // seqs
    block = rows if seq_len % rows == 0 else seq_len
    for first in range(0, every, block):
        row = first // seq_len * seq_len
        low_key = max(0, first - row - MOST_CELL + 1) // 128 * 128
        high_key = min(seq_len, -(-(first - row + block + MOST_CELL - 1) // 128) * 128)
        yield first, block, row + low_key, row + high_key


def attend_back(r, seqs, advance, finished):
    every, wide = r.d_att.shape
    heads, scale = wide // HEAD_DIM, HEAD_DIM**-0.5
    r.turned[...] = r.lse[...].T[: r.turned.shape[0]]
    r.d_keys[...] = jnp.zeros_like(r.d_keys)
    r.d_values[...] = jnp.zeros_like(r.d_values)
    for h in range(heads):
        at = h * HEAD_DIM
        cols = slice(at, at + HEAD_DIM)
        for first, block, low_key, high_key in windows(seqs, every, r.tokens.shape[0]):
            here, keys = slice(first, first + block), slice(low_key, high_key)
            query = r.qkv[here, cols] * jnp.bfloat16(scale)
            key = r.qkv[keys, wide + at : wide + at + HEAD_DIM]
            value = r.qkv[keys, 2 * wide + at : 2 * wide + at + HEAD_DIM]
            cot = r.d_att[here, cols]
            seen = r.lse[here, heads : heads + 1] == r.turned[heads : heads + 1, keys]
            scores = jnp.where(seen, times_transposed(query, key), MASKED)
            probs = jnp.exp(scores - r.lse[here, h : h + 1])
            r.d_values[h, keys] += inner_rows(probs.astype(jnp.bfloat16), cot)
            d_probs = times_transposed(cot, value)
            offset = jnp.sum(probs * d_probs, axis=1, keepdims=True)
            d_scores = (probs * (d_probs - offset)).astype(jnp.bfloat16)
            r.cots[here, cols] = (jnp.dot(d_scores, key, preferred_element_type=jnp.float32) * scale).astype(jnp.bfloat16)
            r.d_keys[h, keys] += inner_rows(d_scores, query)
            advance()
        for i, part in ((1, r.d_keys), (2, r.d_values)):
            r.cots[:, i * wide + at : i * wide + at + HEAD_DIM] = part[h].astype(jnp.bfloat16)
        finished(h)


def head_pieces(h, heads):
    if h % 2 == 0 and h + 1 < heads:
        return []
    first = h // 2 * 2 * HEAD_DIM
    size = (h + 1) * HEAD_DIM - first
    return [(i * heads * HEAD_DIM + first, size) for i in range(3)]


def tail_kernel(chunks, order, land_at, reduce, seqs, r):
    place = Place()
    rows = r.tokens.shape[0]
    wide = r.w.shape[0]
    step = iter(order)
    late = [
        pltpu.make_async_copy(src, dst, r.fill.at[2 + i])
        for i, (src, dst) in enumerate(zip((r.normed_in, r.w_in, r.tokens_in, r.d_mid_in), (r.normed, r.w, r.tokens, r.d_mid)))
    ]
    if reduce:
        up, out, joined = r.up, r.out, r.joined
        ar = AllReduce(
            chunks, (up, out, joined), (r.sum_up, r.sum_out, r.sum_joined), (r.land0, r.land1, r.land2),
            land_at, r.send, r.recv)
        ar.small = SmallSums(r.small, r.totals, r.small_lands, r.small_send, r.small_recv)
        peers = [ar.to[TO_Y], ar.to[TO_PAIR], ar.to[TO_MID], ar.small.to[2]] + place.group()
    else:
        up, out, joined = r.sum_up, r.sum_out, r.sum_joined
        peers = place.group()
    fills = [pltpu.make_async_copy(r.up_in, up, r.fill.at[0]), pltpu.make_async_copy(r.out_in, out, r.fill.at[1])]
    for f in fills + late:
        f.start()
    meet(peers)
    for f in fills:
        f.wait()

    def advance():
        if reduce:
            ar.run(next(step))

    scatter = scatter_of(r, "s", place, rows)
    advance()
    for f in late:
        f.wait()

    def finished(h):
        for i, n in head_pieces(h, wide // 3 // HEAD_DIM):
            joined[i : i + n] = inner_rows(r.cots[:, i : i + n], r.normed[...]).astype(jnp.bfloat16)
            advance()

    attend_back(r, seqs, advance, finished)

    def to_first(first, store):
        cots = r.cots[at_row(first, rows)]
        each_col(D, lambda j: store(j, jnp.dot(cots, r.w[:, at_col(j)], preferred_element_type=jnp.float32)))

    scatter.start(to_first, advance)
    advance()
    r.small[...] = r.small_in[...]
    r.small[7:8, :wide] = lax.fori_loop(
        0, r.cots.shape[0] // rows,
        lambda i, c: c + jnp.sum(r.cots[at_row(i * rows, rows)].astype(jnp.float32), axis=0, keepdims=True),
        jnp.zeros((1, wide), jnp.float32))
    advance()
    scatter.arrive(0)
    scatter.arrive(1)
    gain = r.vectors[GAIN_ATTN]

    def back(first, count, carry):
        at = at_row(first, count)
        cot = scatter.total(at)
        part, gained = norm_back(r.tokens[at].astype(jnp.float32), cot, gain)
        r.d_tokens[at] = r.d_mid[at] + part
        return carry + jnp.stack([jnp.sum(gained, axis=0), jnp.sum(cot, axis=0)])

    r.small[2:4] = each_block(rows, back, jnp.zeros((2, D), jnp.float32))
    scatter.finish()
    advance()
    if reduce:
        ar.finish()
        ar.small.finish()
        r.small_dp[...] = r.totals[2]
        r.small_all[...] = r.totals[4]
    else:
        r.small_dp[...] = r.small[...]
        r.small_all[...] = r.small[...]


def copy_of(x):
    return jax.ShapeDtypeStruct(x.shape, x.dtype)


TAIL_KINDS = (2, 0, 0, 0, 2, 2, 0, 0, 0, 0, 0, 2, 2, 0, 2, 0, 0, 0, 0, 0, 1)
MID_KINDS = (2, 2, 0, 2, 2, 0, 2, 0, 0, 0)
UNIT_US = 1.45
TAIL_SIZE, TAIL_PACE, MID_SIZE, MID_PACE = 128, 0.0, 128, 0.52


def tail(qkv, d_att, lse, seqs, normed, w, tokens, d_mid, vectors, up, out, small, reduce):
    rows, wide = tokens.shape[0], w.shape[0]
    every = qkv.shape[0]
    heads = d_att.shape[1] // HEAD_DIM
    blocks = len(list(windows(seqs, every, rows)))
    joined = jax.ShapeDtypeStruct((wide, D), jnp.bfloat16)
    shapes = [up.shape, out.shape, joined.shape]
    pieces = [(0, 0, up.shape[0], D, 0), (1, 0, out.shape[0], D, 0)]
    gaps = [(0.0, 0.0)]
    for h in range(heads):
        gaps += [(UNIT_US, 0.0)] * blocks
        for i, n in head_pieces(h, heads):
            pieces.append((2, i, n, D, len(gaps)))
            gaps.append((n / 128, 0.0))
    gaps += [(2.2, 0.0)] * 4 + [(1.5, 10.0), (3.0, 0.0)]
    chunks, timed = cut_rows(pieces, TAIL_SIZE, TAIL_KINDS)
    order, _ = plan_order(timed, gaps, True, TAIL_PACE)
    scratch = scatter_scratch("s", rows)
    scratch.update(
        small=full(8, D), fill=dma(6), turned=full(8, every), cots=low(*qkv.shape), d_keys=full(heads, every, HEAD_DIM),
        d_values=full(heads, every, HEAD_DIM), normed=low(every, D), w=low(wide, D), tokens=low(rows, D),
        d_mid=full(rows, D))
    land_at = None
    if reduce:
        more, land_at = reduce_scratch(chunks, shapes)
        scratch.update(more)
        scratch.update(
            up=low(*up.shape), out=low(*out.shape), joined=low(wide, D), totals=full(5, 8, D),
            small_lands=full(5, 8, D), small_send=dma(5), small_recv=dma(5))
    return call(
        functools.partial(tail_kernel, chunks, order, land_at, reduce, seqs), "tail",
        dict(qkv=qkv, d_att=d_att, lse=lse, vectors=vectors, small_in=small),
        dict(normed_in=normed, w_in=w, tokens_in=tokens, d_mid_in=d_mid, up_in=up, out_in=out),
        dict(d_tokens=jax.ShapeDtypeStruct((rows, D), jnp.float32), sum_up=copy_of(up), sum_out=copy_of(out),
             sum_joined=joined, small_dp=copy_of(small), small_all=copy_of(small)),
        {}, scratch, 0)


def gelu_and_slope(x):
    rate = (2.0 / jnp.pi) ** 0.5
    square = x * x
    bent = jnp.tanh(rate * x * (1.0 + 0.044715 * square))
    half = 0.5 * (1.0 + bent)
    return x * half, half + 0.5 * x * (1.0 - bent * bent) * rate * (1.0 + 0.134145 * square)


def middle_kernel(chunks, order, land_at, reduce, r):
    place = Place()
    rows = r.tokens.shape[0]
    every = r.attended.shape[0]
    hidden = r.act.shape[1]
    step = iter(order)
    down = r.down if reduce else r.sum_down
    peers = place.group()
    if reduce:
        ar = AllReduce(chunks, (down,), (r.sum_down,), (r.land0,), land_at, r.send, r.recv)
        peers += [ar.to[TO_Y], ar.to[TO_PAIR], ar.to[TO_MID]]

    def advance():
        if reduce:
            ar.run(next(step))

    soon = cuts_of(rows)[0][1]
    cots = Gather(place, r.cots, r.cots_send, r.cots_recv, ((soon, rows - soon),), rows)
    second = Gather(place, r.second, r.second_send, r.second_recv, cuts_of(rows), rows)
    branch = Gather(place, r.branch, r.branch_send, r.branch_recv, cuts_of(rows), rows)
    mine = place.t * rows

    fills = [
        pltpu.make_async_copy(
            r.d_output.at[pl.ds(soon, rows - soon)], r.cots.at[at_row(mine + soon, rows - soon)], r.fill.at[0])
    ] + [
        pltpu.make_async_copy(r.early.at[pl.ds(i * soon, soon)], r.cots.at[pl.ds(i * rows, soon)], r.fill.at[1 + i])
        for i in range(4)
    ] + [
        pltpu.make_async_copy(r.w_up_in, r.w_up, r.fill.at[5]),
        pltpu.make_async_copy(r.w_down_in, r.w_down, r.fill.at[6]),
    ]
    drains = [
        pltpu.make_async_copy(r.grad_up, r.grad_up_out, r.fill.at[7]),
        pltpu.make_async_copy(r.output, r.output_out, r.fill.at[8]),
        pltpu.make_async_copy(r.mid, r.d_mid_out, r.fill.at[9]),
    ]
    for f in fills:
        f.start()
    meet(peers)

    def to_out(first, store):
        att = r.attended[at_row(first, rows)]
        each_col(D, lambda j: store(j, jnp.dot(att, r.w_out[:, at_col(j)], preferred_element_type=jnp.float32)))

    one = scatter_of(r, "s", place, rows)
    one.start(to_out)
    gain, shift = r.vectors[GAIN_FFN], r.vectors[SHIFT_FFN]
    for i, (first, count) in enumerate(second.cuts):
        at = at_row(first, count)
        one.arrive(i)
        mid = r.tokens[at].astype(jnp.float32) + one.total(at) + r.vectors[B_OUT]
        r.mid[at] = mid
        r.second[at_row(mine + first, count)] = norm_rows(mid, gain, shift).astype(jnp.bfloat16)
        second.start(i)
    for f in fills[:5]:
        f.wait()
    cots.start(0)
    one.finish()

    def up(first, count):
        at = at_row(first, count)

        def tile(j):
            col = at_col(j)
            pre = jnp.dot(r.second[at], r.w_up[:, col], preferred_element_type=jnp.float32) + r.vectors[B_UP, col]
            act, slope = gelu_and_slope(pre)
            r.act[at, col] = act.astype(jnp.bfloat16)
            r.slope[at, col] = slope

        each_col(hidden, tile)

    pair = place.t // 2 * 2 * rows
    fills[5].wait()
    fills[6].wait()
    second.across()
    up(pair, 2 * rows)
    second.rest()
    up(2 * rows - pair, 2 * rows)

    def to_down(first, store):
        act = r.act[at_row(first, rows)]
        each_col(D, lambda j: store(j, jnp.dot(act, r.w_down[:, at_col(j)], preferred_element_type=jnp.float32)))

    cots.across()
    cots.rest()
    for i in range(hidden // COLS):
        col = slice(i * COLS, (i + 1) * COLS)
        down[col] = inner_rows(r.act[:, col], r.cots[...]).astype(jnp.bfloat16)
        advance()
    three = Scatter(place, rows, r.sout, r.snear, r.scross, r.slast, r.sown, r.again_send, r.again_recv)
    three.start(to_down, advance)
    advance()
    for j in range(hidden // COLS):
        col = slice(j * COLS, (j + 1) * COLS)
        d_pre = (times_transposed(r.cots[...], r.w_down[col]) * r.slope[:, col]).astype(jnp.bfloat16)
        r.d_pre[:, col] = d_pre
        r.small[6:7, col] = jnp.sum(d_pre.astype(jnp.float32), axis=0, keepdims=True)
        advance()

    def to_second(first, store):
        d_pre = r.d_pre[at_row(first, rows)]
        each_col(D, lambda j: store(j, times_transposed(d_pre, r.w_up[at_row(j * COLS, COLS)])))

    two = scatter_of(r, "t", place, rows)
    two.start(to_second, advance)
    advance()
    for i in range(D // COLS):
        col = slice(i * COLS, (i + 1) * COLS)
        r.grad_up[col] = inner_rows(r.second[:, col], r.d_pre[...]).astype(jnp.bfloat16)
        advance()
    drains[0].start()
    three.arrive(0)
    three.arrive(1)

    def finish(first, count, carry):
        at = at_row(first, count)
        r.output[at] = (r.mid[at] + three.total(at) + r.vectors[B_DOWN]).astype(jnp.bfloat16)

    each_block(rows, finish)
    drains[1].start()
    advance()
    sums = jnp.zeros((4, D), jnp.float32)
    for i, (first, count) in enumerate(branch.cuts):
        at = at_row(first, count)
        two.arrive(i)
        cot = two.total(at)
        part, gained = norm_back(r.mid[at], cot, gain)
        d_output = r.cots[at_row(mine + first, count)].astype(jnp.float32)
        d_mid = d_output + part
        r.mid[at] = d_mid
        low_part = d_mid.astype(jnp.bfloat16)
        r.branch[at_row(mine + first, count)] = low_part
        branch.start(i)
        parts = (low_part.astype(jnp.float32), d_output, gained, cot)
        sums = sums + jnp.stack([jnp.sum(p, axis=0) for p in parts])
    drains[2].start()
    r.small[0:2] = sums[0:2]
    r.small[2:4] = jnp.zeros((2, D), jnp.float32)
    r.small[4:6] = sums[2:4]
    r.small[7:8] = jnp.zeros((1, D), jnp.float32)

    def attn(first, count):
        at = at_row(first, count)
        r.d_att[at] = times_transposed(r.branch[at], r.w_out[...]).astype(jnp.bfloat16)

    advance()
    branch.across()
    attn(pair, 2 * rows)
    advance()
    branch.rest()
    attn(2 * rows - pair, 2 * rows)
    wide = r.attended.shape[1]
    for i in range(0, wide, COLS):
        col = slice(i, min(wide, i + COLS))
        r.grad_out[col] = inner_rows(r.attended[:, col], r.branch[...]).astype(jnp.bfloat16)
    advance()
    for part in (cots, second, branch, two, three):
        part.finish()
    for part in drains:
        part.wait()
    if reduce:
        ar.finish()


def middle(attended, tokens, d_output, early, w_out, w_up, w_down, vectors, reduce):
    rows, every = tokens.shape[0], attended.shape[0]
    hidden = w_up.shape[1]
    groups = hidden // COLS
    chunks, timed = cut_rows([(0, i * COLS, COLS, D, i) for i in range(groups)], MID_SIZE, MID_KINDS)
    gaps = [(1.5, 0.0)] * groups + [(2.2, 0.0)] * 4 + [(1.8, 0.0)] * groups + [(2.2, 0.0)] * 4 + [(1.5, 0.0)] * (D // COLS)
    gaps += [(1.5, 3.0), (2.5, 2.0), (2.0, 12.0), (5.0, 0.0)]
    order, _ = plan_order(timed, gaps, False, MID_PACE)
    scratch = scatter_scratch("s", rows)
    scratch.update(scatter_scratch("t", rows))
    scratch.update(
        again_send=dma(4), again_recv=dma(4), cots=low(every, D), second=low(every, D), branch=low(every, D),
        cots_send=dma(3, 2), cots_recv=dma(3, 2), second_send=dma(3, 2), second_recv=dma(3, 2),
        branch_send=dma(3, 2), branch_recv=dma(3, 2), mid=full(rows, D), act=low(every, hidden),
        slope=full(every, hidden), d_pre=low(every, hidden), w_up=low(*w_up.shape), w_down=low(*w_down.shape),
        output=low(rows, D), grad_up=low(*w_up.shape), fill=dma(10))
    land_at = None
    if reduce:
        more, land_at = reduce_scratch(chunks, [w_down.shape])
        scratch.update(more, down=low(*w_down.shape))
    return call(
        functools.partial(middle_kernel, chunks, order, land_at, reduce), "middle",
        dict(attended=attended, tokens=tokens, w_out=w_out, vectors=vectors),
        dict(d_output=d_output, early=early, w_up_in=w_up, w_down_in=w_down),
        dict(d_att=copy_of(attended), sum_down=copy_of(w_down), grad_out=copy_of(w_out),
             small=jax.ShapeDtypeStruct((8, D), jnp.float32)),
        dict(output_out=copy_of(tokens), d_mid_out=jax.ShapeDtypeStruct((rows, D), jnp.float32), grad_up_out=copy_of(w_up)),
        scratch, 1)


def front_kernel(r):
    place = Place()
    rows = r.tokens.shape[0]
    wide = r.w.shape[0]
    third = wide // 3
    cuts = cuts_of(rows)
    soon = cuts[0][1]
    tokens = Gather(place, r.whole, r.send, r.recv, cuts, rows)
    cots = Gather(place, r.early, r.cots_send, r.cots_recv, ((0, soon),), soon)
    mine = place.t * rows
    r.whole[at_row(mine, rows)] = r.tokens[...]
    fill = pltpu.make_async_copy(r.d_output.at[pl.ds(0, soon)], r.early.at[at_row(place.t * soon, soon)], r.fill.at[0])
    fill.start()
    meet(place.group())
    tokens.start(0)
    tokens.start(1)
    fill.wait()
    cots.start(0)
    for i, part in enumerate((r.w_query, r.w_key, r.w_value)):
        r.w[i * third : (i + 1) * third] = part[...]
    drains = [pltpu.make_async_copy(r.w, r.w_out, r.fill.at[1])]
    drains[0].start()
    gain, shift = r.vectors[GAIN_ATTN], r.vectors[SHIFT_ATTN]

    def project(owner, first, count):
        at = at_row(owner * rows + first, count)
        r.normed[at] = norm_rows(r.whole[at].astype(jnp.float32), gain, shift).astype(jnp.bfloat16)
        for i in range(0, wide, COLS):
            col = slice(i, min(wide, i + COLS))
            part = times_transposed(r.normed[at], r.w[col]) + r.vectors[B_QKV, col]
            r.joined[at, col] = part.astype(jnp.bfloat16)
        for src, dst in ((r.normed, r.normed_out), (r.joined, r.joined_out)):
            drains.append(pltpu.make_async_copy(src.at[at], dst.at[at], r.fill.at[1 + len(drains)]))
            drains[-1].start()

    project(place.t, 0, rows)
    tokens.across()
    project(place.across, 0, rows)
    for i, cut in enumerate(cuts):
        tokens.beyond(i)
        project(place.beyond, *cut)
        tokens.far(i)
        project(place.far, *cut)
    tokens.finish()
    cots.across()
    cots.rest()
    cots.finish()
    for part in drains:
        part.wait()


def front(tokens, d_output, w_query, w_key, w_value, vectors):
    rows = tokens.shape[0]
    every = rows * lax.axis_size(TP)
    parts = [w.T for w in (w_query, w_key, w_value)]
    wide = 3 * parts[0].shape[0]
    early = cuts_of(rows)[0][1] * lax.axis_size(TP)
    bf16 = jnp.bfloat16
    return call(
        front_kernel, "front",
        dict(tokens=tokens, w_query=parts[0], w_key=parts[1], w_value=parts[2], vectors=vectors),
        dict(d_output=d_output),
        dict(early=jax.ShapeDtypeStruct((early, D), bf16)),
        dict(normed_out=jax.ShapeDtypeStruct((every, D), bf16), joined_out=jax.ShapeDtypeStruct((every, wide), bf16),
             w_out=jax.ShapeDtypeStruct((wide, D), bf16)),
        dict(whole=low(every, D), normed=low(every, D), joined=low(every, wide), w=low(wide, D), send=dma(3, 2),
             recv=dma(3, 2), cots_send=dma(3, 1), cots_recv=dma(3, 1), fill=dma(16)), 2)


def local(
    tokens, w_query, w_key, w_value, b_query, b_value, w_out, b_out, w_up, b_up, w_down, b_down,
    gain_attn, shift_attn, gain_ffn, shift_ffn, cell_lengths, d_output,
):
    cols = w_query.shape[1]
    reduce = lax.axis_size(DP) == 8
    vectors = jnp.concatenate(
        [b_out, b_down, b_up, gain_attn, shift_attn, gain_ffn, shift_ffn, b_query, jnp.zeros_like(b_query), b_value,
         jnp.zeros(D - 3 * cols)]
    ).reshape(8, D)
    f = front(tokens, d_output, w_query, w_key, w_value, vectors)
    attended, lse = attend(f.joined_out, cell_lengths)
    m = middle(attended, tokens, d_output, f.early, w_out, w_up, w_down, vectors, reduce)
    seqs = cell_lengths.shape[0]
    e = tail(f.joined_out, m.d_att, lse, seqs, f.normed_out, f.w_out, tokens, m.d_mid_out, vectors, m.grad_up_out, m.grad_out, m.small, reduce)
    sums = tuple(g.astype(jnp.float32) for g in (m.sum_down, e.sum_up, e.sum_out, e.sum_joined))
    small_dp, small_all = e.small_dp, e.small_all
    if not reduce:
        sums = lax.psum(sums, DP)
        small_dp = lax.psum(small_dp, DP)
        small_all = lax.psum(small_all, (DP, TP))
    grad_down, grad_up, grad_out, joined = sums
    last = small_dp[7]
    return (
        m.output_out, e.d_tokens, joined[:cols].T, joined[cols : 2 * cols].T, joined[2 * cols :].T,
        last[:cols], last[2 * cols : 3 * cols], grad_out, small_all[0], grad_up, small_dp[6], grad_down,
        small_all[1], small_all[2], small_all[3], small_all[4], small_all[5],
    )


def solution(mesh):
    in_specs = (
        P((DP, TP), None),
        P(None, TP),
        P(None, TP),
        P(None, TP),
        P(TP),
        P(TP),
        P(TP, None),
        P(),
        P(None, TP),
        P(TP),
        P(TP, None),
        P(),
        P(),
        P(),
        P(),
        P(),
        P(DP, None),
        P((DP, TP), None),
    )
    out_specs = (
        P((DP, TP), None),
        P((DP, TP), None),
        P(None, TP),
        P(None, TP),
        P(None, TP),
        P(TP),
        P(TP),
        P(TP, None),
        P(),
        P(None, TP),
        P(TP),
        P(TP, None),
        P(),
        P(),
        P(),
        P(),
        P(),
    )
    return jax.shard_map(local, mesh=mesh, in_specs=in_specs, out_specs=out_specs, check_vma=False)
```
